32 devices in a mesh: sx: 4 (over x, core), sy: 8 (over z, y).
Axes of the slice: x: 2, y: 2, z: 4, core: 2. Of those that a mesh axis runs over, the one named last changes fastest.
Arguments:
- disp: float32 [2, 3, 256, 512], P(None, None, 'sy', 'sx'), may hold values from -0.2 to 0.2
- velocity: float32 [2, 3, 256, 512], P(None, None, 'sy', 'sx'), may hold values from -3 to 3
- kinds: int32 [2, 256, 512], P(None, 'sy', 'sx'), may hold values from 0 to 1
- neighbours: int32 [2, 6, 256, 512], P(None, None, 'sy', 'sx'), may hold values from 0 to 17, as said below
- pad_mask: int32 [2, 6, 256, 512], P(None, None, 'sy', 'sx'), may hold values from 0 to 1, as said below
- kernel: float32 [512, 3, 3, 2, 256], P('sy', None, None, None, 'sx'), may hold values from -12 to 140, as said below
Outputs:
- new_disp: float32 [2, 3, 256, 512], P(None, None, 'sy', 'sx')
- new_velocity: float32 [2, 3, 256, 512], P(None, None, 'sy', 'sx')
The draws below stay inside these ranges and needn't reach their ends.
Inputs may be any that keep to these rules, and one draw needn't show every extreme that they name: `neighbours`: slots 0 to 3 of every atom hold four different face codes (0 to 5); the other slots hold different edge codes (6 to 17). `pad_mask`: slots 0 to 3 of every atom are live. `kernel`: for every wavevector the 3 x 3 complex matrix is Hermitian.
All inputs are finite; a program needn't handle non-finite values.
Results may differ from the reference program's by a relative error of at most 0.0003.
Values sent between devices are 32-bit elements; how exact they have to be, the bound alone decides.
A program may use at most 64 MiB of HBM per device.

```python
import math
import jax
import jax.numpy as jnp
import numpy as np
from jax import lax

LAYERS = 2
NB = 6
NX = 512
NY = 256


def draw_neighbours(key, part):
    first_key, second_key = jax.random.split(jax.random.fold_in(key, 11))
    face_start = jax.random.randint(first_key, (LAYERS, 1, NY, NX), 0, 6)
    edge_start = jax.random.randint(second_key, (LAYERS, 1, NY, NX), 0, 12)
    face_steps = jnp.arange(4, dtype=jnp.int32)[None, :, None, None]
    edge_steps = jnp.arange(NB - 4, dtype=jnp.int32)[None, :, None, None]
    faces = (face_start + face_steps) % 6
    edges = 6 + (edge_start + 5 * edge_steps) % 12
    return jnp.concatenate([faces, edges], axis=1).astype(jnp.int32)


def draw_pad_mask(key, part):
    draws = jax.random.randint(jax.random.fold_in(key, 23), (LAYERS, NB - 4, NY, NX), 0, 3)
    tail = (draws > 0).astype(jnp.int32)
    head = jnp.ones((LAYERS, 4, NY, NX), jnp.int32)
    return jnp.concatenate([head, tail], axis=1)


def draw_kernel(key, part):
    diag_key, sym_key, anti_key = jax.random.split(jax.random.fold_in(key, 37), 3)
    diagonal = jnp.exp(jax.random.uniform(diag_key, (NX, 3, NY), jnp.float32, math.log(10.0), math.log(100.0)))
    symmetric = jax.random.uniform(sym_key, (NX, 3, NY), jnp.float32, -12.0, 12.0)
    antisym = jax.random.uniform(anti_key, (NX, 3, NY), jnp.float32, -12.0, 12.0)
    zeros = jnp.zeros((NX, NY), jnp.float32)
    real_rows = [jnp.stack([diagonal[:, 0], symmetric[:, 0], symmetric[:, 1]], axis=1), jnp.stack([symmetric[:, 0], diagonal[:, 1], symmetric[:, 2]], axis=1), jnp.stack([symmetric[:, 1], symmetric[:, 2], diagonal[:, 2]], axis=1)]
    imag_rows = [jnp.stack([zeros, antisym[:, 0], antisym[:, 1]], axis=1), jnp.stack([-antisym[:, 0], zeros, antisym[:, 2]], axis=1), jnp.stack([-antisym[:, 1], -antisym[:, 2], zeros], axis=1)]
    real_part = jnp.stack(real_rows, axis=1)
    imag_part = jnp.stack(imag_rows, axis=1)
    return jnp.stack([real_part, imag_part], axis=3)


def set_ends(drawn, key, least, largest):
    shape = drawn.shape
    place = [jax.random.randint(jax.random.fold_in(key, axis), (), 0, shape[axis]) for axis in range(len(shape))]
    drawn = drawn.at[tuple(place)].set(least)
    longest = shape.index(max(shape))
    place[longest] = (place[longest] + 1) % shape[longest]
    return drawn.at[tuple(place)].set(largest)


def level_of(rng, dims, cuts, smallest, top_value):
    loudness, own = 1.0, jax.random.fold_in(rng, 6)
    for axis_at, parts in cuts:
        steps = jnp.exp(jax.random.uniform(jax.random.fold_in(own, axis_at), (parts,), jnp.float32, smallest / len(cuts), top_value / len(cuts)))
        loudness = loudness * jnp.repeat(steps, dims[axis_at] // parts).reshape([-1 if axis == axis_at else 1 for axis in range(len(dims))])
    return loudness


def normal_values(rng, shape, scale, limit, cuts=(), kind=jnp.bfloat16):
    level = level_of(rng, shape, cuts, -0.22, 0.18) if cuts else 1.0
    result = jax.random.normal(rng, shape, jnp.float32) * scale * level
    return jnp.minimum(jnp.maximum(result, -limit), limit).astype(kind)


def setup_inputs(seed: int = 0) -> dict:
    key_of = jax.random.split(jax.random.key(seed), 7)
    return {
        "disp": normal_values(key_of[0], (LAYERS, 3, NY, NX), 0.05, 0.2, ((2, 8), (3, 4)), jnp.float32),
        "velocity": normal_values(key_of[1], (LAYERS, 3, NY, NX), 0.5, 3.0, ((2, 8), (3, 4)), jnp.float32),
        "kinds": set_ends(jax.random.randint(key_of[2], (LAYERS, NY, NX), 0, 2), jax.random.fold_in(key_of[2], 1), 0, 1).astype(jnp.int32),
        "neighbours": draw_neighbours(jax.random.fold_in(key_of[6], 71), 0),
        "pad_mask": draw_pad_mask(jax.random.fold_in(key_of[6], 71), 0),
        "kernel": draw_kernel(jax.random.fold_in(key_of[6], 71), 0),
    }


silicon = (1830.8, 471.18, 2.4799, 1.7322, 1.1e-06, 0.78734, 100390.0, 16.217, -0.59825, 2.7, 3.0)
germanium = (1769.0, 419.23, 2.4451, 1.7047, 9.0166e-07, 0.75627, 106430.0, 15.652, -0.43884, 2.8, 3.1)
offset_table = np.array([[1, 0, 0], [0, 1, 0], [0, 0, 1], [-1, 0, 0], [0, -1, 0], [0, 0, -1], [1, 1, 0], [1, -1, 0], [-1, 1, 0], [-1, -1, 0], [1, 0, 1], [1, 0, -1], [-1, 0, 1], [-1, 0, -1], [0, 1, 1], [0, 1, -1], [0, -1, 1], [0, -1, -1]], dtype=np.int32)
lattice_step = 2.0
impulse_scale = 0.1
drift_scale = 0.05

def blended(fraction, position):
    return silicon[position] + fraction * (germanium[position] - silicon[position])

def slab_energy(padded_disp, padded_kind, codes, live_slots):
    layers = codes.shape[0]
    slots = codes.shape[1]
    height = padded_disp.shape[2] - 2
    width = padded_disp.shape[3] - 2
    tall = height + 2
    broad = width + 2
    flat_disp = jnp.transpose(padded_disp, (1, 0, 2, 3)).reshape(3, -1)
    flat_kind = padded_kind.reshape(-1)
    row_ids = jnp.arange(height, dtype=jnp.int32)[None, :, None]
    col_ids = jnp.arange(width, dtype=jnp.int32)[None, None, :]
    offdiag = (1.0 - jnp.eye(slots, dtype=jnp.float32))[:, :, None, None]
    total = jnp.float32(0.0)
    for layer in range(layers):
        code = codes[layer]
        shift_x = jnp.zeros(code.shape, jnp.int32)
        shift_y = jnp.zeros(code.shape, jnp.int32)
        shift_z = jnp.zeros(code.shape, jnp.int32)
        for entry in range(offset_table.shape[0]):
            hit = code == entry
            shift_x = shift_x + jnp.where(hit, int(offset_table[entry, 0]), 0).astype(jnp.int32)
            shift_y = shift_y + jnp.where(hit, int(offset_table[entry, 1]), 0).astype(jnp.int32)
            shift_z = shift_z + jnp.where(hit, int(offset_table[entry, 2]), 0).astype(jnp.int32)
        level = layer + 1 + shift_z
        index = (level * tall + row_ids + 1 + shift_y) * broad + col_ids + 1 + shift_x
        valid = ((layer + shift_z >= 0) & (layer + shift_z < layers)).astype(jnp.float32)
        weight_live = live_slots[layer].astype(jnp.float32) * valid
        other = flat_disp[:, index]
        own = padded_disp[layer + 1, :, 1:-1, 1:-1][:, None]
        lattice_vec = jnp.stack([shift_x, shift_y, shift_z]).astype(jnp.float32) * lattice_step
        bond = lattice_vec + other - own
        dist = jnp.sqrt(lax.optimization_barrier(jnp.sum(bond * bond, axis=0)))
        own_kind = padded_kind[layer + 1, 1:-1, 1:-1][None]
        other_kind = flat_kind[index]
        repulse = jnp.sqrt(blended(own_kind, 0) * blended(other_kind, 0))
        attract = jnp.sqrt(blended(own_kind, 1) * blended(other_kind, 1))
        rep_decay = 0.5 * (blended(own_kind, 2) + blended(other_kind, 2))
        att_decay = 0.5 * (blended(own_kind, 3) + blended(other_kind, 3))
        cut_inner = jnp.sqrt(blended(own_kind, 9) * blended(other_kind, 9))
        cut_outer = jnp.sqrt(blended(own_kind, 10) * blended(other_kind, 10))
        phase = jnp.pi * (dist - cut_inner) / (cut_outer - cut_inner)
        smooth = 0.5 + 0.5 * jnp.cos(phase)
        cutoff = jnp.where(dist < cut_inner, 1.0, jnp.where(dist > cut_outer, 0.0, smooth))
        unit = bond / dist[None]
        cosine = lax.optimization_barrier(jnp.sum(unit[:, :, None] * unit[:, None, :], axis=0))
        angle_c = blended(own_kind, 6)
        angle_d = blended(own_kind, 7)
        angle_h = blended(own_kind, 8)
        gap = (angle_h[None] - cosine) ** 2
        angular = 1.0 + (angle_c * angle_c / (angle_d * angle_d))[None] * gap / ((angle_d * angle_d)[None] + gap)
        weight = weight_live * cutoff
        zeta = lax.optimization_barrier(jnp.sum(offdiag * weight[None, :] * angular, axis=1))
        beta_coef = blended(own_kind, 4)
        exponent = blended(own_kind, 5)
        order = jnp.exp(-jnp.log1p(jnp.exp(exponent * jnp.log(beta_coef * zeta))) / (2.0 * exponent))
        pair_energy = cutoff * (repulse * jnp.exp(-rep_decay * dist) - order * attract * jnp.exp(-att_decay * dist))
        total = total + 0.5 * jnp.sum(weight_live * pair_energy)
    return total

def reference(disp, velocity, kinds, neighbours, pad_mask, kernel):
    layers = disp.shape[0]
    slots = neighbours.shape[1]
    kind_float = kinds.astype(jnp.float32)
    wrapped = jnp.pad(disp, ((0, 0), (0, 0), (1, 1), (1, 1)), mode='wrap')
    wrapped = jnp.pad(wrapped, ((1, 1), (0, 0), (0, 0), (0, 0)))
    kind_wrap = jnp.pad(kind_float, ((0, 0), (1, 1), (1, 1)), mode='wrap')
    kind_wrap = jnp.pad(kind_wrap, ((1, 1), (0, 0), (0, 0)))
    block = 32
    while NY % block:
        block = block - 1
    energy_grad = jax.grad(slab_energy)

    def advance(accum, start_row):
        zero = jnp.zeros((), jnp.int32)
        start_row = start_row.astype(jnp.int32)
        window = lax.dynamic_slice(wrapped, (zero, zero, start_row, zero), (layers + 2, 3, block + 2, NX + 2))
        window_kind = lax.dynamic_slice(kind_wrap, (zero, start_row, zero), (layers + 2, block + 2, NX + 2))
        codes = lax.dynamic_slice(neighbours, (zero, zero, start_row, zero), (layers, slots, block, NX))
        live_slots = lax.dynamic_slice(pad_mask, (zero, zero, start_row, zero), (layers, slots, block, NX))
        local_grad = energy_grad(window, window_kind, codes, live_slots)
        current = lax.dynamic_slice(accum, (zero, zero, start_row, zero), local_grad.shape)
        accum = lax.dynamic_update_slice(accum, current + local_grad, (zero, zero, start_row, zero))
        return (accum, None)
    starts = jnp.arange(NY // block, dtype=jnp.int32) * block
    accum = jnp.zeros((layers + 2, 3, NY + 2, NX + 2), jnp.float32)
    accum, unused = lax.scan(advance, accum, starts)
    grads = accum[1:-1]
    core = grads[..., 1:-1]
    core = core.at[..., 0].add(grads[..., -1]).at[..., -1].add(grads[..., 0])
    inner = core[..., 1:-1, :]
    inner = inner.at[..., 0, :].add(core[..., -1, :]).at[..., -1, :].add(core[..., 0, :])
    force = -inner
    spectrum = jnp.fft.fft2(disp[0])
    real_part = jnp.real(spectrum)
    imag_part = jnp.imag(spectrum)
    kernel_real = jnp.transpose(kernel[:, :, :, 0, :], (1, 2, 3, 0))
    kernel_imag = jnp.transpose(kernel[:, :, :, 1, :], (1, 2, 3, 0))
    force_real = -lax.optimization_barrier(jnp.sum(kernel_real * real_part[None] - kernel_imag * imag_part[None], axis=1))
    force_imag = -lax.optimization_barrier(jnp.sum(kernel_real * imag_part[None] + kernel_imag * real_part[None], axis=1))
    boundary = jnp.real(jnp.fft.ifft2(lax.complex(force_real, force_imag))).astype(jnp.float32)
    total_force = force.at[0].add(boundary)
    new_velocity = velocity + impulse_scale * total_force
    new_disp = disp + drift_scale * new_velocity
    return (new_disp, new_velocity)
```

```python
import functools
import math

import jax
import jax.numpy as jnp
import numpy as np
from jax import lax
from jax.experimental import pallas as pl
from jax.experimental.pallas import tpu as pltpu
from jax.sharding import PartitionSpec as P

silicon = (1830.8, 471.18, 2.4799, 1.7322, 1.1e-06, 0.78734, 100390.0, 16.217, -0.59825, 2.7, 3.0)
germanium = (1769.0, 419.23, 2.4451, 1.7047, 9.0166e-07, 0.75627, 106430.0, 15.652, -0.43884, 2.8, 3.1)
faces = ((1, 0, 0), (0, 1, 0), (0, 0, 1), (-1, 0, 0), (0, -1, 0), (0, 0, -1))
edges = (
    (1, 1, 0), (1, -1, 0), (-1, 1, 0), (-1, -1, 0),
    (1, 0, 1), (1, 0, -1), (-1, 0, 1), (-1, 0, -1),
    (0, 1, 1), (0, 1, -1), (0, -1, 1), (0, -1, -1),
)
FACE_SLOTS = 4
lattice_step = 2.0
impulse_scale = 0.1
drift_scale = 0.05
LANES = 128
ROWS = 8
IM_LANE = 64
f32 = jnp.float32
MESH = pl.DeviceIdType.MESH


def dft_table(length, sign):
    ids = np.arange(length, dtype=np.int64)
    angle = (ids[:, None] * ids[None, :] % length) * (2.0 * math.pi / length)
    table = np.concatenate([np.cos(angle), sign * np.sin(angle)], axis=1).astype(np.float32)
    high = table.astype(jnp.bfloat16)
    low = (table - high.astype(np.float32)).astype(jnp.bfloat16)
    return np.stack([high, low])


def dot3(values, high, low):
    top = values.astype(jnp.bfloat16)
    rest = (values - top.astype(f32)).astype(jnp.bfloat16)
    dot = functools.partial(jnp.dot, preferred_element_type=f32)
    return dot(top, high) + (dot(rest, high) + dot(top, low))


def pick(is_ge, same, position, mean):
    si, ge = silicon[position], germanium[position]
    both = math.sqrt(si * ge) if mean == "geo" else 0.5 * (si + ge)
    return jnp.where(same, jnp.where(is_ge, f32(ge), f32(si)), f32(both))


def own_pick(is_ge, si, ge):
    return jnp.where(is_ge, f32(ge), f32(si))


def poly(v2, coefs):
    out = f32(coefs[-1])
    for coef in coefs[-2::-1]:
        out = out * v2 + f32(coef)
    return out


sin_coefs = [(-1) ** k * math.pi ** (2 * k + 1) / math.factorial(2 * k + 1) for k in range(6)]
cos_coefs = [(-1) ** k * math.pi ** (2 * k) / math.factorial(2 * k) for k in range(7)]


def bonds_of(layer, layers, slot):
    table = faces if slot < FACE_SLOTS else edges
    base = 0 if slot < FACE_SLOTS else len(faces)
    for entry, (dx, dy, dz) in enumerate(table):
        if 0 <= layer + dz < layers:
            yield base + entry, dx, dy, dz


def tersoff_rows(layer, layers, slots, shifted, chunk, codes, masks):
    def near(dx, dy, level, comp):
        return shifted[dx + 1, dy + 1, level, comp, chunk]

    own = [near(0, 0, layer, comp) for comp in range(3)]
    own_ge = near(0, 0, layer, 3) > 0.5
    h = own_pick(own_ge, silicon[8], germanium[8])
    d2 = own_pick(own_ge, silicon[7] ** 2, germanium[7] ** 2)
    c2 = own_pick(own_ge, silicon[6] ** 2, germanium[6] ** 2)
    ratio = own_pick(own_ge, silicon[6] ** 2 / silicon[7] ** 2, germanium[6] ** 2 / germanium[7] ** 2)
    beta = own_pick(own_ge, silicon[4], germanium[4])
    power = own_pick(own_ge, silicon[5], germanium[5])
    half_inv = own_pick(own_ge, 0.5 / silicon[5], 0.5 / germanium[5])
    data = []
    for slot in range(slots):
        code = codes[slot]
        bond = [jnp.full(code.shape, lattice_step, f32)] + [jnp.zeros(code.shape, f32) for _ in range(2)]
        kind = jnp.zeros(code.shape, f32)
        valid = jnp.zeros(code.shape, f32)
        for entry, dx, dy, dz in bonds_of(layer, layers, slot):
            hit = code == entry
            for comp, step in enumerate((dx, dy, dz)):
                place = near(dx, dy, layer + dz, comp)
                if step:
                    place = place + f32(lattice_step * step)
                bond[comp] = jnp.where(hit, place - own[comp], bond[comp])
            kind = jnp.where(hit, near(dx, dy, layer + dz, 3), kind)
            valid = jnp.where(hit, f32(1.0), valid)
        live = masks[slot].astype(f32) * valid
        dist2 = bond[0] * bond[0] + bond[1] * bond[1] + bond[2] * bond[2]
        inv = lax.rsqrt(dist2)
        dist = dist2 * inv
        unit = [b * inv for b in bond]
        same = (kind > 0.5) == own_ge
        inner = pick(own_ge, same, 9, "geo")
        span_si = 1.0 / (silicon[10] - silicon[9])
        span_ge = 1.0 / (germanium[10] - germanium[9])
        span_mix = 1.0 / (math.sqrt(silicon[10] * germanium[10]) - math.sqrt(silicon[9] * germanium[9]))
        span = jnp.where(same, jnp.where(own_ge, f32(span_ge), f32(span_si)), f32(span_mix))
        phase = (dist - inner) * span
        v = jnp.clip(phase, 0.0, 1.0) - 0.5
        v2 = v * v
        fade = 0.5 - 0.5 * v * poly(v2, sin_coefs)
        fade_slope = f32(-0.5 * math.pi) * span * poly(v2, cos_coefs)
        below, above = phase < 0.0, phase > 1.0
        cutoff = jnp.where(below, 1.0, jnp.where(above, 0.0, fade))
        slope = jnp.where(below | above, 0.0, fade_slope) * live
        mu = pick(own_ge, same, 3, "mean")
        lam = pick(own_ge, same, 2, "mean")
        attract = pick(own_ge, same, 1, "geo") * jnp.exp(-mu * dist)
        repulse = pick(own_ge, same, 0, "geo") * jnp.exp(-lam * dist)
        data.append(dict(unit=unit, inv=inv, weight=live * cutoff, slope=slope, mu=mu, lam=lam, att=attract, rep=repulse))
    zeta = [jnp.zeros_like(h) for _ in range(slots)]
    for s in range(slots):
        for t in range(s):
            us, ut = data[s]["unit"], data[t]["unit"]
            q = us[0] * ut[0] + us[1] * ut[1] + us[2] * ut[2]
            away = h - q
            gap = away * away
            g = 1.0 + ratio * gap / (d2 + gap)
            zeta[s] = zeta[s] + data[t]["weight"] * g
            zeta[t] = zeta[t] + data[s]["weight"] * g
    pull, radial = [], []
    for s in range(slots):
        item = data[s]
        z = jnp.exp(power * jnp.log(beta * zeta[s]))
        order = jnp.exp(-jnp.log(1.0 + z) * half_inv)
        bound = order * item["att"]
        pull.append(0.25 * item["weight"] * bound * z / (zeta[s] * (1.0 + z)))
        radial.append(
            0.5 * (item["slope"] * (item["rep"] - bound) + item["weight"] * (item["mu"] * bound - item["lam"] * item["rep"]))
        )
    turn = [[jnp.zeros_like(h) for _ in range(3)] for _ in range(slots)]
    spread = [jnp.zeros_like(h) for _ in range(slots)]
    for s in range(slots):
        for t in range(s):
            us, ut = data[s]["unit"], data[t]["unit"]
            q = us[0] * ut[0] + us[1] * ut[1] + us[2] * ut[2]
            away = h - q
            gap = away * away
            inv = 1.0 / (d2 + gap)
            g = 1.0 + ratio * gap * inv
            tilt = -2.0 * c2 * away * inv * inv
            pair = (pull[s] * data[t]["weight"] + pull[t] * data[s]["weight"]) * tilt
            for comp in range(3):
                turn[s][comp] = turn[s][comp] + pair * ut[comp]
                turn[t][comp] = turn[t][comp] + pair * us[comp]
            spread[s] = spread[s] + pull[t] * g
            spread[t] = spread[t] + pull[s] * g
    grads = []
    for s in range(slots):
        item = data[s]
        unit = item["unit"]
        along = turn[s][0] * unit[0] + turn[s][1] * unit[1] + turn[s][2] * unit[2]
        line = radial[s] + item["slope"] * spread[s] - along * item["inv"]
        grads.append([turn[s][comp] * item["inv"] + line * unit[comp] for comp in range(3)])
    return grads


def step_kernel(
    dims,
    disp_hbm, kinds_hbm, codes_hbm, masks_hbm, kern_hbm, x_hbm, y_hbm,
    out_ref,
    disp_ref, kinds_ref, codes_ref, masks_ref, kern_all, kern_out, x_tab, y_tab, line_in, buf, send2, recv2, send3, recv3, send4, recv4, kern_in,
    col_out, top_out, low_out, col_in, row_in, shifted, spill,
    side_out, edge_out, side_in, edge_in,
    load_sem, p1_sem, k_sem, halo_sem, p2_sem, p3_sem, p4_sem, rim_sem, relay_sem,
):
    nx_dev, ny_dev, layers, slots, rows, total_x, total_y, kxw, kyw = dims
    count = nx_dev * ny_dev
    rp = rows // nx_dev
    chunks = rows // ROWS
    b = lax.axis_index("sx")
    a = lax.axis_index("sy")
    me = a * nx_dev + b
    lane = lax.broadcasted_iota(jnp.int32, (rows, LANES), 1)
    row = lax.broadcasted_iota(jnp.int32, (rows, LANES), 0)
    lane1 = lax.broadcasted_iota(jnp.int32, (ROWS, LANES), 1)

    def wrap(value, size):
        return jnp.where(value >= size, value - size, value)

    def each_other(visit):
        for i in reversed(range(nx_dev)):
            other_x = wrap(b + i, nx_dev)

            def body(j, carry, other_x=other_x):
                visit(other_x, wrap(a + j, ny_dev))
                return carry

            lax.fori_loop(0 if i else 1, ny_dev, body, None, unroll=count <= 64)

    def beside(step_x, step_y):
        return {"sx": wrap(b + step_x % nx_dev, nx_dev), "sy": wrap(a + step_y % ny_dev, ny_dev)}

    def remote(src, dst, sems, index, dev):
        return pltpu.make_async_remote_copy(
            src_ref=src, dst_ref=dst, send_sem=sems.at[0, index], recv_sem=sems.at[1, index],
            device_id=dev, device_id_type=MESH,
        )

    barrier = pltpu.get_barrier_semaphore()

    bits = ny_dev.bit_length() - 1
    partners = [{"sx": b, "sy": a + 2**t * (1 - 2 * ((a // 2**t) % 2))} for t in range(bits)]
    near = [{"sx": wrap(b + k, nx_dev), "sy": a} for k in range(1, nx_dev)] + partners
    for dev in near:
        pl.semaphore_signal(barrier, inc=1, device_id=dev, device_id_type=MESH)

    def pass_on(t):
        pl.semaphore_signal(relay_sem.at[t], inc=1, device_id=partners[t], device_id_type=MESH)


    loads = [
        pltpu.make_async_copy(x_hbm, x_tab, load_sem.at[0]),
        pltpu.make_async_copy(y_hbm, y_tab, load_sem.at[1]),
        pltpu.make_async_copy(disp_hbm, disp_ref, load_sem.at[2]),
        pltpu.make_async_copy(kern_hbm, kern_all, load_sem.at[3]),
        pltpu.make_async_copy(codes_hbm, codes_ref, load_sem.at[4]),
        pltpu.make_async_copy(masks_hbm, masks_ref, load_sem.at[5]),
        pltpu.make_async_copy(kinds_hbm, kinds_ref, load_sem.at[6]),
    ]
    for i in (2, 6, 3, 0, 1, 4, 5):
        loads[i].start()

    def field(level, comp):
        if comp < 3:
            return disp_ref[level, comp].reshape(rows, LANES)
        return kinds_ref[level].astype(f32)

    pl.semaphore_wait(barrier, len(near))
    pass_on(0)
    loads[2].wait()

    p1 = []
    kc = []
    for k in range(1, nx_dev):
        other = wrap(b + k, nx_dev)
        p1.append(remote(disp_ref.at[0, :, other], line_in.at[b], p1_sem, k, {"sx": other, "sy": a}))
        kc.append(remote(kern_out.at[other], kern_in.at[b], k_sem, k, {"sx": other, "sy": a}))
    for copy in p1:
        copy.start()
    for comp in range(3):
        line_in[b, comp] = disp_ref[0, comp, b]
    halo = []
    for i, step in enumerate((1, -1)):
        halo.append(remote(col_out, col_in.at[i], halo_sem, i, beside(step, 0)))
    n = 2
    for j, (step_y, src) in enumerate(((1, low_out), (-1, top_out))):
        for i, step_x in enumerate((1, 0, -1)):
            halo.append(remote(src, row_in.at[j, i], halo_sem, n, beside(step_x, step_y)))
            n += 1
    loads[6].wait()
    packed = jnp.zeros((rows, LANES), f32)
    for q in range(4 * layers):
        base = field(q // 4, q % 4)
        top_out[q : q + 1, :] = base[0:1]
        low_out[q : q + 1, :] = base[rows - 1 : rows]
        packed = jnp.where(lane == q, base[:, 0:1], packed)
        packed = jnp.where(lane == 4 * layers + q, base[:, LANES - 1 : LANES], packed)
    col_out[...] = packed

    for t in range(1, bits):
        pl.semaphore_wait(relay_sem.at[t - 1], 1)
        pass_on(t)
    loads[3].wait()
    spots = [(c, c, 0) for c in range(3)] + [(c, d, ri) for ri in range(2) for c, d in ((0, 1), (0, 2), (1, 2))]

    def stiff_part(dest, m):
        c, d, ri = spots[m]
        return kern_all[dest * kxw : (dest + 1) * kxw, c, d, ri, :]

    for dest in range(nx_dev):
        if kyw % LANES == 0:
            for m in range(9):
                kern_out[dest, m] = stiff_part(dest, m)
        else:
            for m in range(5):
                high = stiff_part(dest, m + 5) if m < 4 else jnp.zeros((kxw, kyw), f32)
                kern_out[dest, m] = jnp.concatenate([stiff_part(dest, m), high], axis=1)
    kern_in[b] = kern_out[b]

    for copy in kc:
        copy.start()
    for copy in p1:
        copy.wait()
    for src in range(nx_dev):
        for comp in range(3):
            buf[comp * rp : (comp + 1) * rp, src * LANES : (src + 1) * LANES] = line_in[src, comp]
    loads[0].wait()
    buf[...] = dot3(buf[:, :total_x], x_tab[0], x_tab[1])
    per = LANES // kxw
    lane_p = lax.broadcasted_iota(jnp.int32, (rp, LANES), 1)
    for dest in range(count):
        block, part = dest // per, dest % per
        tile = jnp.zeros((rp, LANES), f32)
        for ri in range(2):
            for comp in range(3):
                at = ri * IM_LANE + comp * kxw
                col = ri * total_x + block * LANES
                piece = buf[comp * rp : (comp + 1) * rp, col : col + LANES]
                shift = (at - part * kxw) % LANES
                if shift:
                    piece = pltpu.roll(piece, shift, 1)
                tile = jnp.where((lane_p >= at) & (lane_p < at + kxw), piece, tile)
        send2[dest] = tile
    recv2[me] = send2[me]
    pl.semaphore_wait(relay_sem.at[bits - 1], 1)

    def all_start(src, dst, sems):
        def send(other_x, other_y):
            dev = other_y * nx_dev + other_x
            remote(src.at[dev], dst.at[me], sems, 0, {"sx": other_x, "sy": other_y}).start()

        each_other(send)

    def all_wait(src, dst, sems):
        some = pl.ds(0, count - 1)
        pltpu.make_async_copy(src.at[some], src.at[some], sems.at[0, 0]).wait()
        pltpu.make_async_copy(dst.at[some], dst.at[some], sems.at[1, 0]).wait()

    for copy in halo:
        copy.start()
    all_start(send2, recv2, p2_sem)

    for copy in halo:
        copy.wait()
    first_row, last_row = row == 0, row == rows - 1
    first_lane, last_lane = lane == 0, lane == LANES - 1
    full = (rows, LANES)

    def keep(dx, dy, q, value):
        for chunk in range(chunks):
            shifted[dx + 1, dy + 1, q // 4, q % 4, chunk] = value[chunk * ROWS : (chunk + 1) * ROWS]

    for q in range(4 * layers):
        base = field(q // 4, q % 4)
        left = jnp.broadcast_to(col_in[0][:, 4 * layers + q : 4 * layers + q + 1], full)
        right = jnp.broadcast_to(col_in[1][:, q : q + 1], full)
        for dy in (-1, 0, 1):
            if dy == 0:
                mid, lo, hi = base, left, right
            else:
                edge = first_row if dy == -1 else last_row
                j = 0 if dy == -1 else 1
                turn = 1 if dy == -1 else rows - 1
                mid = jnp.where(edge, row_in[j, 1, q : q + 1, :], pltpu.roll(base, turn, 0))
                lo = jnp.where(edge, row_in[j, 0, q : q + 1, LANES - 1 : LANES], pltpu.roll(left, turn, 0))
                hi = jnp.where(edge, row_in[j, 2, q : q + 1, 0:1], pltpu.roll(right, turn, 0))
            keep(0, dy, q, mid)
            keep(-1, dy, q, jnp.where(first_lane, lo, pltpu.roll(mid, 1, 1)))
            keep(1, dy, q, jnp.where(last_lane, hi, pltpu.roll(mid, LANES - 1, 1)))

    for copy in kc:
        copy.wait()
    loads[1].wait()
    all_wait(send2, recv2, p2_sem)
    width = 3 * kxw

    def along_y(table):
        out = dot3(table, y_tab[0], y_tab[1])
        return out[:, :total_y], out[:, total_y:]

    cos_part, sin_part = along_y(jnp.transpose(recv2[...].reshape(total_y, LANES)))
    s_re = cos_part[:width] + sin_part[IM_LANE : IM_LANE + width]
    s_im = cos_part[IM_LANE : IM_LANE + width] - sin_part[:width]
    lane_k = lax.broadcasted_iota(jnp.int32, (kxw, LANES), 1)

    def stiff(m):
        if kyw % LANES == 0:
            return jnp.concatenate([kern_in[src, m] for src in range(nx_dev)], axis=1)
        pieces = []
        for pair in range(nx_dev // 2):
            one, two = kern_in[2 * pair, m % 5], kern_in[2 * pair + 1, m % 5]
            if m < 5:
                two = pltpu.roll(two, LANES // 2, 1)
            else:
                one = pltpu.roll(one, LANES // 2, 1)
            pieces.append(jnp.where(lane_k < LANES // 2, one, two))
        return jnp.concatenate(pieces, axis=1)

    sr = [s_re[comp * kxw : (comp + 1) * kxw] for comp in range(3)]
    si = [s_im[comp * kxw : (comp + 1) * kxw] for comp in range(3)]
    fr, fi = [], []
    for comp in range(3):
        diag = stiff(comp)
        fr.append(diag * sr[comp])
        fi.append(diag * si[comp])
    for m, (c, d) in enumerate(((0, 1), (0, 2), (1, 2))):
        kr, ki = stiff(3 + m), stiff(6 + m)
        fr[c] = fr[c] + kr * sr[d] - ki * si[d]
        fi[c] = fi[c] + kr * si[d] + ki * sr[d]
        fr[d] = fr[d] + kr * sr[c] + ki * si[c]
        fi[d] = fi[d] + kr * si[c] - ki * sr[c]
    blank = jnp.zeros((IM_LANE - width, total_y), f32)
    cos_part, sin_part = along_y(jnp.concatenate(fr + [blank] + fi + [blank], axis=0))
    back = jnp.concatenate(
        [cos_part[:IM_LANE] - sin_part[IM_LANE:], cos_part[IM_LANE:] + sin_part[:IM_LANE]], axis=0
    )
    send3[...] = jnp.transpose(back).reshape(count, rp, LANES)
    recv3[me] = send3[me]
    all_start(send3, recv3, p3_sem)

    loads[4].wait()
    loads[5].wait()

    @pl.loop(0, chunks)
    def _(chunk):
        own_sum = []
        parts = {}
        at = pl.ds(pl.multiple_of(chunk * ROWS, ROWS), ROWS)
        for layer in range(layers):
            codes = [codes_ref[layer, slot, at, :] for slot in range(slots)]
            masks = [masks_ref[layer, slot, at, :] for slot in range(slots)]
            grads = tersoff_rows(layer, layers, slots, shifted, chunk, codes, masks)
            total = [sum(grads[s][comp] for s in range(slots)) for comp in range(3)]
            own_sum.append(total)
            for slot in range(slots):
                for entry, dx, dy, dz in bonds_of(layer, layers, slot):
                    hit = codes[slot] == entry
                    for comp in range(3):
                        key = (dx, dy, layer + dz, comp)
                        term = jnp.where(hit, grads[slot][comp], 0.0)
                        parts[key] = parts[key] + term if key in parts else term
        for level in range(layers):
            for comp in range(3):
                key = (0, 0, level, comp)
                here = own_sum[level][comp]
                parts[key] = here - parts[key] if key in parts else here
        for (dx, dy, level, comp), value in parts.items():
            signed = value if (dx, dy) == (0, 0) else -value
            spill[dx + 1, dy + 1, level, comp, at, :] = signed

    left_pack = jnp.zeros(full, f32)
    right_pack = jnp.zeros(full, f32)
    edge_out[...] = jnp.zeros_like(edge_out)
    for q in range(3 * layers):
        level, comp = q // 3, q % 3
        lines = []
        for dx in (-1, 0, 1):
            part = spill[dx + 1, 1, level, comp]
            down = spill[dx + 1, 2, level, comp]
            up = spill[dx + 1, 0, level, comp]
            part = part + jnp.where(first_row, 0.0, pltpu.roll(down, 1, 0))
            part = part + jnp.where(last_row, 0.0, pltpu.roll(up, rows - 1, 0))
            edge_out[0, dx + 1, q : q + 1, :] = down[rows - 1 : rows]
            edge_out[1, dx + 1, q : q + 1, :] = up[0:1]
            lines.append(part)
        left_pack = jnp.where(lane == q, lines[0][:, 0:1], left_pack)
        right_pack = jnp.where(lane == q, lines[2][:, LANES - 1 : LANES], right_pack)
        out_ref[level, comp] = (
            lines[1]
            + jnp.where(first_lane, 0.0, pltpu.roll(lines[2], 1, 1))
            + jnp.where(last_lane, 0.0, pltpu.roll(lines[0], LANES - 1, 1))
        )
    side_out[0] = right_pack
    side_out[1] = left_pack
    for j in range(2):
        edge_out[j, 1] = (
            edge_out[j, 1]
            + jnp.where(lane1 == 0, 0.0, pltpu.roll(edge_out[j, 2], 1, 1))
            + jnp.where(lane1 == LANES - 1, 0.0, pltpu.roll(edge_out[j, 0], LANES - 1, 1))
        )
    rim = []
    for i, step in enumerate((1, -1)):
        rim.append(remote(side_out.at[i], side_in.at[i], rim_sem, i, beside(step, 0)))
    n = 2
    for j, step_y in enumerate((1, -1)):
        for dx in (-1, 0, 1):
            rim.append(remote(edge_out.at[j, dx + 1], edge_in.at[j, dx + 1], rim_sem, n, beside(dx, step_y)))
            n += 1
    for copy in rim:
        copy.start()

    all_wait(send3, recv3, p3_sem)
    for block in range(total_x // LANES):
        for ri in range(2):
            for comp in range(3):
                tile = jnp.zeros((rp, LANES), f32)
                for part in range(per):
                    at = ri * IM_LANE + comp * kxw
                    piece = recv3[block * per + part]
                    shift = (part * kxw - at) % LANES
                    if shift:
                        piece = pltpu.roll(piece, shift, 1)
                    tile = jnp.where((lane_p >= part * kxw) & (lane_p < (part + 1) * kxw), piece, tile)
                col = ri * total_x + block * LANES
                buf[comp * rp : (comp + 1) * rp, col : col + LANES] = tile
    real = dot3(buf[:, :total_x], x_tab[0, :, :total_x], x_tab[1, :, :total_x])
    real = real + dot3(buf[:, total_x:], x_tab[0, :, total_x:], x_tab[1, :, total_x:])
    real = real * f32(-1.0 / (total_x * total_y))
    for dest in range(nx_dev):
        for comp in range(3):
            send4[dest, comp] = real[comp * rp : (comp + 1) * rp, dest * LANES : (dest + 1) * LANES]
    recv4[b] = send4[b]
    p4 = []
    for k in range(1, nx_dev):
        other = wrap(b + k, nx_dev)
        p4.append(remote(send4.at[other], recv4.at[b], p4_sem, k, {"sx": other, "sy": a}))
    for copy in p4:
        copy.start()
    for copy in rim:
        copy.wait()
    for q in range(3 * layers):
        level, comp = q // 3, q % 3
        value = out_ref[level, comp]
        value = value + jnp.where(first_lane, side_in[0][:, q : q + 1], 0.0)
        value = value + jnp.where(last_lane, side_in[1][:, q : q + 1], 0.0)
        for j, edge in enumerate((first_row, last_row)):
            line = edge_in[j, 1, q : q + 1, :]
            value = value + jnp.where(edge, line, 0.0)
            value = value + jnp.where(edge & first_lane, edge_in[j, 2, q : q + 1, LANES - 1 : LANES], 0.0)
            value = value + jnp.where(edge & last_lane, edge_in[j, 0, q : q + 1, 0:1], 0.0)
        out_ref[level, comp] = value
    for copy in p4:
        copy.wait()
    for src in range(nx_dev):
        for comp in range(3):
            at = slice(src * rp, (src + 1) * rp)
            out_ref[0, comp, at, :] = out_ref[0, comp, at, :] + recv4[src, comp]


def shards(nx_dev, ny_dev, disp, velocity, kinds, neighbours, pad_mask, kernel):
    layers, comps, rows, cols = disp.shape
    slots = neighbours.shape[1]
    total_x, total_y = cols * nx_dev, rows * ny_dev
    count = nx_dev * ny_dev
    kx_block, kyw = kernel.shape[0], kernel.shape[4]
    kxw = kx_block // nx_dev
    rp = rows // nx_dev
    kern_parts = 9 if kyw % LANES == 0 else 5
    kern_tiles = pltpu.VMEM((nx_dev, kern_parts, kxw, kyw if kern_parts == 9 else LANES), f32)
    x_table = jnp.asarray(dft_table(total_x, -1.0))
    y_table = jnp.asarray(dft_table(total_y, 1.0))
    chunks = rows // ROWS
    vmem = pl.BlockSpec(memory_space=pltpu.VMEM)
    hbm = pl.BlockSpec(memory_space=pl.ANY)
    tiles = pltpu.VMEM((count, rp, LANES), f32)
    quarter = pltpu.VMEM((nx_dev, 3, rp, LANES), f32)
    sems = lambda n: pltpu.SemaphoreType.DMA((2, n))
    inputs = (disp.reshape(layers, comps, nx_dev, rp, cols), kinds, neighbours, pad_mask, kernel, x_table, y_table)
    force = pl.pallas_call(
        functools.partial(step_kernel, (nx_dev, ny_dev, layers, slots, rows, total_x, total_y, kxw, kyw)),
        out_shape=jax.ShapeDtypeStruct(disp.shape, f32),
        in_specs=[hbm] * 7,
        out_specs=vmem,
        scratch_shapes=[
            pltpu.VMEM((layers, comps, nx_dev, rp, cols), f32),
            pltpu.VMEM(kinds.shape, jnp.int32),
            pltpu.VMEM(neighbours.shape, jnp.int32),
            pltpu.VMEM(pad_mask.shape, jnp.int32),
            pltpu.VMEM(kernel.shape, f32),
            kern_tiles,
            pltpu.VMEM(x_table.shape, jnp.bfloat16),
            pltpu.VMEM(y_table.shape, jnp.bfloat16),
            quarter,
            pltpu.VMEM((3 * rp, 2 * total_x), f32),
            tiles, tiles, tiles, tiles,
            quarter, quarter,
            kern_tiles,
            pltpu.VMEM((rows, LANES), f32),
            pltpu.VMEM((4 * layers, LANES), f32),
            pltpu.VMEM((4 * layers, LANES), f32),
            pltpu.VMEM((2, rows, LANES), f32),
            pltpu.VMEM((2, 3, 4 * layers, LANES), f32),
            pltpu.VMEM((3, 3, layers, 4, chunks, ROWS, LANES), f32),
            pltpu.VMEM((3, 3, layers, 3, rows, LANES), f32),
            pltpu.VMEM((2, rows, LANES), f32),
            pltpu.VMEM((2, 3, ROWS, LANES), f32),
            pltpu.VMEM((2, rows, LANES), f32),
            pltpu.VMEM((2, 3, ROWS, LANES), f32),
            pltpu.SemaphoreType.DMA((7,)),
            sems(nx_dev), sems(nx_dev), sems(8), sems(1), sems(1), sems(nx_dev), sems(8),
            pltpu.SemaphoreType.REGULAR((ny_dev.bit_length() - 1,)),
        ],
        compiler_params=pltpu.CompilerParams(
            collective_id=0, has_side_effects=True, vmem_limit_bytes=44 * 1024 * 1024
        ),
    )(*(pltpu.with_memory_space_constraint(value, pltpu.HBM) for value in inputs))
    new_velocity = velocity + impulse_scale * force
    new_disp = disp + drift_scale * new_velocity
    return (new_disp, new_velocity)


def solution(mesh):
    in_specs = (
        P(None, None, "sy", "sx"),
        P(None, None, "sy", "sx"),
        P(None, "sy", "sx"),
        P(None, None, "sy", "sx"),
        P(None, None, "sy", "sx"),
        P("sy", None, None, None, "sx"),
    )
    out_specs = (P(None, None, "sy", "sx"), P(None, None, "sy", "sx"))
    body = functools.partial(shards, mesh.shape["sx"], mesh.shape["sy"])
    return jax.shard_map(body, mesh=mesh, in_specs=in_specs, out_specs=out_specs, check_vma=False)
```

```python
import functools
import math

import jax
import jax.numpy as jnp
import numpy as np
from jax import lax
from jax.experimental import pallas as pl
from jax.experimental.pallas import tpu as pltpu
from jax.sharding import PartitionSpec as P

silicon = (1830.8, 471.18, 2.4799, 1.7322, 1.1e-06, 0.78734, 100390.0, 16.217, -0.59825, 2.7, 3.0)
germanium = (1769.0, 419.23, 2.4451, 1.7047, 9.0166e-07, 0.75627, 106430.0, 15.652, -0.43884, 2.8, 3.1)
faces = ((1, 0, 0), (0, 1, 0), (0, 0, 1), (-1, 0, 0), (0, -1, 0), (0, 0, -1))
edges = (
    (1, 1, 0), (1, -1, 0), (-1, 1, 0), (-1, -1, 0),
    (1, 0, 1), (1, 0, -1), (-1, 0, 1), (-1, 0, -1),
    (0, 1, 1), (0, 1, -1), (0, -1, 1), (0, -1, -1),
)
FACE_SLOTS = 4
lattice_step = 2.0
impulse_scale = 0.1
drift_scale = 0.05
LANES = 128
ROWS = 8
IM_LANE = 32
FOLD = 8
f32 = jnp.float32
MESH = pl.DeviceIdType.MESH


def split_table(table):
    table = table.astype(np.float32)
    high = table.astype(jnp.bfloat16)
    low = (table - high.astype(np.float32)).astype(jnp.bfloat16)
    return np.stack([high, low])


def angles(length, columns):
    ids = np.arange(length, dtype=np.int64)
    return (ids[:, None] * np.arange(columns, dtype=np.int64)[None, :] % length) * (2.0 * math.pi / length)


def line_table(length):
    half = length // 2
    angle = angles(length, half)
    sines = -np.sin(angle)
    sines[:, 0] = 1.0 - 2.0 * (np.arange(length) % 2)
    return split_table(np.concatenate([np.cos(angle), sines], axis=1))


def wave_table(length):
    angle = angles(length, length)
    return split_table(np.concatenate([np.cos(angle), np.sin(angle)], axis=1))


def dot3(values, high, low):
    count = values.shape[0]
    top = values.astype(jnp.bfloat16)
    coarse = top.astype(f32)
    both = jnp.concatenate([coarse, values - coarse], axis=0).astype(jnp.bfloat16)
    dot = functools.partial(jnp.dot, preferred_element_type=f32)
    twice = dot(both, high)
    return twice[:count] + (twice[count:] + dot(top, low))


def pick(is_ge, same, position, mean):
    si, ge = silicon[position], germanium[position]
    both = math.sqrt(si * ge) if mean == "geo" else 0.5 * (si + ge)
    return jnp.where(same, jnp.where(is_ge, f32(ge), f32(si)), f32(both))


def own_pick(is_ge, si, ge):
    return jnp.where(is_ge, f32(ge), f32(si))


def poly(v2, coefs):
    out = f32(coefs[-1])
    for coef in coefs[-2::-1]:
        out = out * v2 + f32(coef)
    return out


sin_coefs = [(-1) ** k * math.pi ** (2 * k + 1) / math.factorial(2 * k + 1) for k in range(6)]
cos_coefs = [(-1) ** k * math.pi ** (2 * k) / math.factorial(2 * k) for k in range(7)]


def bonds_of(layer, layers, slot):
    table = faces if slot < FACE_SLOTS else edges
    base = 0 if slot < FACE_SLOTS else len(faces)
    for entry, (dx, dy, dz) in enumerate(table):
        if 0 <= layer + dz < layers:
            yield base + entry, dx, dy, dz


def tersoff_rows(layer, layers, slots, shifted, chunk, codes, masks):
    def near(dx, dy, level, comp):
        return shifted[dx + 1, dy + 1, level, comp, chunk]

    own = [near(0, 0, layer, comp) for comp in range(3)]
    own_ge = near(0, 0, layer, 3) > 0.5
    h = own_pick(own_ge, silicon[8], germanium[8])
    d2 = own_pick(own_ge, silicon[7] ** 2, germanium[7] ** 2)
    c2 = own_pick(own_ge, silicon[6] ** 2, germanium[6] ** 2)
    ratio = own_pick(own_ge, silicon[6] ** 2 / silicon[7] ** 2, germanium[6] ** 2 / germanium[7] ** 2)
    beta = own_pick(own_ge, silicon[4], germanium[4])
    power = own_pick(own_ge, silicon[5], germanium[5])
    half_inv = own_pick(own_ge, 0.5 / silicon[5], 0.5 / germanium[5])
    data = []
    for slot in range(slots):
        code = codes[slot]
        bond = [jnp.full(code.shape, lattice_step, f32)] + [jnp.zeros(code.shape, f32) for _ in range(2)]
        kind = jnp.zeros(code.shape, f32)
        valid = jnp.zeros(code.shape, f32)
        for entry, dx, dy, dz in bonds_of(layer, layers, slot):
            hit = code == entry
            for comp, step in enumerate((dx, dy, dz)):
                place = near(dx, dy, layer + dz, comp)
                if step:
                    place = place + f32(lattice_step * step)
                bond[comp] = jnp.where(hit, place - own[comp], bond[comp])
            kind = jnp.where(hit, near(dx, dy, layer + dz, 3), kind)
            valid = jnp.where(hit, f32(1.0), valid)
        live = masks[slot].astype(f32) * valid
        dist2 = bond[0] * bond[0] + bond[1] * bond[1] + bond[2] * bond[2]
        inv = lax.rsqrt(dist2)
        dist = dist2 * inv
        unit = [b * inv for b in bond]
        same = (kind > 0.5) == own_ge
        inner = pick(own_ge, same, 9, "geo")
        span_si = 1.0 / (silicon[10] - silicon[9])
        span_ge = 1.0 / (germanium[10] - germanium[9])
        span_mix = 1.0 / (math.sqrt(silicon[10] * germanium[10]) - math.sqrt(silicon[9] * germanium[9]))
        span = jnp.where(same, jnp.where(own_ge, f32(span_ge), f32(span_si)), f32(span_mix))
        phase = (dist - inner) * span
        v = jnp.clip(phase, 0.0, 1.0) - 0.5
        v2 = v * v
        fade = 0.5 - 0.5 * v * poly(v2, sin_coefs)
        fade_slope = f32(-0.5 * math.pi) * span * poly(v2, cos_coefs)
        below, above = phase < 0.0, phase > 1.0
        cutoff = jnp.where(below, 1.0, jnp.where(above, 0.0, fade))
        slope = jnp.where(below | above, 0.0, fade_slope) * live
        mu = pick(own_ge, same, 3, "mean")
        lam = pick(own_ge, same, 2, "mean")
        attract = pick(own_ge, same, 1, "geo") * jnp.exp(-mu * dist)
        repulse = pick(own_ge, same, 0, "geo") * jnp.exp(-lam * dist)
        data.append(dict(unit=unit, inv=inv, weight=live * cutoff, slope=slope, mu=mu, lam=lam, att=attract, rep=repulse))
    zeta = [jnp.zeros_like(h) for _ in range(slots)]
    for s in range(slots):
        for t in range(s):
            us, ut = data[s]["unit"], data[t]["unit"]
            q = us[0] * ut[0] + us[1] * ut[1] + us[2] * ut[2]
            away = h - q
            gap = away * away
            g = 1.0 + ratio * gap / (d2 + gap)
            zeta[s] = zeta[s] + data[t]["weight"] * g
            zeta[t] = zeta[t] + data[s]["weight"] * g
    pull, radial = [], []
    for s in range(slots):
        item = data[s]
        z = jnp.exp(power * jnp.log(beta * zeta[s]))
        order = jnp.exp(-jnp.log(1.0 + z) * half_inv)
        bound = order * item["att"]
        pull.append(0.25 * item["weight"] * bound * z / (zeta[s] * (1.0 + z)))
        radial.append(
            0.5 * (item["slope"] * (item["rep"] - bound) + item["weight"] * (item["mu"] * bound - item["lam"] * item["rep"]))
        )
    turn = [[jnp.zeros_like(h) for _ in range(3)] for _ in range(slots)]
    spread = [jnp.zeros_like(h) for _ in range(slots)]
    for s in range(slots):
        for t in range(s):
            us, ut = data[s]["unit"], data[t]["unit"]
            q = us[0] * ut[0] + us[1] * ut[1] + us[2] * ut[2]
            away = h - q
            gap = away * away
            inv = 1.0 / (d2 + gap)
            g = 1.0 + ratio * gap * inv
            tilt = -2.0 * c2 * away * inv * inv
            pair = (pull[s] * data[t]["weight"] + pull[t] * data[s]["weight"]) * tilt
            for comp in range(3):
                turn[s][comp] = turn[s][comp] + pair * ut[comp]
                turn[t][comp] = turn[t][comp] + pair * us[comp]
            spread[s] = spread[s] + pull[t] * g
            spread[t] = spread[t] + pull[s] * g
    grads = []
    for s in range(slots):
        item = data[s]
        unit = item["unit"]
        along = turn[s][0] * unit[0] + turn[s][1] * unit[1] + turn[s][2] * unit[2]
        line = radial[s] + item["slope"] * spread[s] - along * item["inv"]
        grads.append([turn[s][comp] * item["inv"] + line * unit[comp] for comp in range(3)])
    return grads


def step_kernel(
    dims,
    disp_hbm, kinds_hbm, codes_hbm, masks_hbm, kern_hbm, x_hbm, y_hbm,
    out_ref,
    disp_ref, kinds_ref, codes_ref, masks_ref, kern_all, kern_out, x_tab, y_tab, line_in, buf, send2, recv2, send3, recv3, waves, kern_in, rest_in, fields,
    col_out, top_out, low_out, col_in, row_in, shifted, spill,
    side_out, edge_out, side_in, edge_in,
    load_sem, p1_sem, k_sem, rest_sem, halo_sem, p2_sem, p3_sem, rim_sem, relay_sem,
):
    nx_dev, ny_dev, layers, slots, rows, total_x, total_y, pw, kyw = dims
    count = nx_dev * ny_dev
    rp = rows // nx_dev
    chunks = rows // ROWS
    b = lax.axis_index("sx")
    a = lax.axis_index("sy")
    me = a * nx_dev + b
    half = ny_dev // 2
    early = a < half
    kind = jnp.where(early, 0, 1)

    def pair_of(dev_x, dev_y):
        first = dev_y < half
        return jnp.where(first, dev_y, ny_dev - 1 - dev_y) * (2 * nx_dev) + dev_x + jnp.where(first, 0, nx_dev)

    mine = pair_of(b, a)
    lane = lax.broadcasted_iota(jnp.int32, (rows, LANES), 1)
    row = lax.broadcasted_iota(jnp.int32, (rows, LANES), 0)
    lane1 = lax.broadcasted_iota(jnp.int32, (ROWS, LANES), 1)

    def wrap(value, size):
        return jnp.where(value >= size, value - size, value)

    def each_other(visit):
        for i in reversed(range(nx_dev)):
            other_x = wrap(b + i, nx_dev)

            def body(j, carry, other_x=other_x):
                visit(other_x, wrap(a + j, ny_dev))
                return carry

            lax.fori_loop(0 if i else 1, ny_dev, body, None, unroll=count <= 64)

    def beside(step_x, step_y):
        return {"sx": wrap(b + step_x % nx_dev, nx_dev), "sy": wrap(a + step_y % ny_dev, ny_dev)}

    def remote(src, dst, sems, index, dev):
        return pltpu.make_async_remote_copy(
            src_ref=src, dst_ref=dst, send_sem=sems.at[0, index], recv_sem=sems.at[1, index],
            device_id=dev, device_id_type=MESH,
        )

    barrier = pltpu.get_barrier_semaphore()

    low = 2 ** ((ny_dev.bit_length() - 1) // 2)
    lines = ny_dev // low
    side, line = lax.rem(a, low), a // low
    cube = [
        {"sx": wrap(b + i, nx_dev), "sy": line * low + wrap(side + j, low)}
        for j in range(low) for i in range(nx_dev) if i or j
    ]
    near = cube + [{"sx": b, "sy": wrap(line + k, lines) * low + side} for k in range(1, lines)]
    for dev in near:
        pl.semaphore_signal(barrier, inc=1, device_id=dev, device_id_type=MESH)

    loads = [
        pltpu.make_async_copy(x_hbm, x_tab, load_sem.at[0]),
        pltpu.make_async_copy(y_hbm, y_tab, load_sem.at[1]),
        pltpu.make_async_copy(disp_hbm, disp_ref, load_sem.at[2]),
        None,
        pltpu.make_async_copy(codes_hbm, codes_ref, load_sem.at[4]),
        pltpu.make_async_copy(masks_hbm, masks_ref, load_sem.at[5]),
        pltpu.make_async_copy(kinds_hbm, kinds_ref, load_sem.at[6]),
    ]
    def stiff_row(slot):
        group, r = slot // pw, slot % pw
        if group == 2 * nx_dev:
            return 0
        o, t = group // nx_dev, group % nx_dev
        late = (o + 1) * nx_dev - 1 - t
        if r:
            late_row = late * pw + pw - r
        else:
            late_row = (late + 1) * pw if late + 1 < 2 * nx_dev else 0
        return jnp.where(early, group * pw + r, late_row)

    for i in (2, 6):
        loads[i].start()
    for slot in range((2 * nx_dev + 1) * pw):
        pltpu.make_async_copy(kern_hbm.at[stiff_row(slot)], kern_all.at[slot], load_sem.at[3]).start()
    for i in (0, 1, 4, 5):
        loads[i].start()

    def field(level, comp):
        if comp < 3:
            return disp_ref[level, comp].reshape(rows, LANES)
        return kinds_ref[level].astype(f32)

    pl.semaphore_wait(barrier, len(near))
    for dev in cube:
        pl.semaphore_signal(relay_sem, inc=1, device_id=dev, device_id_type=MESH)
    loads[2].wait()

    p1 = []
    kc = []
    for k in range(1, nx_dev):
        other = wrap(b + k, nx_dev)
        p1.append(remote(disp_ref.at[0, :, other], line_in.at[b], p1_sem, k, {"sx": other, "sy": a}))
        kc.append(remote(kern_out.at[other], kern_in.at[kind, b], k_sem, k, {"sx": other, "sy": a}))
    for copy in p1:
        copy.start()
    for comp in range(3):
        line_in[b, comp] = disp_ref[0, comp, b]
    halo = []
    for i, step in enumerate((1, -1)):
        halo.append(remote(col_out, col_in.at[i], halo_sem, i, beside(step, 0)))
    n = 2
    for j, (step_y, src) in enumerate(((1, low_out), (-1, top_out))):
        for i, step_x in enumerate((1, 0, -1)):
            halo.append(remote(src, row_in.at[j, i], halo_sem, n, beside(step_x, step_y)))
            n += 1
    loads[6].wait()
    packed = jnp.zeros((rows, LANES), f32)
    for q in range(4 * layers):
        base = field(q // 4, q % 4)
        top_out[q : q + 1, :] = base[0:1]
        low_out[q : q + 1, :] = base[rows - 1 : rows]
        packed = jnp.where(lane == q, base[:, 0:1], packed)
        packed = jnp.where(lane == 4 * layers + q, base[:, LANES - 1 : LANES], packed)
    col_out[...] = packed

    pltpu.make_async_copy(kern_all, kern_all, load_sem.at[3]).wait()
    spots = [(c, c, 0) for c in range(3)] + [(c, d, ri) for ri in range(2) for c, d in ((0, 1), (0, 2), (1, 2))]

    def stiff_part(group, m):
        c, d, ri = spots[m]
        return kern_all[group * pw : (group + 1) * pw, c, d, ri, :]

    for group in range(2 * nx_dev + 1):
        if kyw % LANES == 0:
            for m in range(9):
                kern_out[group, m] = stiff_part(group, m)
        else:
            for m in range(5):
                high = stiff_part(group, m + 5) if m < 4 else jnp.zeros((pw, kyw), f32)
                kern_out[group, m] = jnp.concatenate([stiff_part(group, m), high], axis=1)
    kern_in[kind, b] = kern_out[b]
    for copy in kc:
        copy.start()
    pl.semaphore_wait(relay_sem, len(cube))
    far = []
    for k in range(nx_dev):
        other = wrap(b + k, nx_dev)
        dev = {"sx": other, "sy": ny_dev - 1 - a}
        far.append(remote(kern_out.at[nx_dev + other], kern_in.at[kind, b], k_sem, nx_dev + k, dev))
    rest_to = {"sx": jnp.zeros_like(b), "sy": jnp.where(a == half, 0, ny_dev - a)}
    rest = remote(
        kern_out.at[2 * nx_dev, :, pl.ds(0, 1)], rest_in.at[b, :, pl.ds(0, 1)], rest_sem, b, rest_to
    )
    for copy in far:
        copy.start()

    @pl.when(a >= half)
    def _():
        rest.start()

    for copy in p1:
        copy.wait()
    for src in range(nx_dev):
        for comp in range(3):
            buf[comp * rp : (comp + 1) * rp, src * LANES : (src + 1) * LANES] = line_in[src, comp]
    loads[0].wait()
    buf[...] = dot3(buf[:, :total_x], x_tab[0], x_tab[1])
    per = LANES // pw
    lane_p = lax.broadcasted_iota(jnp.int32, (rp, LANES), 1)
    for dest in range(count):
        block, part = dest // per, dest % per
        tile = jnp.zeros((rp, LANES), f32)
        for ri in range(2):
            for comp in range(3):
                at = ri * IM_LANE + comp * pw
                col = ri * (total_x // 2) + block * LANES
                piece = buf[comp * rp : (comp + 1) * rp, col : col + LANES]
                shift = (at - part * pw) % LANES
                if shift:
                    piece = pltpu.roll(piece, shift, 1)
                tile = jnp.where((lane_p >= at) & (lane_p < at + pw), piece, tile)
        if rp == FOLD:
            turned = pltpu.roll(pltpu.roll(tile, LANES // 2, 1), FOLD // 2, 0)
            tile = jnp.where(lane_p < LANES // 2, tile, turned)
        send2[dest] = tile
    recv2[me] = send2[mine]
    some_rows = pl.ds(0, rp // 2 if rp == FOLD else rp)

    def all_start2():
        def send(other_x, other_y):
            src = send2.at[pair_of(other_x, other_y), some_rows]
            remote(src, recv2.at[me, some_rows], p2_sem, 0, {"sx": other_x, "sy": other_y}).start()

        each_other(send)

    lot = pl.ds(0, FOLD + (FOLD // 2 if pw == FOLD else pw))

    def all_start3():
        def send(other_x, other_y):
            src = send3.at[other_y, lot]
            remote(src, recv3.at[mine, lot], p3_sem, 0, {"sx": other_x, "sy": other_y}).start()

        each_other(send)

    def all_wait3():
        for i in range(nx_dev):
            some = send3.at[pl.ds(0, ny_dev - (1 if i == 0 else 0)), lot]
            pltpu.make_async_copy(some, some, p3_sem.at[0, 0]).wait()
        some = recv3.at[pl.ds(0, count - 1), lot]
        pltpu.make_async_copy(some, some, p3_sem.at[1, 0]).wait()

    def all_wait2():
        some = pl.ds(0, count - 1)
        pltpu.make_async_copy(send2.at[some, some_rows], send2.at[some, some_rows], p2_sem.at[0, 0]).wait()
        pltpu.make_async_copy(recv2.at[some, some_rows], recv2.at[some, some_rows], p2_sem.at[1, 0]).wait()

    for copy in halo:
        copy.start()
    all_start2()

    for copy in halo:
        copy.wait()
    first_row, last_row = row == 0, row == rows - 1
    first_lane, last_lane = lane == 0, lane == LANES - 1
    full = (rows, LANES)

    def keep(dx, dy, q, value):
        for chunk in range(chunks):
            shifted[dx + 1, dy + 1, q // 4, q % 4, chunk] = value[chunk * ROWS : (chunk + 1) * ROWS]

    for q in range(4 * layers):
        base = field(q // 4, q % 4)
        left = jnp.broadcast_to(col_in[0][:, 4 * layers + q : 4 * layers + q + 1], full)
        right = jnp.broadcast_to(col_in[1][:, q : q + 1], full)
        for dy in (-1, 0, 1):
            if dy == 0:
                mid, lo, hi = base, left, right
            else:
                edge = first_row if dy == -1 else last_row
                j = 0 if dy == -1 else 1
                turn = 1 if dy == -1 else rows - 1
                mid = jnp.where(edge, row_in[j, 1, q : q + 1, :], pltpu.roll(base, turn, 0))
                lo = jnp.where(edge, row_in[j, 0, q : q + 1, LANES - 1 : LANES], pltpu.roll(left, turn, 0))
                hi = jnp.where(edge, row_in[j, 2, q : q + 1, 0:1], pltpu.roll(right, turn, 0))
            keep(0, dy, q, mid)
            keep(-1, dy, q, jnp.where(first_lane, lo, pltpu.roll(mid, 1, 1)))
            keep(1, dy, q, jnp.where(last_lane, hi, pltpu.roll(mid, LANES - 1, 1)))

    for copy in kc:
        copy.wait()
    loads[1].wait()
    all_wait2()
    width = 3 * pw

    for src in range(count if rp == FOLD else 0):
        tile = recv2[src]
        turned = pltpu.roll(pltpu.roll(tile, LANES // 2, 1), FOLD // 2, 0)
        recv2[src] = jnp.where(lax.broadcasted_iota(jnp.int32, (rp, LANES), 0) < FOLD // 2, tile, turned)
    table = jnp.transpose(recv2[...].reshape(total_y, LANES))[: 2 * IM_LANE]
    both = dot3(table, y_tab[0], y_tab[1])
    cos_part, sin_part = both[:, :total_y], both[:, total_y:]
    for copy in far:
        copy.wait()

    @pl.when(a >= half)
    def _():
        rest.wait_send()

    @pl.when(early & (b == 0))
    def _():
        for src in range(nx_dev):
            spot = rest_in.at[src, :, pl.ds(0, 1)]
            pltpu.make_async_copy(spot, spot, rest_sem.at[1, src]).wait()
            for m in range(kern_in.shape[2]):
                kern_in[1, src, m, 0:1, :] = rest_in[src, m, 0:1, :]

    lane_k = lax.broadcasted_iota(jnp.int32, (pw, LANES), 1)
    pair_row = lax.broadcasted_iota(jnp.int32, (pw, total_y), 0) + mine * pw

    def stiff(which, m):
        if kyw % LANES == 0:
            return jnp.concatenate([kern_in[which, src, m] for src in range(nx_dev)], axis=1)
        pieces = []
        for pair in range(nx_dev // 2):
            one, two = kern_in[which, 2 * pair, m % 5], kern_in[which, 2 * pair + 1, m % 5]
            if m < 5:
                two = pltpu.roll(two, LANES // 2, 1)
            else:
                one = pltpu.roll(one, LANES // 2, 1)
            pieces.append(jnp.where(lane_k < LANES // 2, one, two))
        return jnp.concatenate(pieces, axis=1)

    def push(which, sr, si):
        fr, fi = [], []
        for comp in range(3):
            diag = stiff(which, comp)
            fr.append(diag * sr[comp])
            fi.append(diag * si[comp])
        for m, (c, d) in enumerate(((0, 1), (0, 2), (1, 2))):
            kr, ki = stiff(which, 3 + m), stiff(which, 6 + m)
            fr[c] = fr[c] + kr * sr[d] - ki * si[d]
            fi[c] = fi[c] + kr * si[d] + ki * sr[d]
            fr[d] = fr[d] + kr * sr[c] + ki * si[c]
            fi[d] = fi[d] + kr * si[c] - ki * sr[c]
        return fr, fi

    ends = pair_row == 0
    ar, ai, br, bi = [], [], [], []
    for comp in range(3):
        re_at = slice(comp * pw, (comp + 1) * pw)
        im_at = slice(IM_LANE + comp * pw, IM_LANE + (comp + 1) * pw)
        re_c, re_s, im_c, im_s = cos_part[re_at], sin_part[re_at], cos_part[im_at], sin_part[im_at]
        ar.append(re_c + jnp.where(ends, 0.0, im_s))
        ai.append(jnp.where(ends, 0.0, im_c) - re_s)
        br.append(jnp.where(ends, im_c, re_c - im_s))
        bi.append(jnp.where(ends, -im_s, -im_c - re_s))
    ar, ai = push(0, ar, ai)
    br, bi = push(1, br, bi)
    up, down = [], []
    for comp in range(3):
        up.append(jnp.where(ends, ar[comp], ar[comp] + br[comp]))
        down.append(jnp.where(ends, ai[comp], ai[comp] + bi[comp]))
    for comp in range(3):
        up.append(jnp.where(ends, br[comp], ai[comp] - bi[comp]))
        down.append(jnp.where(ends, bi[comp], br[comp] - ar[comp]))
    waves[: 2 * width] = dot3(jnp.concatenate(up, axis=0), y_tab[0, :, :total_y], y_tab[1, :, :total_y]) - dot3(
        jnp.concatenate(down, axis=0), y_tab[0, :, total_y:], y_tab[1, :, total_y:]
    )
    lane_w = lax.broadcasted_iota(jnp.int32, (pw, LANES), 1)
    quarter = LANES // 4
    for dest in range(ny_dev):
        col, part = dest * rows // LANES * LANES, dest * rows % LANES

        def block_of(index, at):
            piece = waves[index * pw : (index + 1) * pw, col : col + LANES]
            shift = (at - part) % LANES
            return pltpu.roll(piece, shift, 1) if shift else piece

        tile = block_of(3, 3 * quarter)
        for comp in (2, 1, 0):
            tile = jnp.where(lane_w < (comp + 1) * quarter, block_of(comp, comp * quarter), tile)
        send3[dest, :pw] = tile
        tile = jnp.where(lane_w < 2 * quarter, block_of(4, quarter), block_of(5, 2 * quarter))
        if pw == FOLD:
            turned = pltpu.roll(pltpu.roll(tile, LANES // 2, 1), FOLD // 2, 0)
            tile = jnp.where((lane_w >= quarter) & (lane_w < 3 * quarter), tile, turned)
        send3[dest, FOLD : FOLD + pw] = tile
    recv3[mine] = send3[a]
    all_start3()

    loads[4].wait()
    loads[5].wait()

    @pl.loop(0, chunks)
    def _(chunk):
        own_sum = []
        parts = {}
        at = pl.ds(pl.multiple_of(chunk * ROWS, ROWS), ROWS)
        for layer in range(layers):
            codes = [codes_ref[layer, slot, at, :] for slot in range(slots)]
            masks = [masks_ref[layer, slot, at, :] for slot in range(slots)]
            grads = tersoff_rows(layer, layers, slots, shifted, chunk, codes, masks)
            total = [sum(grads[s][comp] for s in range(slots)) for comp in range(3)]
            own_sum.append(total)
            for slot in range(slots):
                for entry, dx, dy, dz in bonds_of(layer, layers, slot):
                    hit = codes[slot] == entry
                    for comp in range(3):
                        key = (dx, dy, layer + dz, comp)
                        term = jnp.where(hit, grads[slot][comp], 0.0)
                        parts[key] = parts[key] + term if key in parts else term
        for level in range(layers):
            for comp in range(3):
                key = (0, 0, level, comp)
                here = own_sum[level][comp]
                parts[key] = here - parts[key] if key in parts else here
        for (dx, dy, level, comp), value in parts.items():
            signed = value if (dx, dy) == (0, 0) else -value
            spill[dx + 1, dy + 1, level, comp, at, :] = signed

    left_pack = jnp.zeros(full, f32)
    right_pack = jnp.zeros(full, f32)
    edge_out[...] = jnp.zeros_like(edge_out)
    for q in range(3 * layers):
        level, comp = q // 3, q % 3
        lines = []
        for dx in (-1, 0, 1):
            part = spill[dx + 1, 1, level, comp]
            down = spill[dx + 1, 2, level, comp]
            up = spill[dx + 1, 0, level, comp]
            part = part + jnp.where(first_row, 0.0, pltpu.roll(down, 1, 0))
            part = part + jnp.where(last_row, 0.0, pltpu.roll(up, rows - 1, 0))
            edge_out[0, dx + 1, q : q + 1, :] = down[rows - 1 : rows]
            edge_out[1, dx + 1, q : q + 1, :] = up[0:1]
            lines.append(part)
        left_pack = jnp.where(lane == q, lines[0][:, 0:1], left_pack)
        right_pack = jnp.where(lane == q, lines[2][:, LANES - 1 : LANES], right_pack)
        out_ref[level, comp] = (
            lines[1]
            + jnp.where(first_lane, 0.0, pltpu.roll(lines[2], 1, 1))
            + jnp.where(last_lane, 0.0, pltpu.roll(lines[0], LANES - 1, 1))
        )
    side_out[0] = right_pack
    side_out[1] = left_pack
    for j in range(2):
        edge_out[j, 1] = (
            edge_out[j, 1]
            + jnp.where(lane1 == 0, 0.0, pltpu.roll(edge_out[j, 2], 1, 1))
            + jnp.where(lane1 == LANES - 1, 0.0, pltpu.roll(edge_out[j, 0], LANES - 1, 1))
        )
    rim = []
    for i, step in enumerate((1, -1)):
        rim.append(remote(side_out.at[i], side_in.at[i], rim_sem, i, beside(step, 0)))
    n = 2
    for j, step_y in enumerate((1, -1)):
        for dx in (-1, 0, 1):
            rim.append(remote(edge_out.at[j, dx + 1], edge_in.at[j, dx + 1], rim_sem, n, beside(dx, step_y)))
            n += 1
    for copy in rim:
        copy.start()

    all_wait3()
    row_w = lax.broadcasted_iota(jnp.int32, (pw, LANES), 0)
    for src in range(count):
        first, second = recv3[src, :pw], recv3[src, FOLD : FOLD + pw]
        if pw == FOLD:
            turned = pltpu.roll(pltpu.roll(second, LANES // 2, 1), FOLD // 2, 0)
            second = jnp.where(row_w < FOLD // 2, second, turned)
        fields[src * pw : (src + 1) * pw] = first
        fields[total_x // 2 + src * pw : total_x // 2 + (src + 1) * pw] = jnp.where(
            lane_w < quarter, pltpu.roll(first, quarter, 1), second
        )
    own_x = pl.ds(pl.multiple_of(b * LANES, LANES), LANES)
    top = fields[...].astype(jnp.bfloat16)
    low_part = (fields[...] - top.astype(f32)).astype(jnp.bfloat16)
    dot = functools.partial(jnp.dot, preferred_element_type=f32)
    lines_x = x_tab[0, own_x, :]
    real = dot(lines_x, top) + (dot(lines_x, low_part) + dot(x_tab[1, own_x, :], top))
    real = jnp.transpose(real) * f32(-1.0 / (total_x * total_y))
    for copy in rim:
        copy.wait()
    for q in range(3 * layers):
        level, comp = q // 3, q % 3
        value = out_ref[level, comp]
        value = value + jnp.where(first_lane, side_in[0][:, q : q + 1], 0.0)
        value = value + jnp.where(last_lane, side_in[1][:, q : q + 1], 0.0)
        for j, edge in enumerate((first_row, last_row)):
            line = edge_in[j, 1, q : q + 1, :]
            value = value + jnp.where(edge, line, 0.0)
            value = value + jnp.where(edge & first_lane, edge_in[j, 2, q : q + 1, LANES - 1 : LANES], 0.0)
            value = value + jnp.where(edge & last_lane, edge_in[j, 0, q : q + 1, 0:1], 0.0)
        out_ref[level, comp] = value
    for comp in range(3):
        out_ref[0, comp] = out_ref[0, comp] + real[comp * rows : (comp + 1) * rows]


def shards(nx_dev, ny_dev, disp, velocity, kinds, neighbours, pad_mask, kernel):
    layers, comps, rows, cols = disp.shape
    slots = neighbours.shape[1]
    total_x, total_y = cols * nx_dev, rows * ny_dev
    count = nx_dev * ny_dev
    kx_block, kyw = kernel.shape[0], kernel.shape[4]
    pw = kx_block // (2 * nx_dev)
    rp = rows // nx_dev
    kern_parts = 9 if kyw % LANES == 0 else 5
    lanes = kyw if kern_parts == 9 else LANES
    x_table = jnp.asarray(line_table(total_x))
    y_table = jnp.asarray(wave_table(total_y))
    chunks = rows // ROWS
    vmem = pl.BlockSpec(memory_space=pltpu.VMEM)
    hbm = pl.BlockSpec(memory_space=pl.ANY)
    tiles = pltpu.VMEM((count, rp, LANES), f32)
    quarter = pltpu.VMEM((nx_dev, 3, rp, LANES), f32)
    sems = lambda n: pltpu.SemaphoreType.DMA((2, n))
    inputs = (disp.reshape(layers, comps, nx_dev, rp, cols), kinds, neighbours, pad_mask, kernel, x_table, y_table)
    force = pl.pallas_call(
        functools.partial(step_kernel, (nx_dev, ny_dev, layers, slots, rows, total_x, total_y, pw, kyw)),
        out_shape=jax.ShapeDtypeStruct(disp.shape, f32),
        in_specs=[hbm] * 7,
        out_specs=vmem,
        scratch_shapes=[
            pltpu.VMEM((layers, comps, nx_dev, rp, cols), f32),
            pltpu.VMEM(kinds.shape, jnp.int32),
            pltpu.VMEM(neighbours.shape, jnp.int32),
            pltpu.VMEM(pad_mask.shape, jnp.int32),
            pltpu.VMEM(((2 * nx_dev + 1) * pw, *kernel.shape[1:]), f32),
            pltpu.VMEM((2 * nx_dev + 1, kern_parts, pw, lanes), f32),
            pltpu.VMEM(x_table.shape, jnp.bfloat16),
            pltpu.VMEM(y_table.shape, jnp.bfloat16),
            quarter,
            pltpu.VMEM((3 * rp, total_x), f32),
            tiles, tiles,
            pltpu.VMEM((ny_dev, 2 * FOLD, LANES), f32),
            pltpu.VMEM((count, 2 * FOLD, LANES), f32),
            pltpu.VMEM((6 * pw, total_y), f32),
            pltpu.VMEM((2, nx_dev, kern_parts, pw, lanes), f32),
            pltpu.VMEM((nx_dev, kern_parts, 8, lanes), f32),
            pltpu.VMEM((total_x, LANES), f32),
            pltpu.VMEM((rows, LANES), f32),
            pltpu.VMEM((4 * layers, LANES), f32),
            pltpu.VMEM((4 * layers, LANES), f32),
            pltpu.VMEM((2, rows, LANES), f32),
            pltpu.VMEM((2, 3, 4 * layers, LANES), f32),
            pltpu.VMEM((3, 3, layers, 4, chunks, ROWS, LANES), f32),
            pltpu.VMEM((3, 3, layers, 3, rows, LANES), f32),
            pltpu.VMEM((2, rows, LANES), f32),
            pltpu.VMEM((2, 3, ROWS, LANES), f32),
            pltpu.VMEM((2, rows, LANES), f32),
            pltpu.VMEM((2, 3, ROWS, LANES), f32),
            pltpu.SemaphoreType.DMA((7,)),
            sems(nx_dev), sems(2 * nx_dev), sems(nx_dev), sems(8), sems(1), sems(1), sems(8),
            pltpu.SemaphoreType.REGULAR,
        ],
        compiler_params=pltpu.CompilerParams(
            collective_id=0, has_side_effects=True, vmem_limit_bytes=44 * 1024 * 1024
        ),
    )(*(pltpu.with_memory_space_constraint(value, pltpu.HBM) for value in inputs))
    new_velocity = velocity + impulse_scale * force
    new_disp = disp + drift_scale * new_velocity
    return (new_disp, new_velocity)


def solution(mesh):
    in_specs = (
        P(None, None, "sy", "sx"),
        P(None, None, "sy", "sx"),
        P(None, "sy", "sx"),
        P(None, None, "sy", "sx"),
        P(None, None, "sy", "sx"),
        P("sy", None, None, None, "sx"),
    )
    out_specs = (P(None, None, "sy", "sx"), P(None, None, "sy", "sx"))
    body = functools.partial(shards, mesh.shape["sx"], mesh.shape["sy"])
    return jax.shard_map(body, mesh=mesh, in_specs=in_specs, out_specs=out_specs, check_vma=False)
```

```python
import functools
import math

import jax
import jax.numpy as jnp
import numpy as np
from jax import lax
from jax.experimental import pallas as pl
from jax.experimental.pallas import tpu as pltpu
from jax.sharding import PartitionSpec as P

silicon = (1830.8, 471.18, 2.4799, 1.7322, 1.1e-06, 0.78734, 100390.0, 16.217, -0.59825, 2.7, 3.0)
germanium = (1769.0, 419.23, 2.4451, 1.7047, 9.0166e-07, 0.75627, 106430.0, 15.652, -0.43884, 2.8, 3.1)
faces = ((1, 0, 0), (0, 1, 0), (0, 0, 1), (-1, 0, 0), (0, -1, 0), (0, 0, -1))
edges = (
    (1, 1, 0), (1, -1, 0), (-1, 1, 0), (-1, -1, 0),
    (1, 0, 1), (1, 0, -1), (-1, 0, 1), (-1, 0, -1),
    (0, 1, 1), (0, 1, -1), (0, -1, 1), (0, -1, -1),
)
FACE_SLOTS = 4
lattice_step = 2.0
impulse_scale = 0.1
drift_scale = 0.05
LANES = 128
ROWS = 8
IM_LANE = 32
FOLD = 8
f32 = jnp.float32
MESH = pl.DeviceIdType.MESH


def split_table(table):
    table = table.astype(np.float32)
    high = table.astype(jnp.bfloat16)
    low = (table - high.astype(np.float32)).astype(jnp.bfloat16)
    return np.stack([high, low])


def angles(length, columns):
    ids = np.arange(length, dtype=np.int64)
    return (ids[:, None] * np.arange(columns, dtype=np.int64)[None, :] % length) * (2.0 * math.pi / length)


def line_table(length):
    half = length // 2
    angle = angles(length, half)
    sines = -np.sin(angle)
    sines[:, 0] = 1.0 - 2.0 * (np.arange(length) % 2)
    return split_table(np.concatenate([np.cos(angle), sines], axis=1))


def wave_table(length):
    angle = angles(length, length)
    return split_table(np.concatenate([np.cos(angle), np.sin(angle)], axis=1))


def dot3(values, high, low):
    count = values.shape[0]
    top = values.astype(jnp.bfloat16)
    coarse = top.astype(f32)
    both = jnp.concatenate([coarse, values - coarse], axis=0).astype(jnp.bfloat16)
    dot = functools.partial(jnp.dot, preferred_element_type=f32)
    twice = dot(both, high)
    return twice[:count] + (twice[count:] + dot(top, low))


def pick(is_ge, same, position, mean):
    si, ge = silicon[position], germanium[position]
    both = math.sqrt(si * ge) if mean == "geo" else 0.5 * (si + ge)
    return jnp.where(same, jnp.where(is_ge, f32(ge), f32(si)), f32(both))


def own_pick(is_ge, si, ge):
    return jnp.where(is_ge, f32(ge), f32(si))


def poly(v2, coefs):
    out = f32(coefs[-1])
    for coef in coefs[-2::-1]:
        out = out * v2 + f32(coef)
    return out


sin_coefs = [(-1) ** k * math.pi ** (2 * k + 1) / math.factorial(2 * k + 1) for k in range(6)]
cos_coefs = [(-1) ** k * math.pi ** (2 * k) / math.factorial(2 * k) for k in range(7)]


def bonds_of(layer, layers, slot):
    table = faces if slot < FACE_SLOTS else edges
    base = 0 if slot < FACE_SLOTS else len(faces)
    for entry, (dx, dy, dz) in enumerate(table):
        if 0 <= layer + dz < layers:
            yield base + entry, dx, dy, dz


def tersoff_rows(layer, layers, slots, shifted, chunk, codes, masks):
    def near(dx, dy, level, comp):
        return shifted[dx + 1, dy + 1, level, comp, chunk]

    own = [near(0, 0, layer, comp) for comp in range(3)]
    own_ge = near(0, 0, layer, 3) > 0.5
    h = own_pick(own_ge, silicon[8], germanium[8])
    d2 = own_pick(own_ge, silicon[7] ** 2, germanium[7] ** 2)
    c2 = own_pick(own_ge, silicon[6] ** 2, germanium[6] ** 2)
    ratio = own_pick(own_ge, silicon[6] ** 2 / silicon[7] ** 2, germanium[6] ** 2 / germanium[7] ** 2)
    beta = own_pick(own_ge, silicon[4], germanium[4])
    power = own_pick(own_ge, silicon[5], germanium[5])
    half_inv = own_pick(own_ge, 0.5 / silicon[5], 0.5 / germanium[5])
    data = []
    for slot in range(slots):
        code = codes[slot]
        bond = [jnp.full(code.shape, lattice_step, f32)] + [jnp.zeros(code.shape, f32) for _ in range(2)]
        kind = jnp.zeros(code.shape, f32)
        valid = jnp.zeros(code.shape, f32)
        for entry, dx, dy, dz in bonds_of(layer, layers, slot):
            hit = code == entry
            for comp, step in enumerate((dx, dy, dz)):
                place = near(dx, dy, layer + dz, comp)
                if step:
                    place = place + f32(lattice_step * step)
                bond[comp] = jnp.where(hit, place - own[comp], bond[comp])
            kind = jnp.where(hit, near(dx, dy, layer + dz, 3), kind)
            valid = jnp.where(hit, f32(1.0), valid)
        live = masks[slot].astype(f32) * valid
        dist2 = bond[0] * bond[0] + bond[1] * bond[1] + bond[2] * bond[2]
        inv = lax.rsqrt(dist2)
        dist = dist2 * inv
        unit = [b * inv for b in bond]
        same = (kind > 0.5) == own_ge
        inner = pick(own_ge, same, 9, "geo")
        span_si = 1.0 / (silicon[10] - silicon[9])
        span_ge = 1.0 / (germanium[10] - germanium[9])
        span_mix = 1.0 / (math.sqrt(silicon[10] * germanium[10]) - math.sqrt(silicon[9] * germanium[9]))
        span = jnp.where(same, jnp.where(own_ge, f32(span_ge), f32(span_si)), f32(span_mix))
        phase = (dist - inner) * span
        v = jnp.clip(phase, 0.0, 1.0) - 0.5
        v2 = v * v
        fade = 0.5 - 0.5 * v * poly(v2, sin_coefs)
        fade_slope = f32(-0.5 * math.pi) * span * poly(v2, cos_coefs)
        below, above = phase < 0.0, phase > 1.0
        cutoff = jnp.where(below, 1.0, jnp.where(above, 0.0, fade))
        slope = jnp.where(below | above, 0.0, fade_slope) * live
        mu = pick(own_ge, same, 3, "mean")
        lam = pick(own_ge, same, 2, "mean")
        attract = pick(own_ge, same, 1, "geo") * jnp.exp(-mu * dist)
        repulse = pick(own_ge, same, 0, "geo") * jnp.exp(-lam * dist)
        data.append(dict(unit=unit, inv=inv, weight=live * cutoff, slope=slope, mu=mu, lam=lam, att=attract, rep=repulse))
    zeta = [jnp.zeros_like(h) for _ in range(slots)]
    for s in range(slots):
        for t in range(s):
            us, ut = data[s]["unit"], data[t]["unit"]
            q = us[0] * ut[0] + us[1] * ut[1] + us[2] * ut[2]
            away = h - q
            gap = away * away
            g = 1.0 + ratio * gap / (d2 + gap)
            zeta[s] = zeta[s] + data[t]["weight"] * g
            zeta[t] = zeta[t] + data[s]["weight"] * g
    pull, radial = [], []
    for s in range(slots):
        item = data[s]
        z = jnp.exp(power * jnp.log(beta * zeta[s]))
        order = jnp.exp(-jnp.log(1.0 + z) * half_inv)
        bound = order * item["att"]
        pull.append(0.25 * item["weight"] * bound * z / (zeta[s] * (1.0 + z)))
        radial.append(
            0.5 * (item["slope"] * (item["rep"] - bound) + item["weight"] * (item["mu"] * bound - item["lam"] * item["rep"]))
        )
    turn = [[jnp.zeros_like(h) for _ in range(3)] for _ in range(slots)]
    spread = [jnp.zeros_like(h) for _ in range(slots)]
    for s in range(slots):
        for t in range(s):
            us, ut = data[s]["unit"], data[t]["unit"]
            q = us[0] * ut[0] + us[1] * ut[1] + us[2] * ut[2]
            away = h - q
            gap = away * away
            inv = 1.0 / (d2 + gap)
            g = 1.0 + ratio * gap * inv
            tilt = -2.0 * c2 * away * inv * inv
            pair = (pull[s] * data[t]["weight"] + pull[t] * data[s]["weight"]) * tilt
            for comp in range(3):
                turn[s][comp] = turn[s][comp] + pair * ut[comp]
                turn[t][comp] = turn[t][comp] + pair * us[comp]
            spread[s] = spread[s] + pull[t] * g
            spread[t] = spread[t] + pull[s] * g
    grads = []
    for s in range(slots):
        item = data[s]
        unit = item["unit"]
        along = turn[s][0] * unit[0] + turn[s][1] * unit[1] + turn[s][2] * unit[2]
        line = radial[s] + item["slope"] * spread[s] - along * item["inv"]
        grads.append([turn[s][comp] * item["inv"] + line * unit[comp] for comp in range(3)])
    return grads


def step_kernel(
    dims,
    disp_hbm, kinds_hbm, codes_hbm, masks_hbm, kern_hbm, x_hbm, y_hbm,
    out_ref,
    disp_ref, kinds_ref, codes_ref, masks_ref, kern_all, kern_out, kern_rest, x_tab, y_tab, line_in, buf, send2, recv2, send3, recv3, waves, kern_in, rest_in, fields,
    col_out, top_out, low_out, col_in, row_in, shifted, spill,
    side_out, edge_out, side_in, edge_in,
    load_sem, p1_sem, k_sem, rest_sem, halo_sem, p2_sem, p3_sem, rim_sem, relay_sem,
):
    nx_dev, ny_dev, layers, slots, rows, total_x, total_y, pw, kyw = dims
    count = nx_dev * ny_dev
    rp = rows // nx_dev
    chunks = rows // ROWS
    b = lax.axis_index("sx")
    a = lax.axis_index("sy")
    me = a * nx_dev + b
    half = ny_dev // 2
    early = a < half
    kind = jnp.where(early, 0, 1)

    def pair_of(dev_x, dev_y):
        first = dev_y < half
        return jnp.where(first, dev_y, ny_dev - 1 - dev_y) * (2 * nx_dev) + dev_x + jnp.where(first, 0, nx_dev)

    mine = pair_of(b, a)
    lane = lax.broadcasted_iota(jnp.int32, (rows, LANES), 1)
    row = lax.broadcasted_iota(jnp.int32, (rows, LANES), 0)
    lane1 = lax.broadcasted_iota(jnp.int32, (ROWS, LANES), 1)

    def wrap(value, size):
        return jnp.where(value >= size, value - size, value)

    def each_other(visit):
        for i in reversed(range(nx_dev)):
            other_x = wrap(b + i, nx_dev)

            def body(j, carry, other_x=other_x):
                visit(other_x, wrap(a + j, ny_dev))
                return carry

            lax.fori_loop(0 if i else 1, ny_dev, body, None, unroll=count <= 64)

    def beside(step_x, step_y):
        return {"sx": wrap(b + step_x % nx_dev, nx_dev), "sy": wrap(a + step_y % ny_dev, ny_dev)}

    def remote(src, dst, sems, index, dev):
        return pltpu.make_async_remote_copy(
            src_ref=src, dst_ref=dst, send_sem=sems.at[0, index], recv_sem=sems.at[1, index],
            device_id=dev, device_id_type=MESH,
        )

    barrier = pltpu.get_barrier_semaphore()

    low = 2 ** ((ny_dev.bit_length() - 1) // 2)
    lines = ny_dev // low
    side, line = lax.rem(a, low), a // low
    cube = [
        {"sx": wrap(b + i, nx_dev), "sy": line * low + wrap(side + j, low)}
        for j in range(low) for i in range(nx_dev) if i or j
    ]
    near = cube + [{"sx": b, "sy": wrap(line + k, lines) * low + side} for k in range(1, lines)]
    for dev in near:
        pl.semaphore_signal(barrier, inc=1, device_id=dev, device_id_type=MESH)

    loads = [
        pltpu.make_async_copy(x_hbm, x_tab, load_sem.at[0]),
        pltpu.make_async_copy(y_hbm, y_tab, load_sem.at[1]),
        pltpu.make_async_copy(disp_hbm, disp_ref, load_sem.at[2]),
        None,
        pltpu.make_async_copy(codes_hbm, codes_ref, load_sem.at[4]),
        pltpu.make_async_copy(masks_hbm, masks_ref, load_sem.at[5]),
        pltpu.make_async_copy(kinds_hbm, kinds_ref, load_sem.at[6]),
    ]
    def stiff_row(slot):
        group, r = slot // pw, slot % pw
        if group == 2 * nx_dev:
            return 0
        o, t = group // nx_dev, group % nx_dev
        late = (o + 1) * nx_dev - 1 - t
        if r:
            late_row = late * pw + pw - r
        else:
            late_row = (late + 1) * pw if late + 1 < 2 * nx_dev else 0
        return jnp.where(early, group * pw + r, late_row)

    for i in (2, 6):
        loads[i].start()
    for slot in range((2 * nx_dev + 1) * pw):
        pltpu.make_async_copy(kern_hbm.at[stiff_row(slot)], kern_all.at[slot], load_sem.at[3]).start()
    for i in (0, 1, 4, 5):
        loads[i].start()

    def field(level, comp):
        if comp < 3:
            return disp_ref[level, comp].reshape(rows, LANES)
        return kinds_ref[level].astype(f32)

    pl.semaphore_wait(barrier, len(near))
    for dev in cube:
        pl.semaphore_signal(relay_sem, inc=1, device_id=dev, device_id_type=MESH)
    loads[2].wait()

    p1 = []
    kc = []
    for k in range(1, nx_dev):
        other = wrap(b + k, nx_dev)
        p1.append(remote(disp_ref.at[0, :, other], line_in.at[b], p1_sem, k, {"sx": other, "sy": a}))
    for copy in p1:
        copy.start()
    for comp in range(3):
        line_in[b, comp] = disp_ref[0, comp, b]
    halo = []
    for i, step in enumerate((1, -1)):
        halo.append(remote(col_out, col_in.at[i], halo_sem, i, beside(step, 0)))
    n = 2
    for j, (step_y, src) in enumerate(((1, low_out), (-1, top_out))):
        for i, step_x in enumerate((1, 0, -1)):
            halo.append(remote(src, row_in.at[j, i], halo_sem, n, beside(step_x, step_y)))
            n += 1
    loads[6].wait()
    packed = jnp.zeros((rows, LANES), f32)
    for q in range(4 * layers):
        base = field(q // 4, q % 4)
        top_out[q : q + 1, :] = base[0:1]
        low_out[q : q + 1, :] = base[rows - 1 : rows]
        packed = jnp.where(lane == q, base[:, 0:1], packed)
        packed = jnp.where(lane == 4 * layers + q, base[:, LANES - 1 : LANES], packed)
    col_out[...] = packed

    pltpu.make_async_copy(kern_all, kern_all, load_sem.at[3]).wait()
    spots = [(c, c, 0) for c in range(3)] + [(c, d, ri) for ri in range(2) for c, d in ((0, 1), (0, 2), (1, 2))]

    def stiff_part(group, m):
        c, d, ri = spots[m]
        return kern_all[group * pw : (group + 1) * pw, c, d, ri, :]

    lane_k = lax.broadcasted_iota(jnp.int32, (pw, LANES), 1)
    for group in range(2 * nx_dev):
        if kyw % LANES == 0:
            for m in range(9):
                kern_out[group, m * pw : (m + 1) * pw] = stiff_part(group, m)
        else:
            for m in range(5):
                high = stiff_part(group, m + 5) if m < 4 else jnp.zeros((pw, kyw), f32)
                tile = jnp.concatenate([stiff_part(group, m), high], axis=1)
                if m == 4 and pw == FOLD:
                    turned = pltpu.roll(pltpu.roll(tile, LANES // 2, 1), FOLD // 2, 0)
                    tile = jnp.where(lane_k < LANES // 2, tile, turned)
                kern_out[group, m * pw : (m + 1) * pw] = tile
    kern_rest[...] = jnp.zeros_like(kern_rest)
    for m in range(9 if kyw % LANES == 0 else 5):
        edge_part = stiff_part(2 * nx_dev, m)
        if kyw % LANES:
            high = stiff_part(2 * nx_dev, m + 5) if m < 4 else jnp.zeros((pw, kyw), f32)
            edge_part = jnp.concatenate([edge_part, high], axis=1)
        kern_rest[m : m + 1] = edge_part[0:1]
    kern_in[kind, b] = kern_out[b]
    used = pl.ds(0, 4 * FOLD + FOLD // 2 if kyw % LANES and pw == FOLD else kern_out.shape[1])
    for k in range(1, nx_dev):
        other = wrap(b + k, nx_dev)
        kc.append(remote(kern_out.at[other, used], kern_in.at[kind, b, used], k_sem, k, {"sx": other, "sy": a}))
    for copy in kc:
        copy.start()
    pl.semaphore_wait(relay_sem, len(cube))
    far = []
    for k in range(nx_dev):
        other = wrap(b + k, nx_dev)
        dev = {"sx": other, "sy": ny_dev - 1 - a}
        far.append(remote(kern_out.at[nx_dev + other, used], kern_in.at[kind, b, used], k_sem, nx_dev + k, dev))
    rest_to = {"sx": jnp.zeros_like(b), "sy": jnp.where(a == half, 0, ny_dev - a)}
    rest = remote(kern_rest, rest_in.at[b], rest_sem, b, rest_to)
    for copy in far:
        copy.start()

    @pl.when(a >= half)
    def _():
        rest.start()

    for copy in p1:
        copy.wait()
    for src in range(nx_dev):
        for comp in range(3):
            buf[comp * rp : (comp + 1) * rp, src * LANES : (src + 1) * LANES] = line_in[src, comp]
    loads[0].wait()
    buf[...] = dot3(buf[:, :total_x], x_tab[0], x_tab[1])
    per = LANES // pw
    lane_p = lax.broadcasted_iota(jnp.int32, (rp, LANES), 1)
    for dest in range(count):
        block, part = dest // per, dest % per
        tile = jnp.zeros((rp, LANES), f32)
        for ri in range(2):
            for comp in range(3):
                at = ri * IM_LANE + comp * pw
                col = ri * (total_x // 2) + block * LANES
                piece = buf[comp * rp : (comp + 1) * rp, col : col + LANES]
                shift = (at - part * pw) % LANES
                if shift:
                    piece = pltpu.roll(piece, shift, 1)
                tile = jnp.where((lane_p >= at) & (lane_p < at + pw), piece, tile)
        if rp == FOLD:
            turned = pltpu.roll(pltpu.roll(tile, LANES // 2, 1), FOLD // 2, 0)
            tile = jnp.where(lane_p < LANES // 2, tile, turned)
        send2[dest] = tile
    recv2[me] = send2[mine]
    some_rows = pl.ds(0, rp // 2 if rp == FOLD else rp)

    def all_start2():
        def send(other_x, other_y):
            src = send2.at[pair_of(other_x, other_y), some_rows]
            remote(src, recv2.at[me, some_rows], p2_sem, 0, {"sx": other_x, "sy": other_y}).start()

        each_other(send)

    lot = pl.ds(0, FOLD + (FOLD // 2 if pw == FOLD else pw))

    def all_start3():
        def send(other_x, other_y):
            src = send3.at[other_y, lot]
            remote(src, recv3.at[mine, lot], p3_sem, 0, {"sx": other_x, "sy": other_y}).start()

        each_other(send)

    def all_wait3():
        for i in range(nx_dev):
            some = send3.at[pl.ds(0, ny_dev - (1 if i == 0 else 0)), lot]
            pltpu.make_async_copy(some, some, p3_sem.at[0, 0]).wait()
        some = recv3.at[pl.ds(0, count - 1), lot]
        pltpu.make_async_copy(some, some, p3_sem.at[1, 0]).wait()

    def all_wait2():
        some = pl.ds(0, count - 1)
        pltpu.make_async_copy(send2.at[some, some_rows], send2.at[some, some_rows], p2_sem.at[0, 0]).wait()
        pltpu.make_async_copy(recv2.at[some, some_rows], recv2.at[some, some_rows], p2_sem.at[1, 0]).wait()

    for copy in halo:
        copy.start()
    all_start2()

    for copy in halo:
        copy.wait()
    first_row, last_row = row == 0, row == rows - 1
    first_lane, last_lane = lane == 0, lane == LANES - 1
    full = (rows, LANES)

    def keep(dx, dy, q, value):
        for chunk in range(chunks):
            shifted[dx + 1, dy + 1, q // 4, q % 4, chunk] = value[chunk * ROWS : (chunk + 1) * ROWS]

    for q in range(4 * layers):
        base = field(q // 4, q % 4)
        left = jnp.broadcast_to(col_in[0][:, 4 * layers + q : 4 * layers + q + 1], full)
        right = jnp.broadcast_to(col_in[1][:, q : q + 1], full)
        for dy in (-1, 0, 1):
            if dy == 0:
                mid, lo, hi = base, left, right
            else:
                edge = first_row if dy == -1 else last_row
                j = 0 if dy == -1 else 1
                turn = 1 if dy == -1 else rows - 1
                mid = jnp.where(edge, row_in[j, 1, q : q + 1, :], pltpu.roll(base, turn, 0))
                lo = jnp.where(edge, row_in[j, 0, q : q + 1, LANES - 1 : LANES], pltpu.roll(left, turn, 0))
                hi = jnp.where(edge, row_in[j, 2, q : q + 1, 0:1], pltpu.roll(right, turn, 0))
            keep(0, dy, q, mid)
            keep(-1, dy, q, jnp.where(first_lane, lo, pltpu.roll(mid, 1, 1)))
            keep(1, dy, q, jnp.where(last_lane, hi, pltpu.roll(mid, LANES - 1, 1)))

    for copy in kc:
        copy.wait()
    loads[1].wait()
    all_wait2()
    width = 3 * pw

    for src in range(count if rp == FOLD else 0):
        tile = recv2[src]
        turned = pltpu.roll(pltpu.roll(tile, LANES // 2, 1), FOLD // 2, 0)
        recv2[src] = jnp.where(lax.broadcasted_iota(jnp.int32, (rp, LANES), 0) < FOLD // 2, tile, turned)
    table = jnp.transpose(recv2[...].reshape(total_y, LANES))[: 2 * IM_LANE]
    both = dot3(table, y_tab[0], y_tab[1])
    cos_part, sin_part = both[:, :total_y], both[:, total_y:]
    for copy in far:
        copy.wait()

    @pl.when(a >= half)
    def _():
        rest.wait_send()

    @pl.when(early & (b == 0))
    def _():
        for src in range(nx_dev):
            pltpu.make_async_copy(rest_in.at[src], rest_in.at[src], rest_sem.at[1, src]).wait()
            for m in range(9 if kyw % LANES == 0 else 5):
                line = rest_in[src, m : m + 1, :]
                if m == 4 and kyw % LANES:
                    line = jnp.where(lane_k[0:1] < LANES // 2, line, kern_in[1, src, m * pw : m * pw + 1, :])
                kern_in[1, src, m * pw : m * pw + 1, :] = line

    row_k = lax.broadcasted_iota(jnp.int32, (pw, LANES), 0)
    pair_row = lax.broadcasted_iota(jnp.int32, (pw, total_y), 0) + mine * pw

    def stiff(which, m):
        if kyw % LANES == 0:
            return jnp.concatenate([kern_in[which, src, m * pw : (m + 1) * pw] for src in range(nx_dev)], axis=1)

        def tile_of(src):
            tile = kern_in[which, src, m % 5 * pw : (m % 5 + 1) * pw]
            if m == 4 and pw == FOLD:
                turned = pltpu.roll(pltpu.roll(tile, LANES // 2, 1), FOLD // 2, 0)
                tile = jnp.where(row_k < FOLD // 2, tile, turned)
            return tile

        pieces = []
        for pair in range(nx_dev // 2):
            one, two = tile_of(2 * pair), tile_of(2 * pair + 1)
            if m < 5:
                two = pltpu.roll(two, LANES // 2, 1)
            else:
                one = pltpu.roll(one, LANES // 2, 1)
            pieces.append(jnp.where(lane_k < LANES // 2, one, two))
        return jnp.concatenate(pieces, axis=1)

    def push(which, sr, si):
        fr, fi = [], []
        for comp in range(3):
            diag = stiff(which, comp)
            fr.append(diag * sr[comp])
            fi.append(diag * si[comp])
        for m, (c, d) in enumerate(((0, 1), (0, 2), (1, 2))):
            kr, ki = stiff(which, 3 + m), stiff(which, 6 + m)
            fr[c] = fr[c] + kr * sr[d] - ki * si[d]
            fi[c] = fi[c] + kr * si[d] + ki * sr[d]
            fr[d] = fr[d] + kr * sr[c] + ki * si[c]
            fi[d] = fi[d] + kr * si[c] - ki * sr[c]
        return fr, fi

    ends = pair_row == 0
    ar, ai, br, bi = [], [], [], []
    for comp in range(3):
        re_at = slice(comp * pw, (comp + 1) * pw)
        im_at = slice(IM_LANE + comp * pw, IM_LANE + (comp + 1) * pw)
        re_c, re_s, im_c, im_s = cos_part[re_at], sin_part[re_at], cos_part[im_at], sin_part[im_at]
        ar.append(re_c + jnp.where(ends, 0.0, im_s))
        ai.append(jnp.where(ends, 0.0, im_c) - re_s)
        br.append(jnp.where(ends, im_c, re_c - im_s))
        bi.append(jnp.where(ends, -im_s, -im_c - re_s))
    ar, ai = push(0, ar, ai)
    br, bi = push(1, br, bi)
    up, down = [], []
    for comp in range(3):
        up.append(jnp.where(ends, ar[comp], ar[comp] + br[comp]))
        down.append(jnp.where(ends, ai[comp], ai[comp] + bi[comp]))
    for comp in range(3):
        up.append(jnp.where(ends, br[comp], ai[comp] - bi[comp]))
        down.append(jnp.where(ends, bi[comp], br[comp] - ar[comp]))
    waves[: 2 * width] = dot3(jnp.concatenate(up, axis=0), y_tab[0, :, :total_y], y_tab[1, :, :total_y]) - dot3(
        jnp.concatenate(down, axis=0), y_tab[0, :, total_y:], y_tab[1, :, total_y:]
    )
    lane_w = lax.broadcasted_iota(jnp.int32, (pw, LANES), 1)
    quarter = LANES // 4
    for dest in range(ny_dev):
        col, part = dest * rows // LANES * LANES, dest * rows % LANES

        def block_of(index, at):
            piece = waves[index * pw : (index + 1) * pw, col : col + LANES]
            shift = (at - part) % LANES
            return pltpu.roll(piece, shift, 1) if shift else piece

        tile = block_of(3, 3 * quarter)
        for comp in (2, 1, 0):
            tile = jnp.where(lane_w < (comp + 1) * quarter, block_of(comp, comp * quarter), tile)
        send3[dest, :pw] = tile
        tile = jnp.where(lane_w < 2 * quarter, block_of(4, quarter), block_of(5, 2 * quarter))
        if pw == FOLD:
            turned = pltpu.roll(pltpu.roll(tile, LANES // 2, 1), FOLD // 2, 0)
            tile = jnp.where((lane_w >= quarter) & (lane_w < 3 * quarter), tile, turned)
        send3[dest, FOLD : FOLD + pw] = tile
    recv3[mine] = send3[a]
    all_start3()

    loads[4].wait()
    loads[5].wait()

    @pl.loop(0, chunks)
    def _(chunk):
        own_sum = []
        parts = {}
        at = pl.ds(pl.multiple_of(chunk * ROWS, ROWS), ROWS)
        for layer in range(layers):
            codes = [codes_ref[layer, slot, at, :] for slot in range(slots)]
            masks = [masks_ref[layer, slot, at, :] for slot in range(slots)]
            grads = tersoff_rows(layer, layers, slots, shifted, chunk, codes, masks)
            total = [sum(grads[s][comp] for s in range(slots)) for comp in range(3)]
            own_sum.append(total)
            for slot in range(slots):
                for entry, dx, dy, dz in bonds_of(layer, layers, slot):
                    hit = codes[slot] == entry
                    for comp in range(3):
                        key = (dx, dy, layer + dz, comp)
                        term = jnp.where(hit, grads[slot][comp], 0.0)
                        parts[key] = parts[key] + term if key in parts else term
        for level in range(layers):
            for comp in range(3):
                key = (0, 0, level, comp)
                here = own_sum[level][comp]
                parts[key] = here - parts[key] if key in parts else here
        for (dx, dy, level, comp), value in parts.items():
            signed = value if (dx, dy) == (0, 0) else -value
            spill[dx + 1, dy + 1, level, comp, at, :] = signed

    left_pack = jnp.zeros(full, f32)
    right_pack = jnp.zeros(full, f32)
    edge_out[...] = jnp.zeros_like(edge_out)
    for q in range(3 * layers):
        level, comp = q // 3, q % 3
        lines = []
        for dx in (-1, 0, 1):
            part = spill[dx + 1, 1, level, comp]
            down = spill[dx + 1, 2, level, comp]
            up = spill[dx + 1, 0, level, comp]
            part = part + jnp.where(first_row, 0.0, pltpu.roll(down, 1, 0))
            part = part + jnp.where(last_row, 0.0, pltpu.roll(up, rows - 1, 0))
            edge_out[0, dx + 1, q : q + 1, :] = down[rows - 1 : rows]
            edge_out[1, dx + 1, q : q + 1, :] = up[0:1]
            lines.append(part)
        left_pack = jnp.where(lane == q, lines[0][:, 0:1], left_pack)
        right_pack = jnp.where(lane == q, lines[2][:, LANES - 1 : LANES], right_pack)
        out_ref[level, comp] = (
            lines[1]
            + jnp.where(first_lane, 0.0, pltpu.roll(lines[2], 1, 1))
            + jnp.where(last_lane, 0.0, pltpu.roll(lines[0], LANES - 1, 1))
        )
    side_out[0] = right_pack
    side_out[1] = left_pack
    for j in range(2):
        edge_out[j, 1] = (
            edge_out[j, 1]
            + jnp.where(lane1 == 0, 0.0, pltpu.roll(edge_out[j, 2], 1, 1))
            + jnp.where(lane1 == LANES - 1, 0.0, pltpu.roll(edge_out[j, 0], LANES - 1, 1))
        )
    rim = []
    for i, step in enumerate((1, -1)):
        rim.append(remote(side_out.at[i], side_in.at[i], rim_sem, i, beside(step, 0)))
    n = 2
    for j, step_y in enumerate((1, -1)):
        for dx in (-1, 0, 1):
            rim.append(remote(edge_out.at[j, dx + 1], edge_in.at[j, dx + 1], rim_sem, n, beside(dx, step_y)))
            n += 1
    for copy in rim:
        copy.start()

    all_wait3()
    row_w = lax.broadcasted_iota(jnp.int32, (pw, LANES), 0)
    for src in range(count):
        first, second = recv3[src, :pw], recv3[src, FOLD : FOLD + pw]
        if pw == FOLD:
            turned = pltpu.roll(pltpu.roll(second, LANES // 2, 1), FOLD // 2, 0)
            second = jnp.where(row_w < FOLD // 2, second, turned)
        fields[src * pw : (src + 1) * pw] = first
        fields[total_x // 2 + src * pw : total_x // 2 + (src + 1) * pw] = jnp.where(
            lane_w < quarter, pltpu.roll(first, quarter, 1), second
        )
    own_x = pl.ds(pl.multiple_of(b * LANES, LANES), LANES)
    top = fields[...].astype(jnp.bfloat16)
    low_part = (fields[...] - top.astype(f32)).astype(jnp.bfloat16)
    dot = functools.partial(jnp.dot, preferred_element_type=f32)
    lines_x = x_tab[0, own_x, :]
    real = dot(lines_x, top) + (dot(lines_x, low_part) + dot(x_tab[1, own_x, :], top))
    real = jnp.transpose(real) * f32(-1.0 / (total_x * total_y))
    for copy in rim:
        copy.wait()
    for q in range(3 * layers):
        level, comp = q // 3, q % 3
        value = out_ref[level, comp]
        value = value + jnp.where(first_lane, side_in[0][:, q : q + 1], 0.0)
        value = value + jnp.where(last_lane, side_in[1][:, q : q + 1], 0.0)
        for j, edge in enumerate((first_row, last_row)):
            line = edge_in[j, 1, q : q + 1, :]
            value = value + jnp.where(edge, line, 0.0)
            value = value + jnp.where(edge & first_lane, edge_in[j, 2, q : q + 1, LANES - 1 : LANES], 0.0)
            value = value + jnp.where(edge & last_lane, edge_in[j, 0, q : q + 1, 0:1], 0.0)
        out_ref[level, comp] = value
    for comp in range(3):
        out_ref[0, comp] = out_ref[0, comp] + real[comp * rows : (comp + 1) * rows]


def shards(nx_dev, ny_dev, disp, velocity, kinds, neighbours, pad_mask, kernel):
    layers, comps, rows, cols = disp.shape
    slots = neighbours.shape[1]
    total_x, total_y = cols * nx_dev, rows * ny_dev
    count = nx_dev * ny_dev
    kx_block, kyw = kernel.shape[0], kernel.shape[4]
    pw = kx_block // (2 * nx_dev)
    rp = rows // nx_dev
    kern_parts = 9 if kyw % LANES == 0 else 5
    lanes = kyw if kern_parts == 9 else LANES
    x_table = jnp.asarray(line_table(total_x))
    y_table = jnp.asarray(wave_table(total_y))
    chunks = rows // ROWS
    vmem = pl.BlockSpec(memory_space=pltpu.VMEM)
    hbm = pl.BlockSpec(memory_space=pl.ANY)
    tiles = pltpu.VMEM((count, rp, LANES), f32)
    quarter = pltpu.VMEM((nx_dev, 3, rp, LANES), f32)
    sems = lambda n: pltpu.SemaphoreType.DMA((2, n))
    inputs = (disp.reshape(layers, comps, nx_dev, rp, cols), kinds, neighbours, pad_mask, kernel, x_table, y_table)
    force = pl.pallas_call(
        functools.partial(step_kernel, (nx_dev, ny_dev, layers, slots, rows, total_x, total_y, pw, kyw)),
        out_shape=jax.ShapeDtypeStruct(disp.shape, f32),
        in_specs=[hbm] * 7,
        out_specs=vmem,
        scratch_shapes=[
            pltpu.VMEM((layers, comps, nx_dev, rp, cols), f32),
            pltpu.VMEM(kinds.shape, jnp.int32),
            pltpu.VMEM(neighbours.shape, jnp.int32),
            pltpu.VMEM(pad_mask.shape, jnp.int32),
            pltpu.VMEM(((2 * nx_dev + 1) * pw, *kernel.shape[1:]), f32),
            pltpu.VMEM((2 * nx_dev, kern_parts * pw, lanes), f32),
            pltpu.VMEM((2 * ROWS, lanes), f32),
            pltpu.VMEM(x_table.shape, jnp.bfloat16),
            pltpu.VMEM(y_table.shape, jnp.bfloat16),
            quarter,
            pltpu.VMEM((3 * rp, total_x), f32),
            tiles, tiles,
            pltpu.VMEM((ny_dev, 2 * FOLD, LANES), f32),
            pltpu.VMEM((count, 2 * FOLD, LANES), f32),
            pltpu.VMEM((6 * pw, total_y), f32),
            pltpu.VMEM((2, nx_dev, kern_parts * pw, lanes), f32),
            pltpu.VMEM((nx_dev, 2 * ROWS, lanes), f32),
            pltpu.VMEM((total_x, LANES), f32),
            pltpu.VMEM((rows, LANES), f32),
            pltpu.VMEM((4 * layers, LANES), f32),
            pltpu.VMEM((4 * layers, LANES), f32),
            pltpu.VMEM((2, rows, LANES), f32),
            pltpu.VMEM((2, 3, 4 * layers, LANES), f32),
            pltpu.VMEM((3, 3, layers, 4, chunks, ROWS, LANES), f32),
            pltpu.VMEM((3, 3, layers, 3, rows, LANES), f32),
            pltpu.VMEM((2, rows, LANES), f32),
            pltpu.VMEM((2, 3, ROWS, LANES), f32),
            pltpu.VMEM((2, rows, LANES), f32),
            pltpu.VMEM((2, 3, ROWS, LANES), f32),
            pltpu.SemaphoreType.DMA((7,)),
            sems(nx_dev), sems(2 * nx_dev), sems(nx_dev), sems(8), sems(1), sems(1), sems(8),
            pltpu.SemaphoreType.REGULAR,
        ],
        compiler_params=pltpu.CompilerParams(
            collective_id=0, has_side_effects=True, vmem_limit_bytes=44 * 1024 * 1024
        ),
    )(*(pltpu.with_memory_space_constraint(value, pltpu.HBM) for value in inputs))
    new_velocity = velocity + impulse_scale * force
    new_disp = disp + drift_scale * new_velocity
    return (new_disp, new_velocity)


def solution(mesh):
    in_specs = (
        P(None, None, "sy", "sx"),
        P(None, None, "sy", "sx"),
        P(None, "sy", "sx"),
        P(None, None, "sy", "sx"),
        P(None, None, "sy", "sx"),
        P("sy", None, None, None, "sx"),
    )
    out_specs = (P(None, None, "sy", "sx"), P(None, None, "sy", "sx"))
    body = functools.partial(shards, mesh.shape["sx"], mesh.shape["sy"])
    return jax.shard_map(body, mesh=mesh, in_specs=in_specs, out_specs=out_specs, check_vma=False)
```

```python
import functools
import math

import jax
import jax.numpy as jnp
import numpy as np
from jax import lax
from jax.experimental import pallas as pl
from jax.experimental.pallas import tpu as pltpu
from jax.sharding import PartitionSpec as P

silicon = (1830.8, 471.18, 2.4799, 1.7322, 1.1e-06, 0.78734, 100390.0, 16.217, -0.59825, 2.7, 3.0)
germanium = (1769.0, 419.23, 2.4451, 1.7047, 9.0166e-07, 0.75627, 106430.0, 15.652, -0.43884, 2.8, 3.1)
faces = ((1, 0, 0), (0, 1, 0), (0, 0, 1), (-1, 0, 0), (0, -1, 0), (0, 0, -1))
edges = (
    (1, 1, 0), (1, -1, 0), (-1, 1, 0), (-1, -1, 0),
    (1, 0, 1), (1, 0, -1), (-1, 0, 1), (-1, 0, -1),
    (0, 1, 1), (0, 1, -1), (0, -1, 1), (0, -1, -1),
)
FACE_SLOTS = 4
lattice_step = 2.0
impulse_scale = 0.1
drift_scale = 0.05
LANES = 128
ROWS = 8
IM_LANE = 32
FOLD = 8
f32 = jnp.float32
MESH = pl.DeviceIdType.MESH


def split_table(table):
    table = table.astype(np.float32)
    high = table.astype(jnp.bfloat16)
    low = (table - high.astype(np.float32)).astype(jnp.bfloat16)
    return np.stack([high, low])


def angles(length, columns):
    ids = np.arange(length, dtype=np.int64)
    return (ids[:, None] * np.arange(columns, dtype=np.int64)[None, :] % length) * (2.0 * math.pi / length)


def line_table(length):
    half = length // 2
    angle = angles(length, half)
    sines = -np.sin(angle)
    sines[:, 0] = 1.0 - 2.0 * (np.arange(length) % 2)
    return split_table(np.concatenate([np.cos(angle), sines], axis=1))


def wave_table(length):
    angle = angles(length, length)
    return split_table(np.concatenate([np.cos(angle), np.sin(angle)], axis=1))


def dot3(values, high, low):
    count = values.shape[0]
    top = values.astype(jnp.bfloat16)
    coarse = top.astype(f32)
    both = jnp.concatenate([coarse, values - coarse], axis=0).astype(jnp.bfloat16)
    dot = functools.partial(jnp.dot, preferred_element_type=f32)
    twice = dot(both, high)
    return twice[:count] + (twice[count:] + dot(top, low))


def pick(is_ge, same, position, mean):
    si, ge = silicon[position], germanium[position]
    both = math.sqrt(si * ge) if mean == "geo" else 0.5 * (si + ge)
    return jnp.where(same, jnp.where(is_ge, f32(ge), f32(si)), f32(both))


def own_pick(is_ge, si, ge):
    return jnp.where(is_ge, f32(ge), f32(si))


def poly(v2, coefs):
    out = f32(coefs[-1])
    for coef in coefs[-2::-1]:
        out = out * v2 + f32(coef)
    return out


sin_coefs = [(-1) ** k * math.pi ** (2 * k + 1) / math.factorial(2 * k + 1) for k in range(6)]
cos_coefs = [(-1) ** k * math.pi ** (2 * k) / math.factorial(2 * k) for k in range(7)]


def bonds_of(layer, layers, slot):
    table = faces if slot < FACE_SLOTS else edges
    base = 0 if slot < FACE_SLOTS else len(faces)
    for entry, (dx, dy, dz) in enumerate(table):
        if 0 <= layer + dz < layers:
            yield base + entry, dx, dy, dz


def tersoff_rows(layer, layers, slots, shifted, chunk, codes, masks):
    def near(dx, dy, level, comp):
        return shifted[dx + 1, dy + 1, level, comp, chunk]

    own = [near(0, 0, layer, comp) for comp in range(3)]
    own_ge = near(0, 0, layer, 3) > 0.5
    h = own_pick(own_ge, silicon[8], germanium[8])
    d2 = own_pick(own_ge, silicon[7] ** 2, germanium[7] ** 2)
    c2 = own_pick(own_ge, silicon[6] ** 2, germanium[6] ** 2)
    ratio = own_pick(own_ge, silicon[6] ** 2 / silicon[7] ** 2, germanium[6] ** 2 / germanium[7] ** 2)
    beta = own_pick(own_ge, silicon[4], germanium[4])
    power = own_pick(own_ge, silicon[5], germanium[5])
    half_inv = own_pick(own_ge, 0.5 / silicon[5], 0.5 / germanium[5])
    data = []
    for slot in range(slots):
        code = codes[slot]
        bond = [jnp.full(code.shape, lattice_step, f32)] + [jnp.zeros(code.shape, f32) for _ in range(2)]
        kind = jnp.zeros(code.shape, f32)
        valid = jnp.zeros(code.shape, f32)
        for entry, dx, dy, dz in bonds_of(layer, layers, slot):
            hit = code == entry
            for comp, step in enumerate((dx, dy, dz)):
                place = near(dx, dy, layer + dz, comp)
                if step:
                    place = place + f32(lattice_step * step)
                bond[comp] = jnp.where(hit, place - own[comp], bond[comp])
            kind = jnp.where(hit, near(dx, dy, layer + dz, 3), kind)
            valid = jnp.where(hit, f32(1.0), valid)
        live = masks[slot].astype(f32) * valid
        dist2 = bond[0] * bond[0] + bond[1] * bond[1] + bond[2] * bond[2]
        inv = lax.rsqrt(dist2)
        dist = dist2 * inv
        unit = [b * inv for b in bond]
        same = (kind > 0.5) == own_ge
        inner = pick(own_ge, same, 9, "geo")
        span_si = 1.0 / (silicon[10] - silicon[9])
        span_ge = 1.0 / (germanium[10] - germanium[9])
        span_mix = 1.0 / (math.sqrt(silicon[10] * germanium[10]) - math.sqrt(silicon[9] * germanium[9]))
        span = jnp.where(same, jnp.where(own_ge, f32(span_ge), f32(span_si)), f32(span_mix))
        phase = (dist - inner) * span
        v = jnp.clip(phase, 0.0, 1.0) - 0.5
        v2 = v * v
        fade = 0.5 - 0.5 * v * poly(v2, sin_coefs)
        fade_slope = f32(-0.5 * math.pi) * span * poly(v2, cos_coefs)
        below, above = phase < 0.0, phase > 1.0
        cutoff = jnp.where(below, 1.0, jnp.where(above, 0.0, fade))
        slope = jnp.where(below | above, 0.0, fade_slope) * live
        mu = pick(own_ge, same, 3, "mean")
        lam = pick(own_ge, same, 2, "mean")
        attract = pick(own_ge, same, 1, "geo") * jnp.exp(-mu * dist)
        repulse = pick(own_ge, same, 0, "geo") * jnp.exp(-lam * dist)
        data.append(dict(unit=unit, inv=inv, weight=live * cutoff, slope=slope, mu=mu, lam=lam, att=attract, rep=repulse))
    zeta = [jnp.zeros_like(h) for _ in range(slots)]
    for s in range(slots):
        for t in range(s):
            us, ut = data[s]["unit"], data[t]["unit"]
            q = us[0] * ut[0] + us[1] * ut[1] + us[2] * ut[2]
            away = h - q
            gap = away * away
            g = 1.0 + ratio * gap / (d2 + gap)
            zeta[s] = zeta[s] + data[t]["weight"] * g
            zeta[t] = zeta[t] + data[s]["weight"] * g
    pull, radial = [], []
    for s in range(slots):
        item = data[s]
        z = jnp.exp(power * jnp.log(beta * zeta[s]))
        order = jnp.exp(-jnp.log(1.0 + z) * half_inv)
        bound = order * item["att"]
        pull.append(0.25 * item["weight"] * bound * z / (zeta[s] * (1.0 + z)))
        radial.append(
            0.5 * (item["slope"] * (item["rep"] - bound) + item["weight"] * (item["mu"] * bound - item["lam"] * item["rep"]))
        )
    turn = [[jnp.zeros_like(h) for _ in range(3)] for _ in range(slots)]
    spread = [jnp.zeros_like(h) for _ in range(slots)]
    for s in range(slots):
        for t in range(s):
            us, ut = data[s]["unit"], data[t]["unit"]
            q = us[0] * ut[0] + us[1] * ut[1] + us[2] * ut[2]
            away = h - q
            gap = away * away
            inv = 1.0 / (d2 + gap)
            g = 1.0 + ratio * gap * inv
            tilt = -2.0 * c2 * away * inv * inv
            pair = (pull[s] * data[t]["weight"] + pull[t] * data[s]["weight"]) * tilt
            for comp in range(3):
                turn[s][comp] = turn[s][comp] + pair * ut[comp]
                turn[t][comp] = turn[t][comp] + pair * us[comp]
            spread[s] = spread[s] + pull[t] * g
            spread[t] = spread[t] + pull[s] * g
    grads = []
    for s in range(slots):
        item = data[s]
        unit = item["unit"]
        along = turn[s][0] * unit[0] + turn[s][1] * unit[1] + turn[s][2] * unit[2]
        line = radial[s] + item["slope"] * spread[s] - along * item["inv"]
        grads.append([turn[s][comp] * item["inv"] + line * unit[comp] for comp in range(3)])
    return grads


def step_kernel(
    dims,
    disp_hbm, kinds_hbm, codes_hbm, masks_hbm, kern_hbm, x_hbm, y_hbm,
    out_ref,
    disp_ref, kinds_ref, codes_ref, masks_ref, kern_all, kern_out, kern_rest, x_tab, y_tab, line_in, buf, send2, recv2, send3, recv3, waves, kern_in, rest_in, fields,
    col_out, top_out, low_out, col_in, row_in, spot_out, spot_in, shifted, spill,
    side_out, edge_out, side_in, edge_in, tip_out, tip_in,
    load_sem, p1_sem, k_sem, rest_sem, halo_sem, p2_sem, p3_sem, rim_sem, relay_sem,
):
    nx_dev, ny_dev, layers, slots, rows, total_x, total_y, pw, kyw = dims
    count = nx_dev * ny_dev
    rp = rows // nx_dev
    chunks = rows // ROWS
    b = lax.axis_index("sx")
    a = lax.axis_index("sy")
    me = a * nx_dev + b
    half = ny_dev // 2
    early = a < half
    kind = jnp.where(early, 0, 1)

    def pair_of(dev_x, dev_y):
        first = dev_y < half
        return jnp.where(first, dev_y, ny_dev - 1 - dev_y) * (2 * nx_dev) + dev_x + jnp.where(first, 0, nx_dev)

    mine = pair_of(b, a)
    lane = lax.broadcasted_iota(jnp.int32, (rows, LANES), 1)
    row = lax.broadcasted_iota(jnp.int32, (rows, LANES), 0)
    lane1 = lax.broadcasted_iota(jnp.int32, (ROWS, LANES), 1)

    def wrap(value, size):
        return jnp.where(value >= size, value - size, value)

    def each_other(visit):
        for i in reversed(range(nx_dev)):
            other_x = wrap(b + i, nx_dev)

            def body(j, carry, other_x=other_x):
                visit(other_x, wrap(a + j, ny_dev))
                return carry

            lax.fori_loop(0 if i else 1, ny_dev, body, None, unroll=count <= 64)

    def beside(step_x, step_y):
        return {"sx": wrap(b + step_x % nx_dev, nx_dev), "sy": wrap(a + step_y % ny_dev, ny_dev)}

    def remote(src, dst, sems, index, dev):
        return pltpu.make_async_remote_copy(
            src_ref=src, dst_ref=dst, send_sem=sems.at[0, index], recv_sem=sems.at[1, index],
            device_id=dev, device_id_type=MESH,
        )

    barrier = pltpu.get_barrier_semaphore()

    low = 2 ** ((ny_dev.bit_length() - 1) // 2)
    lines = ny_dev // low
    side, line = lax.rem(a, low), a // low
    cube = [
        {"sx": wrap(b + i, nx_dev), "sy": line * low + wrap(side + j, low)}
        for j in range(low) for i in range(nx_dev) if i or j
    ]
    near = cube + [{"sx": b, "sy": wrap(line + k, lines) * low + side} for k in range(1, lines)]
    for dev in near:
        pl.semaphore_signal(barrier, inc=1, device_id=dev, device_id_type=MESH)

    loads = [
        pltpu.make_async_copy(x_hbm, x_tab, load_sem.at[0]),
        pltpu.make_async_copy(y_hbm, y_tab, load_sem.at[1]),
        pltpu.make_async_copy(disp_hbm, disp_ref, load_sem.at[2]),
        None,
        pltpu.make_async_copy(codes_hbm, codes_ref, load_sem.at[4]),
        pltpu.make_async_copy(masks_hbm, masks_ref, load_sem.at[5]),
        pltpu.make_async_copy(kinds_hbm, kinds_ref, load_sem.at[6]),
    ]
    def stiff_row(slot):
        group, r = slot // pw, slot % pw
        if group == 2 * nx_dev:
            return 0
        o, t = group // nx_dev, group % nx_dev
        late = (o + 1) * nx_dev - 1 - t
        if r:
            late_row = late * pw + pw - r
        else:
            late_row = (late + 1) * pw if late + 1 < 2 * nx_dev else 0
        return jnp.where(early, group * pw + r, late_row)

    for i in (2, 6):
        loads[i].start()
    for slot in range((2 * nx_dev + 1) * pw):
        pltpu.make_async_copy(kern_hbm.at[stiff_row(slot)], kern_all.at[slot], load_sem.at[3]).start()
    for i in (0, 1, 4, 5):
        loads[i].start()

    def field(level, comp):
        if comp < 3:
            return disp_ref[level, comp].reshape(rows, LANES)
        return kinds_ref[level].astype(f32)

    pl.semaphore_wait(barrier, len(near))
    for dev in cube:
        pl.semaphore_signal(relay_sem, inc=1, device_id=dev, device_id_type=MESH)
    loads[2].wait()

    p1 = []
    kc = []
    for k in range(1, nx_dev):
        other = wrap(b + k, nx_dev)
        p1.append(remote(disp_ref.at[0, :, other], line_in.at[b], p1_sem, k, {"sx": other, "sy": a}))
    for copy in p1:
        copy.start()
    for comp in range(3):
        line_in[b, comp] = disp_ref[0, comp, b]
    halo = []
    for i, step in enumerate((1, -1)):
        halo.append(remote(col_out, col_in.at[i], halo_sem, i, beside(step, 0)))
    n = 2
    for j, (step_y, src) in enumerate(((1, low_out), (-1, top_out))):
        halo.append(remote(src, row_in.at[j], halo_sem, n, beside(0, step_y)))
        for i, step_x in enumerate((1, -1)):
            dest = spot_in.at[j, i, pl.ds(0, 1)]
            halo.append(remote(spot_out.at[j, pl.ds(0, 1)], dest, halo_sem, n + 1 + i, beside(step_x, step_y)))
        n += 3
    loads[6].wait()
    packed = jnp.zeros((rows, LANES), f32)
    for q in range(4 * layers):
        base = field(q // 4, q % 4)
        top_out[q : q + 1, :] = base[0:1]
        low_out[q : q + 1, :] = base[rows - 1 : rows]
        packed = jnp.where(lane == q, base[:, 0:1], packed)
        packed = jnp.where(lane == 4 * layers + q, base[:, LANES - 1 : LANES], packed)
    col_out[...] = packed
    spot_out[0, 0:1] = packed[rows - 1 : rows]
    spot_out[1, 0:1] = packed[0:1]

    pltpu.make_async_copy(kern_all, kern_all, load_sem.at[3]).wait()
    spots = [(c, c, 0) for c in range(3)] + [(c, d, ri) for ri in range(2) for c, d in ((0, 1), (0, 2), (1, 2))]

    def stiff_part(group, m):
        c, d, ri = spots[m]
        return kern_all[group * pw : (group + 1) * pw, c, d, ri, :]

    lane_k = lax.broadcasted_iota(jnp.int32, (pw, LANES), 1)
    for group in range(2 * nx_dev):
        if kyw % LANES == 0:
            for m in range(9):
                kern_out[group, m * pw : (m + 1) * pw] = stiff_part(group, m)
        else:
            for m in range(5):
                high = stiff_part(group, m + 5) if m < 4 else jnp.zeros((pw, kyw), f32)
                tile = jnp.concatenate([stiff_part(group, m), high], axis=1)
                if m == 4 and pw == FOLD:
                    turned = pltpu.roll(pltpu.roll(tile, LANES // 2, 1), FOLD // 2, 0)
                    tile = jnp.where(lane_k < LANES // 2, tile, turned)
                kern_out[group, m * pw : (m + 1) * pw] = tile
    kern_rest[...] = jnp.zeros_like(kern_rest)
    for m in range(9 if kyw % LANES == 0 else 5):
        edge_part = stiff_part(2 * nx_dev, m)
        if kyw % LANES:
            high = stiff_part(2 * nx_dev, m + 5) if m < 4 else jnp.zeros((pw, kyw), f32)
            edge_part = jnp.concatenate([edge_part, high], axis=1)
        kern_rest[m : m + 1] = edge_part[0:1]
    kern_in[kind, b] = kern_out[b]
    used = pl.ds(0, 4 * FOLD + FOLD // 2 if kyw % LANES and pw == FOLD else kern_out.shape[1])
    for k in range(1, nx_dev):
        other = wrap(b + k, nx_dev)
        kc.append(remote(kern_out.at[other, used], kern_in.at[kind, b, used], k_sem, k, {"sx": other, "sy": a}))
    for copy in kc:
        copy.start()
    pl.semaphore_wait(relay_sem, len(cube))
    far = []
    for k in range(nx_dev):
        other = wrap(b + k, nx_dev)
        dev = {"sx": other, "sy": ny_dev - 1 - a}
        far.append(remote(kern_out.at[nx_dev + other, used], kern_in.at[kind, b, used], k_sem, nx_dev + k, dev))
    rest_to = {"sx": jnp.zeros_like(b), "sy": jnp.where(a == half, 0, ny_dev - a)}
    rest = remote(kern_rest, rest_in.at[b], rest_sem, b, rest_to)
    for copy in far:
        copy.start()

    @pl.when(a >= half)
    def _():
        rest.start()

    for copy in p1:
        copy.wait()
    for src in range(nx_dev):
        for comp in range(3):
            buf[comp * rp : (comp + 1) * rp, src * LANES : (src + 1) * LANES] = line_in[src, comp]
    loads[0].wait()
    buf[...] = dot3(buf[:, :total_x], x_tab[0], x_tab[1])
    per = LANES // pw
    lane_p = lax.broadcasted_iota(jnp.int32, (rp, LANES), 1)
    for dest in range(count):
        block, part = dest // per, dest % per
        tile = jnp.zeros((rp, LANES), f32)
        for ri in range(2):
            for comp in range(3):
                at = ri * IM_LANE + comp * pw
                col = ri * (total_x // 2) + block * LANES
                piece = buf[comp * rp : (comp + 1) * rp, col : col + LANES]
                shift = (at - part * pw) % LANES
                if shift:
                    piece = pltpu.roll(piece, shift, 1)
                tile = jnp.where((lane_p >= at) & (lane_p < at + pw), piece, tile)
        if rp == FOLD:
            turned = pltpu.roll(pltpu.roll(tile, LANES // 2, 1), FOLD // 2, 0)
            tile = jnp.where(lane_p < LANES // 2, tile, turned)
        send2[dest] = tile
    recv2[me] = send2[mine]
    some_rows = pl.ds(0, rp // 2 if rp == FOLD else rp)

    def all_start2():
        def send(other_x, other_y):
            src = send2.at[pair_of(other_x, other_y), some_rows]
            remote(src, recv2.at[me, some_rows], p2_sem, 0, {"sx": other_x, "sy": other_y}).start()

        each_other(send)

    lot = pl.ds(0, FOLD + (FOLD // 2 if pw == FOLD else pw))

    def all_start3():
        def send(other_x, other_y):
            src = send3.at[other_y, lot]
            remote(src, recv3.at[mine, lot], p3_sem, 0, {"sx": other_x, "sy": other_y}).start()

        each_other(send)

    def all_wait3():
        for i in range(nx_dev):
            some = send3.at[pl.ds(0, ny_dev - (1 if i == 0 else 0)), lot]
            pltpu.make_async_copy(some, some, p3_sem.at[0, 0]).wait()
        some = recv3.at[pl.ds(0, count - 1), lot]
        pltpu.make_async_copy(some, some, p3_sem.at[1, 0]).wait()

    def all_wait2():
        some = pl.ds(0, count - 1)
        pltpu.make_async_copy(send2.at[some, some_rows], send2.at[some, some_rows], p2_sem.at[0, 0]).wait()
        pltpu.make_async_copy(recv2.at[some, some_rows], recv2.at[some, some_rows], p2_sem.at[1, 0]).wait()

    for copy in halo:
        copy.start()
    all_start2()

    for copy in halo:
        copy.wait()
    first_row, last_row = row == 0, row == rows - 1
    first_lane, last_lane = lane == 0, lane == LANES - 1
    full = (rows, LANES)

    def keep(dx, dy, q, value):
        for chunk in range(chunks):
            shifted[dx + 1, dy + 1, q // 4, q % 4, chunk] = value[chunk * ROWS : (chunk + 1) * ROWS]

    for q in range(4 * layers):
        base = field(q // 4, q % 4)
        left = jnp.broadcast_to(col_in[0][:, 4 * layers + q : 4 * layers + q + 1], full)
        right = jnp.broadcast_to(col_in[1][:, q : q + 1], full)
        for dy in (-1, 0, 1):
            if dy == 0:
                mid, lo, hi = base, left, right
            else:
                edge = first_row if dy == -1 else last_row
                j = 0 if dy == -1 else 1
                turn = 1 if dy == -1 else rows - 1
                mid = jnp.where(edge, row_in[j, q : q + 1, :], pltpu.roll(base, turn, 0))
                at = 4 * layers + q
                lo = jnp.where(edge, spot_in[j, 0, 0:1, at : at + 1], pltpu.roll(left, turn, 0))
                hi = jnp.where(edge, spot_in[j, 1, 0:1, q : q + 1], pltpu.roll(right, turn, 0))
            keep(0, dy, q, mid)
            keep(-1, dy, q, jnp.where(first_lane, lo, pltpu.roll(mid, 1, 1)))
            keep(1, dy, q, jnp.where(last_lane, hi, pltpu.roll(mid, LANES - 1, 1)))

    for copy in kc:
        copy.wait()
    loads[1].wait()
    all_wait2()
    width = 3 * pw

    for src in range(count if rp == FOLD else 0):
        tile = recv2[src]
        turned = pltpu.roll(pltpu.roll(tile, LANES // 2, 1), FOLD // 2, 0)
        recv2[src] = jnp.where(lax.broadcasted_iota(jnp.int32, (rp, LANES), 0) < FOLD // 2, tile, turned)
    table = jnp.transpose(recv2[...].reshape(total_y, LANES))[: 2 * IM_LANE]
    both = dot3(table, y_tab[0], y_tab[1])
    cos_part, sin_part = both[:, :total_y], both[:, total_y:]
    for copy in far:
        copy.wait()

    @pl.when(a >= half)
    def _():
        rest.wait_send()

    @pl.when(early & (b == 0))
    def _():
        for src in range(nx_dev):
            pltpu.make_async_copy(rest_in.at[src], rest_in.at[src], rest_sem.at[1, src]).wait()
            for m in range(9 if kyw % LANES == 0 else 5):
                line = rest_in[src, m : m + 1, :]
                if m == 4 and kyw % LANES:
                    line = jnp.where(lane_k[0:1] < LANES // 2, line, kern_in[1, src, m * pw : m * pw + 1, :])
                kern_in[1, src, m * pw : m * pw + 1, :] = line

    row_k = lax.broadcasted_iota(jnp.int32, (pw, LANES), 0)
    pair_row = lax.broadcasted_iota(jnp.int32, (pw, total_y), 0) + mine * pw

    def stiff(which, m):
        if kyw % LANES == 0:
            return jnp.concatenate([kern_in[which, src, m * pw : (m + 1) * pw] for src in range(nx_dev)], axis=1)

        def tile_of(src):
            tile = kern_in[which, src, m % 5 * pw : (m % 5 + 1) * pw]
            if m == 4 and pw == FOLD:
                turned = pltpu.roll(pltpu.roll(tile, LANES // 2, 1), FOLD // 2, 0)
                tile = jnp.where(row_k < FOLD // 2, tile, turned)
            return tile

        pieces = []
        for pair in range(nx_dev // 2):
            one, two = tile_of(2 * pair), tile_of(2 * pair + 1)
            if m < 5:
                two = pltpu.roll(two, LANES // 2, 1)
            else:
                one = pltpu.roll(one, LANES // 2, 1)
            pieces.append(jnp.where(lane_k < LANES // 2, one, two))
        return jnp.concatenate(pieces, axis=1)

    def push(which, sr, si):
        fr, fi = [], []
        for comp in range(3):
            diag = stiff(which, comp)
            fr.append(diag * sr[comp])
            fi.append(diag * si[comp])
        for m, (c, d) in enumerate(((0, 1), (0, 2), (1, 2))):
            kr, ki = stiff(which, 3 + m), stiff(which, 6 + m)
            fr[c] = fr[c] + kr * sr[d] - ki * si[d]
            fi[c] = fi[c] + kr * si[d] + ki * sr[d]
            fr[d] = fr[d] + kr * sr[c] + ki * si[c]
            fi[d] = fi[d] + kr * si[c] - ki * sr[c]
        return fr, fi

    ends = pair_row == 0
    ar, ai, br, bi = [], [], [], []
    for comp in range(3):
        re_at = slice(comp * pw, (comp + 1) * pw)
        im_at = slice(IM_LANE + comp * pw, IM_LANE + (comp + 1) * pw)
        re_c, re_s, im_c, im_s = cos_part[re_at], sin_part[re_at], cos_part[im_at], sin_part[im_at]
        ar.append(re_c + jnp.where(ends, 0.0, im_s))
        ai.append(jnp.where(ends, 0.0, im_c) - re_s)
        br.append(jnp.where(ends, im_c, re_c - im_s))
        bi.append(jnp.where(ends, -im_s, -im_c - re_s))
    ar, ai = push(0, ar, ai)
    br, bi = push(1, br, bi)
    up, down = [], []
    for comp in range(3):
        up.append(jnp.where(ends, ar[comp], ar[comp] + br[comp]))
        down.append(jnp.where(ends, ai[comp], ai[comp] + bi[comp]))
    for comp in range(3):
        up.append(jnp.where(ends, br[comp], ai[comp] - bi[comp]))
        down.append(jnp.where(ends, bi[comp], br[comp] - ar[comp]))
    waves[: 2 * width] = dot3(jnp.concatenate(up, axis=0), y_tab[0, :, :total_y], y_tab[1, :, :total_y]) - dot3(
        jnp.concatenate(down, axis=0), y_tab[0, :, total_y:], y_tab[1, :, total_y:]
    )
    lane_w = lax.broadcasted_iota(jnp.int32, (pw, LANES), 1)
    quarter = LANES // 4
    for dest in range(ny_dev):
        col, part = dest * rows // LANES * LANES, dest * rows % LANES

        def block_of(index, at):
            piece = waves[index * pw : (index + 1) * pw, col : col + LANES]
            shift = (at - part) % LANES
            return pltpu.roll(piece, shift, 1) if shift else piece

        tile = block_of(3, 3 * quarter)
        for comp in (2, 1, 0):
            tile = jnp.where(lane_w < (comp + 1) * quarter, block_of(comp, comp * quarter), tile)
        send3[dest, :pw] = tile
        tile = jnp.where(lane_w < 2 * quarter, block_of(4, quarter), block_of(5, 2 * quarter))
        if pw == FOLD:
            turned = pltpu.roll(pltpu.roll(tile, LANES // 2, 1), FOLD // 2, 0)
            tile = jnp.where((lane_w >= quarter) & (lane_w < 3 * quarter), tile, turned)
        send3[dest, FOLD : FOLD + pw] = tile
    recv3[mine] = send3[a]
    all_start3()

    loads[4].wait()
    loads[5].wait()

    @pl.loop(0, chunks)
    def _(chunk):
        own_sum = []
        parts = {}
        at = pl.ds(pl.multiple_of(chunk * ROWS, ROWS), ROWS)
        for layer in range(layers):
            codes = [codes_ref[layer, slot, at, :] for slot in range(slots)]
            masks = [masks_ref[layer, slot, at, :] for slot in range(slots)]
            grads = tersoff_rows(layer, layers, slots, shifted, chunk, codes, masks)
            total = [sum(grads[s][comp] for s in range(slots)) for comp in range(3)]
            own_sum.append(total)
            for slot in range(slots):
                for entry, dx, dy, dz in bonds_of(layer, layers, slot):
                    hit = codes[slot] == entry
                    for comp in range(3):
                        key = (dx, dy, layer + dz, comp)
                        term = jnp.where(hit, grads[slot][comp], 0.0)
                        parts[key] = parts[key] + term if key in parts else term
        for level in range(layers):
            for comp in range(3):
                key = (0, 0, level, comp)
                here = own_sum[level][comp]
                parts[key] = here - parts[key] if key in parts else here
        for (dx, dy, level, comp), value in parts.items():
            signed = value if (dx, dy) == (0, 0) else -value
            spill[dx + 1, dy + 1, level, comp, at, :] = signed

    left_pack = jnp.zeros(full, f32)
    right_pack = jnp.zeros(full, f32)
    edge_out[...] = jnp.zeros_like(edge_out)
    spots_out = [jnp.zeros((1, LANES), f32) for _ in range(2)]
    lane0 = lane1[0:1]
    for q in range(3 * layers):
        level, comp = q // 3, q % 3
        lines = []
        for dx in (-1, 0, 1):
            part = spill[dx + 1, 1, level, comp]
            down = spill[dx + 1, 2, level, comp]
            up = spill[dx + 1, 0, level, comp]
            part = part + jnp.where(first_row, 0.0, pltpu.roll(down, 1, 0))
            part = part + jnp.where(last_row, 0.0, pltpu.roll(up, rows - 1, 0))
            edge_out[0, dx + 1, q : q + 1, :] = down[rows - 1 : rows]
            edge_out[1, dx + 1, q : q + 1, :] = up[0:1]
            if dx:
                end = LANES - 1 if dx > 0 else 0
                for j, line in enumerate((down[rows - 1 : rows], up[0:1])):
                    hit = lane0 == (ROWS if dx > 0 else 0) + q
                    spots_out[j] = jnp.where(hit, line[:, end : end + 1], spots_out[j])
            lines.append(part)
        left_pack = jnp.where(lane == q, lines[0][:, 0:1], left_pack)
        right_pack = jnp.where(lane == q, lines[2][:, LANES - 1 : LANES], right_pack)
        out_ref[level, comp] = (
            lines[1]
            + jnp.where(first_lane, 0.0, pltpu.roll(lines[2], 1, 1))
            + jnp.where(last_lane, 0.0, pltpu.roll(lines[0], LANES - 1, 1))
        )
    side_out[0] = right_pack
    side_out[1] = left_pack
    for j in range(2):
        edge_out[j, 1] = (
            edge_out[j, 1]
            + jnp.where(lane1 == 0, 0.0, pltpu.roll(edge_out[j, 2], 1, 1))
            + jnp.where(lane1 == LANES - 1, 0.0, pltpu.roll(edge_out[j, 0], LANES - 1, 1))
        )
    for j in range(2):
        tip_out[j, 0:1] = spots_out[j]
    rim = []
    for i, step in enumerate((1, -1)):
        rim.append(remote(side_out.at[i], side_in.at[i], rim_sem, i, beside(step, 0)))
    n = 2
    for j, step_y in enumerate((1, -1)):
        rim.append(remote(edge_out.at[j, 1], edge_in.at[j], rim_sem, n, beside(0, step_y)))
        for i, dx in enumerate((-1, 1)):
            dest = tip_in.at[j, i, pl.ds(0, 1)]
            rim.append(remote(tip_out.at[j, pl.ds(0, 1)], dest, rim_sem, n + 1 + i, beside(dx, step_y)))
        n += 3
    for copy in rim:
        copy.start()

    all_wait3()
    row_w = lax.broadcasted_iota(jnp.int32, (pw, LANES), 0)
    for src in range(count):
        first, second = recv3[src, :pw], recv3[src, FOLD : FOLD + pw]
        if pw == FOLD:
            turned = pltpu.roll(pltpu.roll(second, LANES // 2, 1), FOLD // 2, 0)
            second = jnp.where(row_w < FOLD // 2, second, turned)
        fields[src * pw : (src + 1) * pw] = first
        fields[total_x // 2 + src * pw : total_x // 2 + (src + 1) * pw] = jnp.where(
            lane_w < quarter, pltpu.roll(first, quarter, 1), second
        )
    own_x = pl.ds(pl.multiple_of(b * LANES, LANES), LANES)
    top = fields[...].astype(jnp.bfloat16)
    low_part = (fields[...] - top.astype(f32)).astype(jnp.bfloat16)
    dot = functools.partial(jnp.dot, preferred_element_type=f32)
    lines_x = x_tab[0, own_x, :]
    real = dot(lines_x, top) + (dot(lines_x, low_part) + dot(x_tab[1, own_x, :], top))
    real = jnp.transpose(real) * f32(-1.0 / (total_x * total_y))
    for copy in rim:
        copy.wait()
    for q in range(3 * layers):
        level, comp = q // 3, q % 3
        value = out_ref[level, comp]
        value = value + jnp.where(first_lane, side_in[0][:, q : q + 1], 0.0)
        value = value + jnp.where(last_lane, side_in[1][:, q : q + 1], 0.0)
        for j, edge in enumerate((first_row, last_row)):
            line = edge_in[j, q : q + 1, :]
            value = value + jnp.where(edge, line, 0.0)
            value = value + jnp.where(edge & first_lane, tip_in[j, 1, 0:1, ROWS + q : ROWS + q + 1], 0.0)
            value = value + jnp.where(edge & last_lane, tip_in[j, 0, 0:1, q : q + 1], 0.0)
        out_ref[level, comp] = value
    for comp in range(3):
        out_ref[0, comp] = out_ref[0, comp] + real[comp * rows : (comp + 1) * rows]


def shards(nx_dev, ny_dev, disp, velocity, kinds, neighbours, pad_mask, kernel):
    layers, comps, rows, cols = disp.shape
    slots = neighbours.shape[1]
    total_x, total_y = cols * nx_dev, rows * ny_dev
    count = nx_dev * ny_dev
    kx_block, kyw = kernel.shape[0], kernel.shape[4]
    pw = kx_block // (2 * nx_dev)
    rp = rows // nx_dev
    kern_parts = 9 if kyw % LANES == 0 else 5
    lanes = kyw if kern_parts == 9 else LANES
    x_table = jnp.asarray(line_table(total_x))
    y_table = jnp.asarray(wave_table(total_y))
    chunks = rows // ROWS
    vmem = pl.BlockSpec(memory_space=pltpu.VMEM)
    hbm = pl.BlockSpec(memory_space=pl.ANY)
    tiles = pltpu.VMEM((count, rp, LANES), f32)
    quarter = pltpu.VMEM((nx_dev, 3, rp, LANES), f32)
    sems = lambda n: pltpu.SemaphoreType.DMA((2, n))
    inputs = (disp.reshape(layers, comps, nx_dev, rp, cols), kinds, neighbours, pad_mask, kernel, x_table, y_table)
    force = pl.pallas_call(
        functools.partial(step_kernel, (nx_dev, ny_dev, layers, slots, rows, total_x, total_y, pw, kyw)),
        out_shape=jax.ShapeDtypeStruct(disp.shape, f32),
        in_specs=[hbm] * 7,
        out_specs=vmem,
        scratch_shapes=[
            pltpu.VMEM((layers, comps, nx_dev, rp, cols), f32),
            pltpu.VMEM(kinds.shape, jnp.int32),
            pltpu.VMEM(neighbours.shape, jnp.int32),
            pltpu.VMEM(pad_mask.shape, jnp.int32),
            pltpu.VMEM(((2 * nx_dev + 1) * pw, *kernel.shape[1:]), f32),
            pltpu.VMEM((2 * nx_dev, kern_parts * pw, lanes), f32),
            pltpu.VMEM((2 * ROWS, lanes), f32),
            pltpu.VMEM(x_table.shape, jnp.bfloat16),
            pltpu.VMEM(y_table.shape, jnp.bfloat16),
            quarter,
            pltpu.VMEM((3 * rp, total_x), f32),
            tiles, tiles,
            pltpu.VMEM((ny_dev, 2 * FOLD, LANES), f32),
            pltpu.VMEM((count, 2 * FOLD, LANES), f32),
            pltpu.VMEM((6 * pw, total_y), f32),
            pltpu.VMEM((2, nx_dev, kern_parts * pw, lanes), f32),
            pltpu.VMEM((nx_dev, 2 * ROWS, lanes), f32),
            pltpu.VMEM((total_x, LANES), f32),
            pltpu.VMEM((rows, LANES), f32),
            pltpu.VMEM((4 * layers, LANES), f32),
            pltpu.VMEM((4 * layers, LANES), f32),
            pltpu.VMEM((2, rows, LANES), f32),
            pltpu.VMEM((2, 4 * layers, LANES), f32),
            pltpu.VMEM((2, ROWS, LANES), f32),
            pltpu.VMEM((2, 2, ROWS, LANES), f32),
            pltpu.VMEM((3, 3, layers, 4, chunks, ROWS, LANES), f32),
            pltpu.VMEM((3, 3, layers, 3, rows, LANES), f32),
            pltpu.VMEM((2, rows, LANES), f32),
            pltpu.VMEM((2, 3, ROWS, LANES), f32),
            pltpu.VMEM((2, rows, LANES), f32),
            pltpu.VMEM((2, ROWS, LANES), f32),
            pltpu.VMEM((2, ROWS, LANES), f32),
            pltpu.VMEM((2, 2, ROWS, LANES), f32),
            pltpu.SemaphoreType.DMA((7,)),
            sems(nx_dev), sems(2 * nx_dev), sems(nx_dev), sems(8), sems(1), sems(1), sems(8),
            pltpu.SemaphoreType.REGULAR,
        ],
        compiler_params=pltpu.CompilerParams(
            collective_id=0, has_side_effects=True, vmem_limit_bytes=44 * 1024 * 1024
        ),
    )(*(pltpu.with_memory_space_constraint(value, pltpu.HBM) for value in inputs))
    new_velocity = velocity + impulse_scale * force
    new_disp = disp + drift_scale * new_velocity
    return (new_disp, new_velocity)


def solution(mesh):
    in_specs = (
        P(None, None, "sy", "sx"),
        P(None, None, "sy", "sx"),
        P(None, "sy", "sx"),
        P(None, None, "sy", "sx"),
        P(None, None, "sy", "sx"),
        P("sy", None, None, None, "sx"),
    )
    out_specs = (P(None, None, "sy", "sx"), P(None, None, "sy", "sx"))
    body = functools.partial(shards, mesh.shape["sx"], mesh.shape["sy"])
    return jax.shard_map(body, mesh=mesh, in_specs=in_specs, out_specs=out_specs, check_vma=False)
```

```python
import functools
import math

import jax
import jax.numpy as jnp
import numpy as np
from jax import lax
from jax.experimental import pallas as pl
from jax.experimental.pallas import tpu as pltpu
from jax.sharding import PartitionSpec as P

silicon = (1830.8, 471.18, 2.4799, 1.7322, 1.1e-06, 0.78734, 100390.0, 16.217, -0.59825, 2.7, 3.0)
germanium = (1769.0, 419.23, 2.4451, 1.7047, 9.0166e-07, 0.75627, 106430.0, 15.652, -0.43884, 2.8, 3.1)
faces = ((1, 0, 0), (0, 1, 0), (0, 0, 1), (-1, 0, 0), (0, -1, 0), (0, 0, -1))
edges = (
    (1, 1, 0), (1, -1, 0), (-1, 1, 0), (-1, -1, 0),
    (1, 0, 1), (1, 0, -1), (-1, 0, 1), (-1, 0, -1),
    (0, 1, 1), (0, 1, -1), (0, -1, 1), (0, -1, -1),
)
FACE_SLOTS = 4
lattice_step = 2.0
impulse_scale = 0.1
drift_scale = 0.05
LANES = 128
ROWS = 8
IM_LANE = 32
FOLD = 8
f32 = jnp.float32
MESH = pl.DeviceIdType.MESH


def split_table(table):
    table = table.astype(np.float32)
    high = table.astype(jnp.bfloat16)
    low = (table - high.astype(np.float32)).astype(jnp.bfloat16)
    return np.stack([high, low])


def angles(length, columns):
    ids = np.arange(length, dtype=np.int64)
    return (ids[:, None] * np.arange(columns, dtype=np.int64)[None, :] % length) * (2.0 * math.pi / length)


def line_table(length):
    half = length // 2
    angle = angles(length, half)
    sines = -np.sin(angle)
    sines[:, 0] = 1.0 - 2.0 * (np.arange(length) % 2)
    return split_table(np.concatenate([np.cos(angle), sines], axis=1))


def wave_table(length):
    angle = angles(length, length)
    return split_table(np.concatenate([np.cos(angle), np.sin(angle)], axis=1))


def dot3(values, high, low):
    count = values.shape[0]
    top = values.astype(jnp.bfloat16)
    coarse = top.astype(f32)
    both = jnp.concatenate([coarse, values - coarse], axis=0).astype(jnp.bfloat16)
    dot = functools.partial(jnp.dot, preferred_element_type=f32)
    twice = dot(both, high)
    return twice[:count] + (twice[count:] + dot(top, low))


def pick(is_ge, same, position, mean):
    si, ge = silicon[position], germanium[position]
    both = math.sqrt(si * ge) if mean == "geo" else 0.5 * (si + ge)
    return jnp.where(same, jnp.where(is_ge, f32(ge), f32(si)), f32(both))


def own_pick(is_ge, si, ge):
    return jnp.where(is_ge, f32(ge), f32(si))


def poly(v2, coefs):
    out = f32(coefs[-1])
    for coef in coefs[-2::-1]:
        out = out * v2 + f32(coef)
    return out


sin_coefs = [(-1) ** k * math.pi ** (2 * k + 1) / math.factorial(2 * k + 1) for k in range(6)]
cos_coefs = [(-1) ** k * math.pi ** (2 * k) / math.factorial(2 * k) for k in range(7)]


def bonds_of(layer, layers, slot):
    table = faces if slot < FACE_SLOTS else edges
    base = 0 if slot < FACE_SLOTS else len(faces)
    for entry, (dx, dy, dz) in enumerate(table):
        if 0 <= layer + dz < layers:
            yield base + entry, dx, dy, dz


def tersoff_rows(layer, layers, slots, shifted, chunk, codes, masks):
    def near(dx, dy, level, comp):
        return shifted[dx + 1, dy + 1, level, comp, chunk]

    own = [near(0, 0, layer, comp) for comp in range(3)]
    own_ge = near(0, 0, layer, 3) > 0.5
    h = own_pick(own_ge, silicon[8], germanium[8])
    d2 = own_pick(own_ge, silicon[7] ** 2, germanium[7] ** 2)
    c2 = own_pick(own_ge, silicon[6] ** 2, germanium[6] ** 2)
    ratio = own_pick(own_ge, silicon[6] ** 2 / silicon[7] ** 2, germanium[6] ** 2 / germanium[7] ** 2)
    beta = own_pick(own_ge, silicon[4], germanium[4])
    power = own_pick(own_ge, silicon[5], germanium[5])
    half_inv = own_pick(own_ge, 0.5 / silicon[5], 0.5 / germanium[5])
    data = []
    for slot in range(slots):
        code = codes[slot]
        bond = [jnp.full(code.shape, lattice_step, f32)] + [jnp.zeros(code.shape, f32) for _ in range(2)]
        kind = jnp.zeros(code.shape, f32)
        valid = jnp.zeros(code.shape, f32)
        for entry, dx, dy, dz in bonds_of(layer, layers, slot):
            hit = code == entry
            for comp, step in enumerate((dx, dy, dz)):
                place = near(dx, dy, layer + dz, comp)
                if step:
                    place = place + f32(lattice_step * step)
                bond[comp] = jnp.where(hit, place - own[comp], bond[comp])
            kind = jnp.where(hit, near(dx, dy, layer + dz, 3), kind)
            valid = jnp.where(hit, f32(1.0), valid)
        live = masks[slot].astype(f32) * valid
        dist2 = bond[0] * bond[0] + bond[1] * bond[1] + bond[2] * bond[2]
        inv = lax.rsqrt(dist2)
        dist = dist2 * inv
        unit = [b * inv for b in bond]
        same = (kind > 0.5) == own_ge
        inner = pick(own_ge, same, 9, "geo")
        span_si = 1.0 / (silicon[10] - silicon[9])
        span_ge = 1.0 / (germanium[10] - germanium[9])
        span_mix = 1.0 / (math.sqrt(silicon[10] * germanium[10]) - math.sqrt(silicon[9] * germanium[9]))
        span = jnp.where(same, jnp.where(own_ge, f32(span_ge), f32(span_si)), f32(span_mix))
        phase = (dist - inner) * span
        v = jnp.clip(phase, 0.0, 1.0) - 0.5
        v2 = v * v
        fade = 0.5 - 0.5 * v * poly(v2, sin_coefs)
        fade_slope = f32(-0.5 * math.pi) * span * poly(v2, cos_coefs)
        below, above = phase < 0.0, phase > 1.0
        cutoff = jnp.where(below, 1.0, jnp.where(above, 0.0, fade))
        slope = jnp.where(below | above, 0.0, fade_slope) * live
        mu = pick(own_ge, same, 3, "mean")
        lam = pick(own_ge, same, 2, "mean")
        attract = pick(own_ge, same, 1, "geo") * jnp.exp(-mu * dist)
        repulse = pick(own_ge, same, 0, "geo") * jnp.exp(-lam * dist)
        data.append(dict(unit=unit, inv=inv, weight=live * cutoff, slope=slope, mu=mu, lam=lam, att=attract, rep=repulse))
    zeta = [jnp.zeros_like(h) for _ in range(slots)]
    for s in range(slots):
        for t in range(s):
            us, ut = data[s]["unit"], data[t]["unit"]
            q = us[0] * ut[0] + us[1] * ut[1] + us[2] * ut[2]
            away = h - q
            gap = away * away
            g = 1.0 + ratio * gap / (d2 + gap)
            zeta[s] = zeta[s] + data[t]["weight"] * g
            zeta[t] = zeta[t] + data[s]["weight"] * g
    pull, radial = [], []
    for s in range(slots):
        item = data[s]
        z = jnp.exp(power * jnp.log(beta * zeta[s]))
        order = jnp.exp(-jnp.log(1.0 + z) * half_inv)
        bound = order * item["att"]
        pull.append(0.25 * item["weight"] * bound * z / (zeta[s] * (1.0 + z)))
        radial.append(
            0.5 * (item["slope"] * (item["rep"] - bound) + item["weight"] * (item["mu"] * bound - item["lam"] * item["rep"]))
        )
    turn = [[jnp.zeros_like(h) for _ in range(3)] for _ in range(slots)]
    spread = [jnp.zeros_like(h) for _ in range(slots)]
    for s in range(slots):
        for t in range(s):
            us, ut = data[s]["unit"], data[t]["unit"]
            q = us[0] * ut[0] + us[1] * ut[1] + us[2] * ut[2]
            away = h - q
            gap = away * away
            inv = 1.0 / (d2 + gap)
            g = 1.0 + ratio * gap * inv
            tilt = -2.0 * c2 * away * inv * inv
            pair = (pull[s] * data[t]["weight"] + pull[t] * data[s]["weight"]) * tilt
            for comp in range(3):
                turn[s][comp] = turn[s][comp] + pair * ut[comp]
                turn[t][comp] = turn[t][comp] + pair * us[comp]
            spread[s] = spread[s] + pull[t] * g
            spread[t] = spread[t] + pull[s] * g
    grads = []
    for s in range(slots):
        item = data[s]
        unit = item["unit"]
        along = turn[s][0] * unit[0] + turn[s][1] * unit[1] + turn[s][2] * unit[2]
        line = radial[s] + item["slope"] * spread[s] - along * item["inv"]
        grads.append([turn[s][comp] * item["inv"] + line * unit[comp] for comp in range(3)])
    return grads


def step_kernel(
    dims,
    disp_hbm, kinds_hbm, codes_hbm, masks_hbm, kern_hbm, x_hbm, y_hbm,
    out_ref,
    disp_ref, kinds_ref, codes_ref, masks_ref, kern_all, kern_out, kern_rest, x_tab, y_tab, line_in, buf, send2, recv2, send3, recv3, waves, kern_in, rest_in, fields,
    col_out, top_out, low_out, col_in, row_in, spot_out, spot_in, shifted, spill,
    side_out, edge_out, side_in, edge_in, tip_out, tip_in,
    load_sem, p1_sem, k_sem, rest_sem, halo_sem, p2_sem, p3_sem, rim_sem, relay_sem,
):
    nx_dev, ny_dev, layers, slots, rows, total_x, total_y, pw, kyw = dims
    count = nx_dev * ny_dev
    rp = rows // nx_dev
    chunks = rows // ROWS
    b = lax.axis_index("sx")
    a = lax.axis_index("sy")
    me = a * nx_dev + b
    half = ny_dev // 2
    early = a < half
    kind = jnp.where(early, 0, 1)

    def pair_of(dev_x, dev_y):
        first = dev_y < half
        return jnp.where(first, dev_y, ny_dev - 1 - dev_y) * (2 * nx_dev) + dev_x + jnp.where(first, 0, nx_dev)

    mine = pair_of(b, a)
    lane = lax.broadcasted_iota(jnp.int32, (rows, LANES), 1)
    row = lax.broadcasted_iota(jnp.int32, (rows, LANES), 0)
    lane1 = lax.broadcasted_iota(jnp.int32, (ROWS, LANES), 1)

    def wrap(value, size):
        return jnp.where(value >= size, value - size, value)

    def each_other(visit):
        for i in reversed(range(nx_dev)):
            other_x = wrap(b + i, nx_dev)

            def body(j, carry, other_x=other_x):
                visit(other_x, wrap(a + j, ny_dev))
                return carry

            lax.fori_loop(0 if i else 1, ny_dev, body, None, unroll=count <= 64)

    def beside(step_x, step_y):
        return {"sx": wrap(b + step_x % nx_dev, nx_dev), "sy": wrap(a + step_y % ny_dev, ny_dev)}

    def remote(src, dst, sems, index, dev):
        return pltpu.make_async_remote_copy(
            src_ref=src, dst_ref=dst, send_sem=sems.at[0, index], recv_sem=sems.at[1, index],
            device_id=dev, device_id_type=MESH,
        )

    barrier = pltpu.get_barrier_semaphore()

    low = 2 ** ((ny_dev.bit_length() - 1) // 2)
    lines = ny_dev // low
    side, line = lax.rem(a, low), a // low
    cube = [
        {"sx": wrap(b + i, nx_dev), "sy": line * low + wrap(side + j, low)}
        for j in range(low) for i in range(nx_dev) if i or j
    ]
    near = cube + [{"sx": b, "sy": wrap(line + k, lines) * low + side} for k in range(1, lines)]
    for dev in near:
        pl.semaphore_signal(barrier, inc=1, device_id=dev, device_id_type=MESH)

    loads = [
        pltpu.make_async_copy(x_hbm, x_tab, load_sem.at[0]),
        pltpu.make_async_copy(y_hbm, y_tab, load_sem.at[1]),
        pltpu.make_async_copy(disp_hbm, disp_ref, load_sem.at[2]),
        None,
        pltpu.make_async_copy(codes_hbm, codes_ref, load_sem.at[4]),
        pltpu.make_async_copy(masks_hbm, masks_ref, load_sem.at[5]),
        pltpu.make_async_copy(kinds_hbm, kinds_ref, load_sem.at[6]),
    ]
    def stiff_row(slot):
        group, r = slot // pw, slot % pw
        if group == 2 * nx_dev:
            return 0
        o, t = group // nx_dev, group % nx_dev
        late = (o + 1) * nx_dev - 1 - t
        if r:
            late_row = late * pw + pw - r
        else:
            late_row = (late + 1) * pw if late + 1 < 2 * nx_dev else 0
        return jnp.where(early, group * pw + r, late_row)

    for i in (2, 6):
        loads[i].start()
    for slot in range((2 * nx_dev + 1) * pw):
        pltpu.make_async_copy(kern_hbm.at[stiff_row(slot)], kern_all.at[slot], load_sem.at[3]).start()
    for i in (0, 1, 4, 5):
        loads[i].start()

    def field(level, comp):
        if comp < 3:
            return disp_ref[level, comp].reshape(rows, LANES)
        return kinds_ref[level].astype(f32)

    pl.semaphore_wait(barrier, len(near))
    for dev in cube:
        pl.semaphore_signal(relay_sem, inc=1, device_id=dev, device_id_type=MESH)
    loads[2].wait()

    p1 = []
    kc = []
    for k in range(1, nx_dev):
        other = wrap(b + k, nx_dev)
        p1.append(remote(disp_ref.at[0, :, other], line_in.at[b], p1_sem, k, {"sx": other, "sy": a}))
    for copy in p1:
        copy.start()
    for comp in range(3):
        line_in[b, comp] = disp_ref[0, comp, b]
    halo = []
    for i, step in enumerate((1, -1)):
        halo.append(remote(col_out, col_in.at[i], halo_sem, i, beside(step, 0)))
    n = 2
    for j, (step_y, src) in enumerate(((1, low_out), (-1, top_out))):
        halo.append(remote(src, row_in.at[j], halo_sem, n, beside(0, step_y)))
        for i, step_x in enumerate((1, -1)):
            dest = spot_in.at[j, i, pl.ds(0, 1)]
            halo.append(remote(spot_out.at[j, pl.ds(0, 1)], dest, halo_sem, n + 1 + i, beside(step_x, step_y)))
        n += 3
    loads[6].wait()
    packed = jnp.zeros((rows, LANES), f32)
    for q in range(4 * layers):
        base = field(q // 4, q % 4)
        top_out[q : q + 1, :] = base[0:1]
        low_out[q : q + 1, :] = base[rows - 1 : rows]
        packed = jnp.where(lane == q, base[:, 0:1], packed)
        packed = jnp.where(lane == 4 * layers + q, base[:, LANES - 1 : LANES], packed)
    col_out[...] = packed
    spot_out[0, 0:1] = packed[rows - 1 : rows]
    spot_out[1, 0:1] = packed[0:1]

    pltpu.make_async_copy(kern_all, kern_all, load_sem.at[3]).wait()
    spots = [(c, c, 0) for c in range(3)] + [(c, d, ri) for ri in range(2) for c, d in ((0, 1), (0, 2), (1, 2))]

    def stiff_part(group, m):
        c, d, ri = spots[m]
        return kern_all[group * pw : (group + 1) * pw, c, d, ri, :]

    lane_k = lax.broadcasted_iota(jnp.int32, (pw, LANES), 1)
    for group in range(2 * nx_dev):
        if kyw % LANES == 0:
            for m in range(9):
                kern_out[group, m * pw : (m + 1) * pw] = stiff_part(group, m)
        else:
            for m in range(5):
                high = stiff_part(group, m + 5) if m < 4 else jnp.zeros((pw, kyw), f32)
                tile = jnp.concatenate([stiff_part(group, m), high], axis=1)
                if m == 4 and pw == FOLD:
                    turned = pltpu.roll(pltpu.roll(tile, LANES // 2, 1), FOLD // 2, 0)
                    tile = jnp.where(lane_k < LANES // 2, tile, turned)
                kern_out[group, m * pw : (m + 1) * pw] = tile
    kern_rest[...] = jnp.zeros_like(kern_rest)
    for m in range(9 if kyw % LANES == 0 else 5):
        edge_part = stiff_part(2 * nx_dev, m)
        if kyw % LANES:
            high = stiff_part(2 * nx_dev, m + 5) if m < 4 else jnp.zeros((pw, kyw), f32)
            edge_part = jnp.concatenate([edge_part, high], axis=1)
        kern_rest[m : m + 1] = edge_part[0:1]
    kern_in[kind, b] = kern_out[b]
    used = pl.ds(0, 4 * FOLD + FOLD // 2 if kyw % LANES and pw == FOLD else kern_out.shape[1])
    for k in range(1, nx_dev):
        other = wrap(b + k, nx_dev)
        kc.append(remote(kern_out.at[other, used], kern_in.at[kind, b, used], k_sem, k, {"sx": other, "sy": a}))
    for copy in kc:
        copy.start()
    pl.semaphore_wait(relay_sem, len(cube))
    far = []
    for k in range(nx_dev):
        other = wrap(b + k, nx_dev)
        dev = {"sx": other, "sy": ny_dev - 1 - a}
        far.append(remote(kern_out.at[nx_dev + other, used], kern_in.at[kind, b, used], k_sem, nx_dev + k, dev))
    rest_to = {"sx": jnp.zeros_like(b), "sy": jnp.where(a == half, 0, ny_dev - a)}
    rest = remote(kern_rest, rest_in.at[b], rest_sem, b, rest_to)
    for copy in far:
        copy.start()

    @pl.when(a >= half)
    def _():
        rest.start()

    for copy in p1:
        copy.wait()
    for src in range(nx_dev):
        for comp in range(3):
            buf[comp * rp : (comp + 1) * rp, src * LANES : (src + 1) * LANES] = line_in[src, comp]
    loads[0].wait()
    buf[...] = dot3(buf[:, :total_x], x_tab[0], x_tab[1])
    per = LANES // pw
    lane_p = lax.broadcasted_iota(jnp.int32, (rp, LANES), 1)
    for dest in range(count):
        block, part = dest // per, dest % per
        tile = jnp.zeros((rp, LANES), f32)
        for ri in range(2):
            for comp in range(3):
                at = ri * IM_LANE + comp * pw
                col = ri * (total_x // 2) + block * LANES
                piece = buf[comp * rp : (comp + 1) * rp, col : col + LANES]
                shift = (at - part * pw) % LANES
                if shift:
                    piece = pltpu.roll(piece, shift, 1)
                tile = jnp.where((lane_p >= at) & (lane_p < at + pw), piece, tile)
        if rp == FOLD:
            turned = pltpu.roll(pltpu.roll(tile, LANES // 2, 1), FOLD // 2, 0)
            tile = jnp.where(lane_p < LANES // 2, tile, turned)
        send2[dest] = tile
    recv2[me] = send2[mine]
    some_rows = pl.ds(0, rp // 2 if rp == FOLD else rp)

    def all_start2():
        def send(other_x, other_y):
            src = send2.at[pair_of(other_x, other_y), some_rows]
            remote(src, recv2.at[me, some_rows], p2_sem, 0, {"sx": other_x, "sy": other_y}).start()

        each_other(send)

    lot = pl.ds(0, FOLD + (FOLD // 2 if pw == FOLD else pw))

    def all_start3():
        def send(other_x, other_y):
            src = send3.at[other_y, lot]
            remote(src, recv3.at[mine, lot], p3_sem, 0, {"sx": other_x, "sy": other_y}).start()

        each_other(send)

    def all_wait3():
        for i in range(nx_dev):
            some = send3.at[pl.ds(0, ny_dev - (1 if i == 0 else 0)), lot]
            pltpu.make_async_copy(some, some, p3_sem.at[0, 0]).wait()
        some = recv3.at[pl.ds(0, count - 1), lot]
        pltpu.make_async_copy(some, some, p3_sem.at[1, 0]).wait()

    def all_wait2():
        some = pl.ds(0, count - 1)
        pltpu.make_async_copy(send2.at[some, some_rows], send2.at[some, some_rows], p2_sem.at[0, 0]).wait()
        pltpu.make_async_copy(recv2.at[some, some_rows], recv2.at[some, some_rows], p2_sem.at[1, 0]).wait()

    for copy in halo:
        copy.start()
    all_start2()

    for copy in halo:
        copy.wait()
    first_row, last_row = row == 0, row == rows - 1
    first_lane, last_lane = lane == 0, lane == LANES - 1
    full = (rows, LANES)

    def keep(dx, dy, q, value):
        for chunk in range(chunks):
            shifted[dx + 1, dy + 1, q // 4, q % 4, chunk] = value[chunk * ROWS : (chunk + 1) * ROWS]

    for q in range(4 * layers):
        base = field(q // 4, q % 4)
        left = jnp.broadcast_to(col_in[0][:, 4 * layers + q : 4 * layers + q + 1], full)
        right = jnp.broadcast_to(col_in[1][:, q : q + 1], full)
        for dy in (-1, 0, 1):
            if dy == 0:
                mid, lo, hi = base, left, right
            else:
                edge = first_row if dy == -1 else last_row
                j = 0 if dy == -1 else 1
                turn = 1 if dy == -1 else rows - 1
                mid = jnp.where(edge, row_in[j, q : q + 1, :], pltpu.roll(base, turn, 0))
                at = 4 * layers + q
                lo = jnp.where(edge, spot_in[j, 0, 0:1, at : at + 1], pltpu.roll(left, turn, 0))
                hi = jnp.where(edge, spot_in[j, 1, 0:1, q : q + 1], pltpu.roll(right, turn, 0))
            keep(0, dy, q, mid)
            keep(-1, dy, q, jnp.where(first_lane, lo, pltpu.roll(mid, 1, 1)))
            keep(1, dy, q, jnp.where(last_lane, hi, pltpu.roll(mid, LANES - 1, 1)))

    for copy in kc:
        copy.wait()
    loads[1].wait()
    all_wait2()
    width = 3 * pw

    arrived = recv2[...].reshape(total_y, LANES)
    if rp == FOLD:
        turned = pltpu.roll(arrived, LANES // 2, 1)
        turned = pltpu.roll(turned, FOLD // 2, 0)
        spread_row = lax.broadcasted_iota(jnp.int32, (total_y, LANES), 0) % FOLD
        arrived = jnp.where(spread_row < FOLD // 2, arrived, turned)
    table = jnp.transpose(arrived)[: 2 * IM_LANE]
    both = dot3(table, y_tab[0], y_tab[1])
    cos_part, sin_part = both[:, :total_y], both[:, total_y:]
    for copy in far:
        copy.wait()

    @pl.when(a >= half)
    def _():
        rest.wait_send()

    @pl.when(early & (b == 0))
    def _():
        for src in range(nx_dev):
            pltpu.make_async_copy(rest_in.at[src], rest_in.at[src], rest_sem.at[1, src]).wait()
            for m in range(9 if kyw % LANES == 0 else 5):
                line = rest_in[src, m : m + 1, :]
                if m == 4 and kyw % LANES:
                    line = jnp.where(lane_k[0:1] < LANES // 2, line, kern_in[1, src, m * pw : m * pw + 1, :])
                kern_in[1, src, m * pw : m * pw + 1, :] = line

    row_k = lax.broadcasted_iota(jnp.int32, (pw, LANES), 0)
    pair_row = lax.broadcasted_iota(jnp.int32, (pw, total_y), 0) + mine * pw

    def stiff(which, m):
        if kyw % LANES == 0:
            return jnp.concatenate([kern_in[which, src, m * pw : (m + 1) * pw] for src in range(nx_dev)], axis=1)

        def tile_of(src):
            tile = kern_in[which, src, m % 5 * pw : (m % 5 + 1) * pw]
            if m == 4 and pw == FOLD:
                turned = pltpu.roll(pltpu.roll(tile, LANES // 2, 1), FOLD // 2, 0)
                tile = jnp.where(row_k < FOLD // 2, tile, turned)
            return tile

        pieces = []
        for pair in range(nx_dev // 2):
            one, two = tile_of(2 * pair), tile_of(2 * pair + 1)
            if m < 5:
                two = pltpu.roll(two, LANES // 2, 1)
            else:
                one = pltpu.roll(one, LANES // 2, 1)
            pieces.append(jnp.where(lane_k < LANES // 2, one, two))
        return jnp.concatenate(pieces, axis=1)

    def push(which, sr, si):
        fr, fi = [], []
        for comp in range(3):
            diag = stiff(which, comp)
            fr.append(diag * sr[comp])
            fi.append(diag * si[comp])
        for m, (c, d) in enumerate(((0, 1), (0, 2), (1, 2))):
            kr, ki = stiff(which, 3 + m), stiff(which, 6 + m)
            fr[c] = fr[c] + kr * sr[d] - ki * si[d]
            fi[c] = fi[c] + kr * si[d] + ki * sr[d]
            fr[d] = fr[d] + kr * sr[c] + ki * si[c]
            fi[d] = fi[d] + kr * si[c] - ki * sr[c]
        return fr, fi

    ends = pair_row == 0
    ar, ai, br, bi = [], [], [], []
    for comp in range(3):
        re_at = slice(comp * pw, (comp + 1) * pw)
        im_at = slice(IM_LANE + comp * pw, IM_LANE + (comp + 1) * pw)
        re_c, re_s, im_c, im_s = cos_part[re_at], sin_part[re_at], cos_part[im_at], sin_part[im_at]
        ar.append(re_c + jnp.where(ends, 0.0, im_s))
        ai.append(jnp.where(ends, 0.0, im_c) - re_s)
        br.append(jnp.where(ends, im_c, re_c - im_s))
        bi.append(jnp.where(ends, -im_s, -im_c - re_s))
    ar, ai = push(0, ar, ai)
    br, bi = push(1, br, bi)
    up, down = [], []
    for comp in range(3):
        up.append(jnp.where(ends, ar[comp], ar[comp] + br[comp]))
        down.append(jnp.where(ends, ai[comp], ai[comp] + bi[comp]))
    for comp in range(3):
        up.append(jnp.where(ends, br[comp], ai[comp] - bi[comp]))
        down.append(jnp.where(ends, bi[comp], br[comp] - ar[comp]))
    waves[: 2 * width] = dot3(jnp.concatenate(up, axis=0), y_tab[0, :, :total_y], y_tab[1, :, :total_y]) - dot3(
        jnp.concatenate(down, axis=0), y_tab[0, :, total_y:], y_tab[1, :, total_y:]
    )
    lane_w = lax.broadcasted_iota(jnp.int32, (pw, LANES), 1)
    quarter = LANES // 4
    for dest in range(ny_dev):
        col, part = dest * rows // LANES * LANES, dest * rows % LANES

        def block_of(index, at):
            piece = waves[index * pw : (index + 1) * pw, col : col + LANES]
            shift = (at - part) % LANES
            return pltpu.roll(piece, shift, 1) if shift else piece

        tile = block_of(3, 3 * quarter)
        for comp in (2, 1, 0):
            tile = jnp.where(lane_w < (comp + 1) * quarter, block_of(comp, comp * quarter), tile)
        send3[dest, :pw] = tile
        tile = jnp.where(lane_w < 2 * quarter, block_of(4, quarter), block_of(5, 2 * quarter))
        if pw == FOLD:
            turned = pltpu.roll(pltpu.roll(tile, LANES // 2, 1), FOLD // 2, 0)
            tile = jnp.where((lane_w >= quarter) & (lane_w < 3 * quarter), tile, turned)
        send3[dest, FOLD : FOLD + pw] = tile
    recv3[mine] = send3[a]
    all_start3()

    loads[4].wait()
    loads[5].wait()

    @pl.loop(0, chunks)
    def _(chunk):
        own_sum = []
        parts = {}
        at = pl.ds(pl.multiple_of(chunk * ROWS, ROWS), ROWS)
        for layer in range(layers):
            codes = [codes_ref[layer, slot, at, :] for slot in range(slots)]
            masks = [masks_ref[layer, slot, at, :] for slot in range(slots)]
            grads = tersoff_rows(layer, layers, slots, shifted, chunk, codes, masks)
            total = [sum(grads[s][comp] for s in range(slots)) for comp in range(3)]
            own_sum.append(total)
            for slot in range(slots):
                for entry, dx, dy, dz in bonds_of(layer, layers, slot):
                    hit = codes[slot] == entry
                    for comp in range(3):
                        key = (dx, dy, layer + dz, comp)
                        term = jnp.where(hit, grads[slot][comp], 0.0)
                        parts[key] = parts[key] + term if key in parts else term
        for level in range(layers):
            for comp in range(3):
                key = (0, 0, level, comp)
                here = own_sum[level][comp]
                parts[key] = here - parts[key] if key in parts else here
        for (dx, dy, level, comp), value in parts.items():
            signed = value if (dx, dy) == (0, 0) else -value
            spill[dx + 1, dy + 1, level, comp, at, :] = signed

    left_pack = jnp.zeros(full, f32)
    right_pack = jnp.zeros(full, f32)
    edge_out[...] = jnp.zeros_like(edge_out)
    spots_out = [jnp.zeros((1, LANES), f32) for _ in range(2)]
    lane0 = lane1[0:1]
    for q in range(3 * layers):
        level, comp = q // 3, q % 3
        lines = []
        for dx in (-1, 0, 1):
            part = spill[dx + 1, 1, level, comp]
            down = spill[dx + 1, 2, level, comp]
            up = spill[dx + 1, 0, level, comp]
            part = part + jnp.where(first_row, 0.0, pltpu.roll(down, 1, 0))
            part = part + jnp.where(last_row, 0.0, pltpu.roll(up, rows - 1, 0))
            edge_out[0, dx + 1, q : q + 1, :] = down[rows - 1 : rows]
            edge_out[1, dx + 1, q : q + 1, :] = up[0:1]
            if dx:
                end = LANES - 1 if dx > 0 else 0
                for j, line in enumerate((down[rows - 1 : rows], up[0:1])):
                    hit = lane0 == (ROWS if dx > 0 else 0) + q
                    spots_out[j] = jnp.where(hit, line[:, end : end + 1], spots_out[j])
            lines.append(part)
        left_pack = jnp.where(lane == q, lines[0][:, 0:1], left_pack)
        right_pack = jnp.where(lane == q, lines[2][:, LANES - 1 : LANES], right_pack)
        out_ref[level, comp] = (
            lines[1]
            + jnp.where(first_lane, 0.0, pltpu.roll(lines[2], 1, 1))
            + jnp.where(last_lane, 0.0, pltpu.roll(lines[0], LANES - 1, 1))
        )
    side_out[0] = right_pack
    side_out[1] = left_pack
    for j in range(2):
        edge_out[j, 1] = (
            edge_out[j, 1]
            + jnp.where(lane1 == 0, 0.0, pltpu.roll(edge_out[j, 2], 1, 1))
            + jnp.where(lane1 == LANES - 1, 0.0, pltpu.roll(edge_out[j, 0], LANES - 1, 1))
        )
    for j in range(2):
        tip_out[j, 0:1] = spots_out[j]
    rim = []
    for i, step in enumerate((1, -1)):
        rim.append(remote(side_out.at[i], side_in.at[i], rim_sem, i, beside(step, 0)))
    n = 2
    for j, step_y in enumerate((1, -1)):
        rim.append(remote(edge_out.at[j, 1], edge_in.at[j], rim_sem, n, beside(0, step_y)))
        for i, dx in enumerate((-1, 1)):
            dest = tip_in.at[j, i, pl.ds(0, 1)]
            rim.append(remote(tip_out.at[j, pl.ds(0, 1)], dest, rim_sem, n + 1 + i, beside(dx, step_y)))
        n += 3
    for copy in rim:
        copy.start()

    all_wait3()
    row_w = lax.broadcasted_iota(jnp.int32, (pw, LANES), 0)
    for src in range(count):
        first, second = recv3[src, :pw], recv3[src, FOLD : FOLD + pw]
        if pw == FOLD:
            turned = pltpu.roll(pltpu.roll(second, LANES // 2, 1), FOLD // 2, 0)
            second = jnp.where(row_w < FOLD // 2, second, turned)
        fields[src * pw : (src + 1) * pw] = first
        fields[total_x // 2 + src * pw : total_x // 2 + (src + 1) * pw] = jnp.where(
            lane_w < quarter, pltpu.roll(first, quarter, 1), second
        )
    own_x = pl.ds(pl.multiple_of(b * LANES, LANES), LANES)
    top = fields[...].astype(jnp.bfloat16)
    low_part = (fields[...] - top.astype(f32)).astype(jnp.bfloat16)
    dot = functools.partial(jnp.dot, preferred_element_type=f32)
    lines_x = x_tab[0, own_x, :]
    real = dot(lines_x, top) + (dot(lines_x, low_part) + dot(x_tab[1, own_x, :], top))
    real = jnp.transpose(real) * f32(-1.0 / (total_x * total_y))
    for copy in rim:
        copy.wait()
    for q in range(3 * layers):
        level, comp = q // 3, q % 3
        value = out_ref[level, comp]
        value = value + jnp.where(first_lane, side_in[0][:, q : q + 1], 0.0)
        value = value + jnp.where(last_lane, side_in[1][:, q : q + 1], 0.0)
        for j, edge in enumerate((first_row, last_row)):
            line = edge_in[j, q : q + 1, :]
            value = value + jnp.where(edge, line, 0.0)
            value = value + jnp.where(edge & first_lane, tip_in[j, 1, 0:1, ROWS + q : ROWS + q + 1], 0.0)
            value = value + jnp.where(edge & last_lane, tip_in[j, 0, 0:1, q : q + 1], 0.0)
        out_ref[level, comp] = value
    for comp in range(3):
        out_ref[0, comp] = out_ref[0, comp] + real[comp * rows : (comp + 1) * rows]


def shards(nx_dev, ny_dev, disp, velocity, kinds, neighbours, pad_mask, kernel):
    layers, comps, rows, cols = disp.shape
    slots = neighbours.shape[1]
    total_x, total_y = cols * nx_dev, rows * ny_dev
    count = nx_dev * ny_dev
    kx_block, kyw = kernel.shape[0], kernel.shape[4]
    pw = kx_block // (2 * nx_dev)
    rp = rows // nx_dev
    kern_parts = 9 if kyw % LANES == 0 else 5
    lanes = kyw if kern_parts == 9 else LANES
    x_table = jnp.asarray(line_table(total_x))
    y_table = jnp.asarray(wave_table(total_y))
    chunks = rows // ROWS
    vmem = pl.BlockSpec(memory_space=pltpu.VMEM)
    hbm = pl.BlockSpec(memory_space=pl.ANY)
    tiles = pltpu.VMEM((count, rp, LANES), f32)
    quarter = pltpu.VMEM((nx_dev, 3, rp, LANES), f32)
    sems = lambda n: pltpu.SemaphoreType.DMA((2, n))
    inputs = (disp.reshape(layers, comps, nx_dev, rp, cols), kinds, neighbours, pad_mask, kernel, x_table, y_table)
    force = pl.pallas_call(
        functools.partial(step_kernel, (nx_dev, ny_dev, layers, slots, rows, total_x, total_y, pw, kyw)),
        out_shape=jax.ShapeDtypeStruct(disp.shape, f32),
        in_specs=[hbm] * 7,
        out_specs=vmem,
        scratch_shapes=[
            pltpu.VMEM((layers, comps, nx_dev, rp, cols), f32),
            pltpu.VMEM(kinds.shape, jnp.int32),
            pltpu.VMEM(neighbours.shape, jnp.int32),
            pltpu.VMEM(pad_mask.shape, jnp.int32),
            pltpu.VMEM(((2 * nx_dev + 1) * pw, *kernel.shape[1:]), f32),
            pltpu.VMEM((2 * nx_dev, kern_parts * pw, lanes), f32),
            pltpu.VMEM((2 * ROWS, lanes), f32),
            pltpu.VMEM(x_table.shape, jnp.bfloat16),
            pltpu.VMEM(y_table.shape, jnp.bfloat16),
            quarter,
            pltpu.VMEM((3 * rp, total_x), f32),
            tiles, tiles,
            pltpu.VMEM((ny_dev, 2 * FOLD, LANES), f32),
            pltpu.VMEM((count, 2 * FOLD, LANES), f32),
            pltpu.VMEM((6 * pw, total_y), f32),
            pltpu.VMEM((2, nx_dev, kern_parts * pw, lanes), f32),
            pltpu.VMEM((nx_dev, 2 * ROWS, lanes), f32),
            pltpu.VMEM((total_x, LANES), f32),
            pltpu.VMEM((rows, LANES), f32),
            pltpu.VMEM((4 * layers, LANES), f32),
            pltpu.VMEM((4 * layers, LANES), f32),
            pltpu.VMEM((2, rows, LANES), f32),
            pltpu.VMEM((2, 4 * layers, LANES), f32),
            pltpu.VMEM((2, ROWS, LANES), f32),
            pltpu.VMEM((2, 2, ROWS, LANES), f32),
            pltpu.VMEM((3, 3, layers, 4, chunks, ROWS, LANES), f32),
            pltpu.VMEM((3, 3, layers, 3, rows, LANES), f32),
            pltpu.VMEM((2, rows, LANES), f32),
            pltpu.VMEM((2, 3, ROWS, LANES), f32),
            pltpu.VMEM((2, rows, LANES), f32),
            pltpu.VMEM((2, ROWS, LANES), f32),
            pltpu.VMEM((2, ROWS, LANES), f32),
            pltpu.VMEM((2, 2, ROWS, LANES), f32),
            pltpu.SemaphoreType.DMA((7,)),
            sems(nx_dev), sems(2 * nx_dev), sems(nx_dev), sems(8), sems(1), sems(1), sems(8),
            pltpu.SemaphoreType.REGULAR,
        ],
        compiler_params=pltpu.CompilerParams(
            collective_id=0, has_side_effects=True, vmem_limit_bytes=44 * 1024 * 1024
        ),
    )(*(pltpu.with_memory_space_constraint(value, pltpu.HBM) for value in inputs))
    new_velocity = velocity + impulse_scale * force
    new_disp = disp + drift_scale * new_velocity
    return (new_disp, new_velocity)


def solution(mesh):
    in_specs = (
        P(None, None, "sy", "sx"),
        P(None, None, "sy", "sx"),
        P(None, "sy", "sx"),
        P(None, None, "sy", "sx"),
        P(None, None, "sy", "sx"),
        P("sy", None, None, None, "sx"),
    )
    out_specs = (P(None, None, "sy", "sx"), P(None, None, "sy", "sx"))
    body = functools.partial(shards, mesh.shape["sx"], mesh.shape["sy"])
    return jax.shard_map(body, mesh=mesh, in_specs=in_specs, out_specs=out_specs, check_vma=False)
```

```python
import functools
import math

import jax
import jax.numpy as jnp
import numpy as np
from jax import lax
from jax.experimental import pallas as pl
from jax.experimental.pallas import tpu as pltpu
from jax.sharding import PartitionSpec as P

silicon = (1830.8, 471.18, 2.4799, 1.7322, 1.1e-06, 0.78734, 100390.0, 16.217, -0.59825, 2.7, 3.0)
germanium = (1769.0, 419.23, 2.4451, 1.7047, 9.0166e-07, 0.75627, 106430.0, 15.652, -0.43884, 2.8, 3.1)
faces = ((1, 0, 0), (0, 1, 0), (0, 0, 1), (-1, 0, 0), (0, -1, 0), (0, 0, -1))
edges = (
    (1, 1, 0), (1, -1, 0), (-1, 1, 0), (-1, -1, 0),
    (1, 0, 1), (1, 0, -1), (-1, 0, 1), (-1, 0, -1),
    (0, 1, 1), (0, 1, -1), (0, -1, 1), (0, -1, -1),
)
FACE_SLOTS = 4
lattice_step = 2.0
impulse_scale = 0.1
drift_scale = 0.05
LANES = 128
ROWS = 8
IM_LANE = 32
FOLD = 8
f32 = jnp.float32
MESH = pl.DeviceIdType.MESH


def split_table(table):
    table = table.astype(np.float32)
    high = table.astype(jnp.bfloat16)
    low = (table - high.astype(np.float32)).astype(jnp.bfloat16)
    return np.stack([high, low])


def angles(length, columns):
    ids = np.arange(length, dtype=np.int64)
    return (ids[:, None] * np.arange(columns, dtype=np.int64)[None, :] % length) * (2.0 * math.pi / length)


def line_table(length):
    half = length // 2
    angle = angles(length, half)
    sines = -np.sin(angle)
    sines[:, 0] = 1.0 - 2.0 * (np.arange(length) % 2)
    return split_table(np.concatenate([np.cos(angle), sines], axis=1))


def wave_table(length):
    angle = angles(length, length)
    return split_table(np.concatenate([np.cos(angle), np.sin(angle)], axis=1))


def dot3(values, high, low):
    count = values.shape[0]
    top = values.astype(jnp.bfloat16)
    coarse = top.astype(f32)
    both = jnp.concatenate([coarse, values - coarse], axis=0).astype(jnp.bfloat16)
    dot = functools.partial(jnp.dot, preferred_element_type=f32)
    twice = dot(both, high)
    return twice[:count] + (twice[count:] + dot(top, low))


def pick(is_ge, same, position, mean):
    si, ge = silicon[position], germanium[position]
    both = math.sqrt(si * ge) if mean == "geo" else 0.5 * (si + ge)
    return jnp.where(same, jnp.where(is_ge, f32(ge), f32(si)), f32(both))


def own_pick(is_ge, si, ge):
    return jnp.where(is_ge, f32(ge), f32(si))


def poly(v2, coefs):
    out = f32(coefs[-1])
    for coef in coefs[-2::-1]:
        out = out * v2 + f32(coef)
    return out


sin_coefs = [(-1) ** k * math.pi ** (2 * k + 1) / math.factorial(2 * k + 1) for k in range(6)]
cos_coefs = [(-1) ** k * math.pi ** (2 * k) / math.factorial(2 * k) for k in range(7)]


def bonds_of(layer, layers, slot):
    table = faces if slot < FACE_SLOTS else edges
    base = 0 if slot < FACE_SLOTS else len(faces)
    for entry, (dx, dy, dz) in enumerate(table):
        if 0 <= layer + dz < layers:
            yield base + entry, dx, dy, dz


def tersoff_rows(layer, layers, slots, shifted, chunk, codes, masks):
    def near(dx, dy, level, comp):
        return shifted[dx + 1, dy + 1, level, comp, chunk]

    own = [near(0, 0, layer, comp) for comp in range(3)]
    own_ge = near(0, 0, layer, 3) > 0.5
    h = own_pick(own_ge, silicon[8], germanium[8])
    d2 = own_pick(own_ge, silicon[7] ** 2, germanium[7] ** 2)
    c2 = own_pick(own_ge, silicon[6] ** 2, germanium[6] ** 2)
    ratio = own_pick(own_ge, silicon[6] ** 2 / silicon[7] ** 2, germanium[6] ** 2 / germanium[7] ** 2)
    beta = own_pick(own_ge, silicon[4], germanium[4])
    power = own_pick(own_ge, silicon[5], germanium[5])
    half_inv = own_pick(own_ge, 0.5 / silicon[5], 0.5 / germanium[5])
    data = []
    for slot in range(slots):
        code = codes[slot]
        bond = [jnp.full(code.shape, lattice_step, f32)] + [jnp.zeros(code.shape, f32) for _ in range(2)]
        kind = jnp.zeros(code.shape, f32)
        valid = jnp.zeros(code.shape, f32)
        for entry, dx, dy, dz in bonds_of(layer, layers, slot):
            hit = code == entry
            for comp, step in enumerate((dx, dy, dz)):
                place = near(dx, dy, layer + dz, comp)
                if step:
                    place = place + f32(lattice_step * step)
                bond[comp] = jnp.where(hit, place - own[comp], bond[comp])
            kind = jnp.where(hit, near(dx, dy, layer + dz, 3), kind)
            valid = jnp.where(hit, f32(1.0), valid)
        live = masks[slot].astype(f32) * valid
        dist2 = bond[0] * bond[0] + bond[1] * bond[1] + bond[2] * bond[2]
        inv = lax.rsqrt(dist2)
        dist = dist2 * inv
        unit = [b * inv for b in bond]
        same = (kind > 0.5) == own_ge
        inner = pick(own_ge, same, 9, "geo")
        span_si = 1.0 / (silicon[10] - silicon[9])
        span_ge = 1.0 / (germanium[10] - germanium[9])
        span_mix = 1.0 / (math.sqrt(silicon[10] * germanium[10]) - math.sqrt(silicon[9] * germanium[9]))
        span = jnp.where(same, jnp.where(own_ge, f32(span_ge), f32(span_si)), f32(span_mix))
        phase = (dist - inner) * span
        v = jnp.clip(phase, 0.0, 1.0) - 0.5
        v2 = v * v
        fade = 0.5 - 0.5 * v * poly(v2, sin_coefs)
        fade_slope = f32(-0.5 * math.pi) * span * poly(v2, cos_coefs)
        below, above = phase < 0.0, phase > 1.0
        cutoff = jnp.where(below, 1.0, jnp.where(above, 0.0, fade))
        slope = jnp.where(below | above, 0.0, fade_slope) * live
        mu = pick(own_ge, same, 3, "mean")
        lam = pick(own_ge, same, 2, "mean")
        attract = pick(own_ge, same, 1, "geo") * jnp.exp(-mu * dist)
        repulse = pick(own_ge, same, 0, "geo") * jnp.exp(-lam * dist)
        data.append(dict(unit=unit, inv=inv, weight=live * cutoff, slope=slope, mu=mu, lam=lam, att=attract, rep=repulse))
    zeta = [jnp.zeros_like(h) for _ in range(slots)]
    for s in range(slots):
        for t in range(s):
            us, ut = data[s]["unit"], data[t]["unit"]
            q = us[0] * ut[0] + us[1] * ut[1] + us[2] * ut[2]
            away = h - q
            gap = away * away
            g = 1.0 + ratio * gap / (d2 + gap)
            zeta[s] = zeta[s] + data[t]["weight"] * g
            zeta[t] = zeta[t] + data[s]["weight"] * g
    pull, radial = [], []
    for s in range(slots):
        item = data[s]
        z = jnp.exp(power * jnp.log(beta * zeta[s]))
        order = jnp.exp(-jnp.log(1.0 + z) * half_inv)
        bound = order * item["att"]
        pull.append(0.25 * item["weight"] * bound * z / (zeta[s] * (1.0 + z)))
        radial.append(
            0.5 * (item["slope"] * (item["rep"] - bound) + item["weight"] * (item["mu"] * bound - item["lam"] * item["rep"]))
        )
    turn = [[jnp.zeros_like(h) for _ in range(3)] for _ in range(slots)]
    spread = [jnp.zeros_like(h) for _ in range(slots)]
    for s in range(slots):
        for t in range(s):
            us, ut = data[s]["unit"], data[t]["unit"]
            q = us[0] * ut[0] + us[1] * ut[1] + us[2] * ut[2]
            away = h - q
            gap = away * away
            inv = 1.0 / (d2 + gap)
            g = 1.0 + ratio * gap * inv
            tilt = -2.0 * c2 * away * inv * inv
            pair = (pull[s] * data[t]["weight"] + pull[t] * data[s]["weight"]) * tilt
            for comp in range(3):
                turn[s][comp] = turn[s][comp] + pair * ut[comp]
                turn[t][comp] = turn[t][comp] + pair * us[comp]
            spread[s] = spread[s] + pull[t] * g
            spread[t] = spread[t] + pull[s] * g
    grads = []
    for s in range(slots):
        item = data[s]
        unit = item["unit"]
        along = turn[s][0] * unit[0] + turn[s][1] * unit[1] + turn[s][2] * unit[2]
        line = radial[s] + item["slope"] * spread[s] - along * item["inv"]
        grads.append([turn[s][comp] * item["inv"] + line * unit[comp] for comp in range(3)])
    return grads


def step_kernel(
    dims,
    disp_hbm, kinds_hbm, codes_hbm, masks_hbm, kern_hbm, x_hbm, y_hbm,
    out_ref,
    disp_ref, kinds_ref, codes_ref, masks_ref, kern_all, kern_out, kern_rest, x_tab, y_tab, line_in, buf, send2, recv2, send3, recv3, waves, kern_in, rest_in, fields,
    col_out, top_out, low_out, col_in, row_in, spot_out, spot_in, shifted, spill,
    side_out, edge_out, side_in, edge_in, tip_out, tip_in,
    load_sem, p1_sem, k_sem, rest_sem, halo_sem, p2_sem, p3_sem, rim_sem, relay_sem,
):
    nx_dev, ny_dev, layers, slots, rows, total_x, total_y, pw, kyw = dims
    count = nx_dev * ny_dev
    rp = rows // nx_dev
    chunks = rows // ROWS
    b = lax.axis_index("sx")
    a = lax.axis_index("sy")
    me = a * nx_dev + b
    half = ny_dev // 2
    early = a < half
    kind = jnp.where(early, 0, 1)

    def pair_of(dev_x, dev_y):
        first = dev_y < half
        return jnp.where(first, dev_y, ny_dev - 1 - dev_y) * (2 * nx_dev) + dev_x + jnp.where(first, 0, nx_dev)

    mine = pair_of(b, a)
    lane = lax.broadcasted_iota(jnp.int32, (rows, LANES), 1)
    row = lax.broadcasted_iota(jnp.int32, (rows, LANES), 0)
    lane1 = lax.broadcasted_iota(jnp.int32, (ROWS, LANES), 1)

    def wrap(value, size):
        return jnp.where(value >= size, value - size, value)

    def each_other(visit):
        for i in reversed(range(nx_dev)):
            other_x = wrap(b + i, nx_dev)

            def body(j, carry, other_x=other_x):
                visit(other_x, wrap(a + j, ny_dev))
                return carry

            lax.fori_loop(0 if i else 1, ny_dev, body, None, unroll=count <= 64)

    def beside(step_x, step_y):
        return {"sx": wrap(b + step_x % nx_dev, nx_dev), "sy": wrap(a + step_y % ny_dev, ny_dev)}

    def remote(src, dst, sems, index, dev):
        return pltpu.make_async_remote_copy(
            src_ref=src, dst_ref=dst, send_sem=sems.at[0, index], recv_sem=sems.at[1, index],
            device_id=dev, device_id_type=MESH,
        )

    barrier = pltpu.get_barrier_semaphore()

    low = 2 ** ((ny_dev.bit_length() - 1) // 2)
    lines = ny_dev // low
    side, line = lax.rem(a, low), a // low
    cube = [
        {"sx": wrap(b + i, nx_dev), "sy": line * low + wrap(side + j, low)}
        for j in range(low) for i in range(nx_dev) if i or j
    ]
    near = cube + [{"sx": b, "sy": wrap(line + k, lines) * low + side} for k in range(1, lines)]
    for dev in near:
        pl.semaphore_signal(barrier, inc=1, device_id=dev, device_id_type=MESH)

    loads = [
        pltpu.make_async_copy(x_hbm, x_tab, load_sem.at[0]),
        pltpu.make_async_copy(y_hbm, y_tab, load_sem.at[1]),
        pltpu.make_async_copy(disp_hbm, disp_ref, load_sem.at[2]),
        None,
        pltpu.make_async_copy(codes_hbm, codes_ref, load_sem.at[4]),
        pltpu.make_async_copy(masks_hbm, masks_ref, load_sem.at[5]),
        pltpu.make_async_copy(kinds_hbm, kinds_ref, load_sem.at[6]),
    ]
    def stiff_row(slot):
        group, r = slot // pw, slot % pw
        if group == 2 * nx_dev:
            return 0
        o, t = group // nx_dev, group % nx_dev
        late = (o + 1) * nx_dev - 1 - t
        if r:
            late_row = late * pw + pw - r
        else:
            late_row = (late + 1) * pw if late + 1 < 2 * nx_dev else 0
        return jnp.where(early, group * pw + r, late_row)

    for i in (2, 6):
        loads[i].start()
    for slot in range((2 * nx_dev + 1) * pw):
        pltpu.make_async_copy(kern_hbm.at[stiff_row(slot)], kern_all.at[slot], load_sem.at[3]).start()
    for i in (0, 1, 4, 5):
        loads[i].start()

    def field(level, comp):
        if comp < 3:
            return disp_ref[level, comp].reshape(rows, LANES)
        return kinds_ref[level].astype(f32)

    pl.semaphore_wait(barrier, len(near))
    for dev in cube:
        pl.semaphore_signal(relay_sem, inc=1, device_id=dev, device_id_type=MESH)
    loads[2].wait()

    p1 = []
    kc = []
    for k in range(1, nx_dev):
        other = wrap(b + k, nx_dev)
        p1.append(remote(disp_ref.at[0, :, other], line_in.at[b], p1_sem, k, {"sx": other, "sy": a}))
    for copy in p1:
        copy.start()
    for comp in range(3):
        line_in[b, comp] = disp_ref[0, comp, b]
    halo = []
    for i, step in enumerate((1, -1)):
        halo.append(remote(col_out, col_in.at[i], halo_sem, i, beside(step, 0)))
    n = 2
    for j, (step_y, src) in enumerate(((1, low_out), (-1, top_out))):
        halo.append(remote(src, row_in.at[j], halo_sem, n, beside(0, step_y)))
        for i, step_x in enumerate((1, -1)):
            dest = spot_in.at[j, i, pl.ds(0, 1)]
            halo.append(remote(spot_out.at[j, pl.ds(0, 1)], dest, halo_sem, n + 1 + i, beside(step_x, step_y)))
        n += 3
    loads[6].wait()
    packed = jnp.zeros((rows, LANES), f32)
    for q in range(4 * layers):
        base = field(q // 4, q % 4)
        top_out[q : q + 1, :] = base[0:1]
        low_out[q : q + 1, :] = base[rows - 1 : rows]
        packed = jnp.where(lane == q, base[:, 0:1], packed)
        packed = jnp.where(lane == 4 * layers + q, base[:, LANES - 1 : LANES], packed)
    col_out[...] = packed
    spot_out[0, 0:1] = packed[rows - 1 : rows]
    spot_out[1, 0:1] = packed[0:1]

    pltpu.make_async_copy(kern_all, kern_all, load_sem.at[3]).wait()
    spots = [(c, c, 0) for c in range(3)] + [(c, d, ri) for ri in range(2) for c, d in ((0, 1), (0, 2), (1, 2))]

    def stiff_part(group, m):
        c, d, ri = spots[m]
        return kern_all[group * pw : (group + 1) * pw, c, d, ri, :]

    lane_k = lax.broadcasted_iota(jnp.int32, (pw, LANES), 1)
    for group in range(2 * nx_dev):
        if kyw % LANES == 0:
            for m in range(9):
                kern_out[group, m * pw : (m + 1) * pw] = stiff_part(group, m)
        else:
            for m in range(5):
                high = stiff_part(group, m + 5) if m < 4 else jnp.zeros((pw, kyw), f32)
                tile = jnp.concatenate([stiff_part(group, m), high], axis=1)
                if m == 4 and pw == FOLD:
                    turned = pltpu.roll(pltpu.roll(tile, LANES // 2, 1), FOLD // 2, 0)
                    tile = jnp.where(lane_k < LANES // 2, tile, turned)
                kern_out[group, m * pw : (m + 1) * pw] = tile
    kern_rest[...] = jnp.zeros_like(kern_rest)
    for m in range(9 if kyw % LANES == 0 else 5):
        edge_part = stiff_part(2 * nx_dev, m)
        if kyw % LANES:
            high = stiff_part(2 * nx_dev, m + 5) if m < 4 else jnp.zeros((pw, kyw), f32)
            edge_part = jnp.concatenate([edge_part, high], axis=1)
        kern_rest[m : m + 1] = edge_part[0:1]
    kern_in[kind, b] = kern_out[b]
    used = pl.ds(0, 4 * FOLD + FOLD // 2 if kyw % LANES and pw == FOLD else kern_out.shape[1])
    for k in range(1, nx_dev):
        other = wrap(b + k, nx_dev)
        kc.append(remote(kern_out.at[other, used], kern_in.at[kind, b, used], k_sem, k, {"sx": other, "sy": a}))
    pl.semaphore_wait(relay_sem, len(cube))
    far = []
    for k in range(nx_dev):
        other = wrap(b + k, nx_dev)
        dev = {"sx": other, "sy": ny_dev - 1 - a}
        far.append(remote(kern_out.at[nx_dev + other, used], kern_in.at[kind, b, used], k_sem, nx_dev + k, dev))
    rest_to = {"sx": jnp.zeros_like(b), "sy": jnp.where(a == half, 0, ny_dev - a)}
    rest = remote(kern_rest, rest_in.at[b], rest_sem, b, rest_to)
    for copy in far:
        copy.start()

    for copy in kc:
        copy.start()

    @pl.when(a >= half)
    def _():
        rest.start()

    for copy in p1:
        copy.wait()
    for src in range(nx_dev):
        for comp in range(3):
            buf[comp * rp : (comp + 1) * rp, src * LANES : (src + 1) * LANES] = line_in[src, comp]
    loads[0].wait()
    buf[...] = dot3(buf[:, :total_x], x_tab[0], x_tab[1])
    per = LANES // pw
    lane_p = lax.broadcasted_iota(jnp.int32, (rp, LANES), 1)
    for dest in range(count):
        block, part = dest // per, dest % per
        tile = jnp.zeros((rp, LANES), f32)
        for ri in range(2):
            for comp in range(3):
                at = ri * IM_LANE + comp * pw
                col = ri * (total_x // 2) + block * LANES
                piece = buf[comp * rp : (comp + 1) * rp, col : col + LANES]
                shift = (at - part * pw) % LANES
                if shift:
                    piece = pltpu.roll(piece, shift, 1)
                tile = jnp.where((lane_p >= at) & (lane_p < at + pw), piece, tile)
        if rp == FOLD:
            turned = pltpu.roll(pltpu.roll(tile, LANES // 2, 1), FOLD // 2, 0)
            tile = jnp.where(lane_p < LANES // 2, tile, turned)
        send2[dest] = tile
    recv2[me] = send2[mine]
    some_rows = pl.ds(0, rp // 2 if rp == FOLD else rp)

    def all_start2():
        def send(other_x, other_y):
            src = send2.at[pair_of(other_x, other_y), some_rows]
            remote(src, recv2.at[me, some_rows], p2_sem, 0, {"sx": other_x, "sy": other_y}).start()

        each_other(send)

    lot = pl.ds(0, FOLD + (FOLD // 2 if pw == FOLD else pw))

    def all_start3():
        def send(other_x, other_y):
            src = send3.at[other_y, lot]
            remote(src, recv3.at[mine, lot], p3_sem, 0, {"sx": other_x, "sy": other_y}).start()

        each_other(send)

    def all_wait3():
        for i in range(nx_dev):
            some = send3.at[pl.ds(0, ny_dev - (1 if i == 0 else 0)), lot]
            pltpu.make_async_copy(some, some, p3_sem.at[0, 0]).wait()
        some = recv3.at[pl.ds(0, count - 1), lot]
        pltpu.make_async_copy(some, some, p3_sem.at[1, 0]).wait()

    def all_wait2():
        some = pl.ds(0, count - 1)
        pltpu.make_async_copy(send2.at[some, some_rows], send2.at[some, some_rows], p2_sem.at[0, 0]).wait()
        pltpu.make_async_copy(recv2.at[some, some_rows], recv2.at[some, some_rows], p2_sem.at[1, 0]).wait()

    for copy in halo:
        copy.start()
    all_start2()

    for copy in halo:
        copy.wait()
    first_row, last_row = row == 0, row == rows - 1
    first_lane, last_lane = lane == 0, lane == LANES - 1
    full = (rows, LANES)

    def keep(dx, dy, q, value):
        for chunk in range(chunks):
            shifted[dx + 1, dy + 1, q // 4, q % 4, chunk] = value[chunk * ROWS : (chunk + 1) * ROWS]

    for q in range(4 * layers):
        base = field(q // 4, q % 4)
        left = jnp.broadcast_to(col_in[0][:, 4 * layers + q : 4 * layers + q + 1], full)
        right = jnp.broadcast_to(col_in[1][:, q : q + 1], full)
        for dy in (-1, 0, 1):
            if dy == 0:
                mid, lo, hi = base, left, right
            else:
                edge = first_row if dy == -1 else last_row
                j = 0 if dy == -1 else 1
                turn = 1 if dy == -1 else rows - 1
                mid = jnp.where(edge, row_in[j, q : q + 1, :], pltpu.roll(base, turn, 0))
                at = 4 * layers + q
                lo = jnp.where(edge, spot_in[j, 0, 0:1, at : at + 1], pltpu.roll(left, turn, 0))
                hi = jnp.where(edge, spot_in[j, 1, 0:1, q : q + 1], pltpu.roll(right, turn, 0))
            keep(0, dy, q, mid)
            keep(-1, dy, q, jnp.where(first_lane, lo, pltpu.roll(mid, 1, 1)))
            keep(1, dy, q, jnp.where(last_lane, hi, pltpu.roll(mid, LANES - 1, 1)))

    for copy in kc:
        copy.wait()
    loads[1].wait()
    all_wait2()
    width = 3 * pw

    arrived = recv2[...].reshape(total_y, LANES)
    if rp == FOLD:
        turned = pltpu.roll(arrived, LANES // 2, 1)
        turned = pltpu.roll(turned, FOLD // 2, 0)
        spread_row = lax.broadcasted_iota(jnp.int32, (total_y, LANES), 0) % FOLD
        arrived = jnp.where(spread_row < FOLD // 2, arrived, turned)
    table = jnp.transpose(arrived)[: 2 * IM_LANE]
    both = dot3(table, y_tab[0], y_tab[1])
    cos_part, sin_part = both[:, :total_y], both[:, total_y:]
    for copy in far:
        copy.wait()

    @pl.when(a >= half)
    def _():
        rest.wait_send()

    @pl.when(early & (b == 0))
    def _():
        for src in range(nx_dev):
            pltpu.make_async_copy(rest_in.at[src], rest_in.at[src], rest_sem.at[1, src]).wait()
            for m in range(9 if kyw % LANES == 0 else 5):
                line = rest_in[src, m : m + 1, :]
                if m == 4 and kyw % LANES:
                    line = jnp.where(lane_k[0:1] < LANES // 2, line, kern_in[1, src, m * pw : m * pw + 1, :])
                kern_in[1, src, m * pw : m * pw + 1, :] = line

    row_k = lax.broadcasted_iota(jnp.int32, (pw, LANES), 0)
    pair_row = lax.broadcasted_iota(jnp.int32, (pw, total_y), 0) + mine * pw

    def stiff(which, m):
        if kyw % LANES == 0:
            return jnp.concatenate([kern_in[which, src, m * pw : (m + 1) * pw] for src in range(nx_dev)], axis=1)

        def tile_of(src):
            tile = kern_in[which, src, m % 5 * pw : (m % 5 + 1) * pw]
            if m == 4 and pw == FOLD:
                turned = pltpu.roll(pltpu.roll(tile, LANES // 2, 1), FOLD // 2, 0)
                tile = jnp.where(row_k < FOLD // 2, tile, turned)
            return tile

        pieces = []
        for pair in range(nx_dev // 2):
            one, two = tile_of(2 * pair), tile_of(2 * pair + 1)
            if m < 5:
                two = pltpu.roll(two, LANES // 2, 1)
            else:
                one = pltpu.roll(one, LANES // 2, 1)
            pieces.append(jnp.where(lane_k < LANES // 2, one, two))
        return jnp.concatenate(pieces, axis=1)

    def push(which, sr, si):
        fr, fi = [], []
        for comp in range(3):
            diag = stiff(which, comp)
            fr.append(diag * sr[comp])
            fi.append(diag * si[comp])
        for m, (c, d) in enumerate(((0, 1), (0, 2), (1, 2))):
            kr, ki = stiff(which, 3 + m), stiff(which, 6 + m)
            fr[c] = fr[c] + kr * sr[d] - ki * si[d]
            fi[c] = fi[c] + kr * si[d] + ki * sr[d]
            fr[d] = fr[d] + kr * sr[c] + ki * si[c]
            fi[d] = fi[d] + kr * si[c] - ki * sr[c]
        return fr, fi

    ends = pair_row == 0
    ar, ai, br, bi = [], [], [], []
    for comp in range(3):
        re_at = slice(comp * pw, (comp + 1) * pw)
        im_at = slice(IM_LANE + comp * pw, IM_LANE + (comp + 1) * pw)
        re_c, re_s, im_c, im_s = cos_part[re_at], sin_part[re_at], cos_part[im_at], sin_part[im_at]
        ar.append(re_c + jnp.where(ends, 0.0, im_s))
        ai.append(jnp.where(ends, 0.0, im_c) - re_s)
        br.append(jnp.where(ends, im_c, re_c - im_s))
        bi.append(jnp.where(ends, -im_s, -im_c - re_s))
    ar, ai = push(0, ar, ai)
    br, bi = push(1, br, bi)
    up, down = [], []
    for comp in range(3):
        up.append(jnp.where(ends, ar[comp], ar[comp] + br[comp]))
        down.append(jnp.where(ends, ai[comp], ai[comp] + bi[comp]))
    for comp in range(3):
        up.append(jnp.where(ends, br[comp], ai[comp] - bi[comp]))
        down.append(jnp.where(ends, bi[comp], br[comp] - ar[comp]))
    waves[: 2 * width] = dot3(jnp.concatenate(up, axis=0), y_tab[0, :, :total_y], y_tab[1, :, :total_y]) - dot3(
        jnp.concatenate(down, axis=0), y_tab[0, :, total_y:], y_tab[1, :, total_y:]
    )
    lane_w = lax.broadcasted_iota(jnp.int32, (pw, LANES), 1)
    quarter = LANES // 4
    for dest in range(ny_dev):
        col, part = dest * rows // LANES * LANES, dest * rows % LANES

        def block_of(index, at):
            piece = waves[index * pw : (index + 1) * pw, col : col + LANES]
            shift = (at - part) % LANES
            return pltpu.roll(piece, shift, 1) if shift else piece

        tile = block_of(3, 3 * quarter)
        for comp in (2, 1, 0):
            tile = jnp.where(lane_w < (comp + 1) * quarter, block_of(comp, comp * quarter), tile)
        send3[dest, :pw] = tile
        tile = jnp.where(lane_w < 2 * quarter, block_of(4, quarter), block_of(5, 2 * quarter))
        if pw == FOLD:
            turned = pltpu.roll(pltpu.roll(tile, LANES // 2, 1), FOLD // 2, 0)
            tile = jnp.where((lane_w >= quarter) & (lane_w < 3 * quarter), tile, turned)
        send3[dest, FOLD : FOLD + pw] = tile
    recv3[mine] = send3[a]
    all_start3()

    loads[4].wait()
    loads[5].wait()

    @pl.loop(0, chunks)
    def _(chunk):
        own_sum = []
        parts = {}
        at = pl.ds(pl.multiple_of(chunk * ROWS, ROWS), ROWS)
        for layer in range(layers):
            codes = [codes_ref[layer, slot, at, :] for slot in range(slots)]
            masks = [masks_ref[layer, slot, at, :] for slot in range(slots)]
            grads = tersoff_rows(layer, layers, slots, shifted, chunk, codes, masks)
            total = [sum(grads[s][comp] for s in range(slots)) for comp in range(3)]
            own_sum.append(total)
            for slot in range(slots):
                for entry, dx, dy, dz in bonds_of(layer, layers, slot):
                    hit = codes[slot] == entry
                    for comp in range(3):
                        key = (dx, dy, layer + dz, comp)
                        term = jnp.where(hit, grads[slot][comp], 0.0)
                        parts[key] = parts[key] + term if key in parts else term
        for level in range(layers):
            for comp in range(3):
                key = (0, 0, level, comp)
                here = own_sum[level][comp]
                parts[key] = here - parts[key] if key in parts else here
        for (dx, dy, level, comp), value in parts.items():
            signed = value if (dx, dy) == (0, 0) else -value
            spill[dx + 1, dy + 1, level, comp, at, :] = signed

    left_pack = jnp.zeros(full, f32)
    right_pack = jnp.zeros(full, f32)
    edge_out[...] = jnp.zeros_like(edge_out)
    spots_out = [jnp.zeros((1, LANES), f32) for _ in range(2)]
    lane0 = lane1[0:1]
    for q in range(3 * layers):
        level, comp = q // 3, q % 3
        lines = []
        for dx in (-1, 0, 1):
            part = spill[dx + 1, 1, level, comp]
            down = spill[dx + 1, 2, level, comp]
            up = spill[dx + 1, 0, level, comp]
            part = part + jnp.where(first_row, 0.0, pltpu.roll(down, 1, 0))
            part = part + jnp.where(last_row, 0.0, pltpu.roll(up, rows - 1, 0))
            edge_out[0, dx + 1, q : q + 1, :] = down[rows - 1 : rows]
            edge_out[1, dx + 1, q : q + 1, :] = up[0:1]
            if dx:
                end = LANES - 1 if dx > 0 else 0
                for j, line in enumerate((down[rows - 1 : rows], up[0:1])):
                    hit = lane0 == (ROWS if dx > 0 else 0) + q
                    spots_out[j] = jnp.where(hit, line[:, end : end + 1], spots_out[j])
            lines.append(part)
        left_pack = jnp.where(lane == q, lines[0][:, 0:1], left_pack)
        right_pack = jnp.where(lane == q, lines[2][:, LANES - 1 : LANES], right_pack)
        out_ref[level, comp] = (
            lines[1]
            + jnp.where(first_lane, 0.0, pltpu.roll(lines[2], 1, 1))
            + jnp.where(last_lane, 0.0, pltpu.roll(lines[0], LANES - 1, 1))
        )
    side_out[0] = right_pack
    side_out[1] = left_pack
    for j in range(2):
        edge_out[j, 1] = (
            edge_out[j, 1]
            + jnp.where(lane1 == 0, 0.0, pltpu.roll(edge_out[j, 2], 1, 1))
            + jnp.where(lane1 == LANES - 1, 0.0, pltpu.roll(edge_out[j, 0], LANES - 1, 1))
        )
    for j in range(2):
        tip_out[j, 0:1] = spots_out[j]
    rim = []
    for i, step in enumerate((1, -1)):
        rim.append(remote(side_out.at[i], side_in.at[i], rim_sem, i, beside(step, 0)))
    n = 2
    for j, step_y in enumerate((1, -1)):
        rim.append(remote(edge_out.at[j, 1], edge_in.at[j], rim_sem, n, beside(0, step_y)))
        for i, dx in enumerate((-1, 1)):
            dest = tip_in.at[j, i, pl.ds(0, 1)]
            rim.append(remote(tip_out.at[j, pl.ds(0, 1)], dest, rim_sem, n + 1 + i, beside(dx, step_y)))
        n += 3
    for copy in rim:
        copy.start()

    all_wait3()
    row_w = lax.broadcasted_iota(jnp.int32, (pw, LANES), 0)
    for src in range(count):
        first, second = recv3[src, :pw], recv3[src, FOLD : FOLD + pw]
        if pw == FOLD:
            turned = pltpu.roll(pltpu.roll(second, LANES // 2, 1), FOLD // 2, 0)
            second = jnp.where(row_w < FOLD // 2, second, turned)
        fields[src * pw : (src + 1) * pw] = first
        fields[total_x // 2 + src * pw : total_x // 2 + (src + 1) * pw] = jnp.where(
            lane_w < quarter, pltpu.roll(first, quarter, 1), second
        )
    own_x = pl.ds(pl.multiple_of(b * LANES, LANES), LANES)
    top = fields[...].astype(jnp.bfloat16)
    low_part = (fields[...] - top.astype(f32)).astype(jnp.bfloat16)
    dot = functools.partial(jnp.dot, preferred_element_type=f32)
    fine_x = x_tab[0, own_x, :]
    twice = dot(jnp.concatenate([fine_x, x_tab[1, own_x, :]], axis=0), top)
    real = twice[:LANES] + (dot(fine_x, low_part) + twice[LANES:])
    real = jnp.transpose(real) * f32(-1.0 / (total_x * total_y))
    for copy in rim:
        copy.wait()
    for q in range(3 * layers):
        level, comp = q // 3, q % 3
        value = out_ref[level, comp]
        value = value + jnp.where(first_lane, side_in[0][:, q : q + 1], 0.0)
        value = value + jnp.where(last_lane, side_in[1][:, q : q + 1], 0.0)
        for j, edge in enumerate((first_row, last_row)):
            line = edge_in[j, q : q + 1, :]
            value = value + jnp.where(edge, line, 0.0)
            value = value + jnp.where(edge & first_lane, tip_in[j, 1, 0:1, ROWS + q : ROWS + q + 1], 0.0)
            value = value + jnp.where(edge & last_lane, tip_in[j, 0, 0:1, q : q + 1], 0.0)
        out_ref[level, comp] = value
    for comp in range(3):
        out_ref[0, comp] = out_ref[0, comp] + real[comp * rows : (comp + 1) * rows]


def shards(nx_dev, ny_dev, disp, velocity, kinds, neighbours, pad_mask, kernel):
    layers, comps, rows, cols = disp.shape
    slots = neighbours.shape[1]
    total_x, total_y = cols * nx_dev, rows * ny_dev
    count = nx_dev * ny_dev
    kx_block, kyw = kernel.shape[0], kernel.shape[4]
    pw = kx_block // (2 * nx_dev)
    rp = rows // nx_dev
    kern_parts = 9 if kyw % LANES == 0 else 5
    lanes = kyw if kern_parts == 9 else LANES
    x_table = jnp.asarray(line_table(total_x))
    y_table = jnp.asarray(wave_table(total_y))
    chunks = rows // ROWS
    vmem = pl.BlockSpec(memory_space=pltpu.VMEM)
    hbm = pl.BlockSpec(memory_space=pl.ANY)
    tiles = pltpu.VMEM((count, rp, LANES), f32)
    quarter = pltpu.VMEM((nx_dev, 3, rp, LANES), f32)
    sems = lambda n: pltpu.SemaphoreType.DMA((2, n))
    inputs = (disp.reshape(layers, comps, nx_dev, rp, cols), kinds, neighbours, pad_mask, kernel, x_table, y_table)
    force = pl.pallas_call(
        functools.partial(step_kernel, (nx_dev, ny_dev, layers, slots, rows, total_x, total_y, pw, kyw)),
        out_shape=jax.ShapeDtypeStruct(disp.shape, f32),
        in_specs=[hbm] * 7,
        out_specs=vmem,
        scratch_shapes=[
            pltpu.VMEM((layers, comps, nx_dev, rp, cols), f32),
            pltpu.VMEM(kinds.shape, jnp.int32),
            pltpu.VMEM(neighbours.shape, jnp.int32),
            pltpu.VMEM(pad_mask.shape, jnp.int32),
            pltpu.VMEM(((2 * nx_dev + 1) * pw, *kernel.shape[1:]), f32),
            pltpu.VMEM((2 * nx_dev, kern_parts * pw, lanes), f32),
            pltpu.VMEM((2 * ROWS, lanes), f32),
            pltpu.VMEM(x_table.shape, jnp.bfloat16),
            pltpu.VMEM(y_table.shape, jnp.bfloat16),
            quarter,
            pltpu.VMEM((3 * rp, total_x), f32),
            tiles, tiles,
            pltpu.VMEM((ny_dev, 2 * FOLD, LANES), f32),
            pltpu.VMEM((count, 2 * FOLD, LANES), f32),
            pltpu.VMEM((6 * pw, total_y), f32),
            pltpu.VMEM((2, nx_dev, kern_parts * pw, lanes), f32),
            pltpu.VMEM((nx_dev, 2 * ROWS, lanes), f32),
            pltpu.VMEM((total_x, LANES), f32),
            pltpu.VMEM((rows, LANES), f32),
            pltpu.VMEM((4 * layers, LANES), f32),
            pltpu.VMEM((4 * layers, LANES), f32),
            pltpu.VMEM((2, rows, LANES), f32),
            pltpu.VMEM((2, 4 * layers, LANES), f32),
            pltpu.VMEM((2, ROWS, LANES), f32),
            pltpu.VMEM((2, 2, ROWS, LANES), f32),
            pltpu.VMEM((3, 3, layers, 4, chunks, ROWS, LANES), f32),
            pltpu.VMEM((3, 3, layers, 3, rows, LANES), f32),
            pltpu.VMEM((2, rows, LANES), f32),
            pltpu.VMEM((2, 3, ROWS, LANES), f32),
            pltpu.VMEM((2, rows, LANES), f32),
            pltpu.VMEM((2, ROWS, LANES), f32),
            pltpu.VMEM((2, ROWS, LANES), f32),
            pltpu.VMEM((2, 2, ROWS, LANES), f32),
            pltpu.SemaphoreType.DMA((7,)),
            sems(nx_dev), sems(2 * nx_dev), sems(nx_dev), sems(8), sems(1), sems(1), sems(8),
            pltpu.SemaphoreType.REGULAR,
        ],
        compiler_params=pltpu.CompilerParams(
            collective_id=0, has_side_effects=True, vmem_limit_bytes=44 * 1024 * 1024
        ),
    )(*(pltpu.with_memory_space_constraint(value, pltpu.HBM) for value in inputs))
    new_velocity = velocity + impulse_scale * force
    new_disp = disp + drift_scale * new_velocity
    return (new_disp, new_velocity)


def solution(mesh):
    in_specs = (
        P(None, None, "sy", "sx"),
        P(None, None, "sy", "sx"),
        P(None, "sy", "sx"),
        P(None, None, "sy", "sx"),
        P(None, None, "sy", "sx"),
        P("sy", None, None, None, "sx"),
    )
    out_specs = (P(None, None, "sy", "sx"), P(None, None, "sy", "sx"))
    body = functools.partial(shards, mesh.shape["sx"], mesh.shape["sy"])
    return jax.shard_map(body, mesh=mesh, in_specs=in_specs, out_specs=out_specs, check_vma=False)
```

```python
import functools
import math

import jax
import jax.numpy as jnp
import numpy as np
from jax import lax
from jax.experimental import pallas as pl
from jax.experimental.pallas import tpu as pltpu
from jax.sharding import PartitionSpec as P

silicon = (1830.8, 471.18, 2.4799, 1.7322, 1.1e-06, 0.78734, 100390.0, 16.217, -0.59825, 2.7, 3.0)
germanium = (1769.0, 419.23, 2.4451, 1.7047, 9.0166e-07, 0.75627, 106430.0, 15.652, -0.43884, 2.8, 3.1)
faces = ((1, 0, 0), (0, 1, 0), (0, 0, 1), (-1, 0, 0), (0, -1, 0), (0, 0, -1))
edges = (
    (1, 1, 0), (1, -1, 0), (-1, 1, 0), (-1, -1, 0),
    (1, 0, 1), (1, 0, -1), (-1, 0, 1), (-1, 0, -1),
    (0, 1, 1), (0, 1, -1), (0, -1, 1), (0, -1, -1),
)
FACE_SLOTS = 4
lattice_step = 2.0
impulse_scale = 0.1
drift_scale = 0.05
LANES = 128
ROWS = 8
IM_LANE = 32
FOLD = 8
f32 = jnp.float32
MESH = pl.DeviceIdType.MESH


def split_table(table):
    table = table.astype(np.float32)
    high = table.astype(jnp.bfloat16)
    low = (table - high.astype(np.float32)).astype(jnp.bfloat16)
    return np.stack([high, low])


def angles(length, columns):
    ids = np.arange(length, dtype=np.int64)
    return (ids[:, None] * np.arange(columns, dtype=np.int64)[None, :] % length) * (2.0 * math.pi / length)


def line_table(length):
    half = length // 2
    angle = angles(length, half)
    sines = -np.sin(angle)
    sines[:, 0] = 1.0 - 2.0 * (np.arange(length) % 2)
    return split_table(np.concatenate([np.cos(angle), sines], axis=1))


def wave_table(length):
    angle = angles(length, length)
    return split_table(np.concatenate([np.cos(angle), np.sin(angle)], axis=1))


def dot3(values, high, low):
    count = values.shape[0]
    top = values.astype(jnp.bfloat16)
    coarse = top.astype(f32)
    both = jnp.concatenate([coarse, values - coarse], axis=0).astype(jnp.bfloat16)
    dot = functools.partial(jnp.dot, preferred_element_type=f32)
    twice = dot(both, high)
    return twice[:count] + (twice[count:] + dot(top, low))


def pick(is_ge, same, position, mean):
    si, ge = silicon[position], germanium[position]
    both = math.sqrt(si * ge) if mean == "geo" else 0.5 * (si + ge)
    return jnp.where(same, jnp.where(is_ge, f32(ge), f32(si)), f32(both))


def own_pick(is_ge, si, ge):
    return jnp.where(is_ge, f32(ge), f32(si))


def poly(v2, coefs):
    out = f32(coefs[-1])
    for coef in coefs[-2::-1]:
        out = out * v2 + f32(coef)
    return out


sin_coefs = [(-1) ** k * math.pi ** (2 * k + 1) / math.factorial(2 * k + 1) for k in range(6)]
cos_coefs = [(-1) ** k * math.pi ** (2 * k) / math.factorial(2 * k) for k in range(7)]


def bonds_of(layer, layers, slot):
    table = faces if slot < FACE_SLOTS else edges
    base = 0 if slot < FACE_SLOTS else len(faces)
    for entry, (dx, dy, dz) in enumerate(table):
        if 0 <= layer + dz < layers:
            yield base + entry, dx, dy, dz


def tersoff_rows(layer, layers, slots, shifted, chunk, codes, masks):
    def near(dx, dy, level, comp):
        return shifted[dx + 1, dy + 1, level, comp, chunk]

    own = [near(0, 0, layer, comp) for comp in range(3)]
    own_ge = near(0, 0, layer, 3) > 0.5
    h = own_pick(own_ge, silicon[8], germanium[8])
    d2 = own_pick(own_ge, silicon[7] ** 2, germanium[7] ** 2)
    c2 = own_pick(own_ge, silicon[6] ** 2, germanium[6] ** 2)
    ratio = own_pick(own_ge, silicon[6] ** 2 / silicon[7] ** 2, germanium[6] ** 2 / germanium[7] ** 2)
    beta = own_pick(own_ge, silicon[4], germanium[4])
    power = own_pick(own_ge, silicon[5], germanium[5])
    half_inv = own_pick(own_ge, 0.5 / silicon[5], 0.5 / germanium[5])
    data = []
    for slot in range(slots):
        code = codes[slot]
        bond = [jnp.full(code.shape, lattice_step, f32)] + [jnp.zeros(code.shape, f32) for _ in range(2)]
        kind = jnp.zeros(code.shape, f32)
        valid = jnp.zeros(code.shape, f32)
        for entry, dx, dy, dz in bonds_of(layer, layers, slot):
            hit = code == entry
            for comp, step in enumerate((dx, dy, dz)):
                place = near(dx, dy, layer + dz, comp)
                if step:
                    place = place + f32(lattice_step * step)
                bond[comp] = jnp.where(hit, place - own[comp], bond[comp])
            kind = jnp.where(hit, near(dx, dy, layer + dz, 3), kind)
            valid = jnp.where(hit, f32(1.0), valid)
        live = masks[slot].astype(f32) * valid
        dist2 = bond[0] * bond[0] + bond[1] * bond[1] + bond[2] * bond[2]
        inv = lax.rsqrt(dist2)
        dist = dist2 * inv
        unit = [b * inv for b in bond]
        same = (kind > 0.5) == own_ge
        inner = pick(own_ge, same, 9, "geo")
        span_si = 1.0 / (silicon[10] - silicon[9])
        span_ge = 1.0 / (germanium[10] - germanium[9])
        span_mix = 1.0 / (math.sqrt(silicon[10] * germanium[10]) - math.sqrt(silicon[9] * germanium[9]))
        span = jnp.where(same, jnp.where(own_ge, f32(span_ge), f32(span_si)), f32(span_mix))
        phase = (dist - inner) * span
        v = jnp.clip(phase, 0.0, 1.0) - 0.5
        v2 = v * v
        fade = 0.5 - 0.5 * v * poly(v2, sin_coefs)
        fade_slope = f32(-0.5 * math.pi) * span * poly(v2, cos_coefs)
        below, above = phase < 0.0, phase > 1.0
        cutoff = jnp.where(below, 1.0, jnp.where(above, 0.0, fade))
        slope = jnp.where(below | above, 0.0, fade_slope) * live
        mu = pick(own_ge, same, 3, "mean")
        lam = pick(own_ge, same, 2, "mean")
        attract = pick(own_ge, same, 1, "geo") * jnp.exp(-mu * dist)
        repulse = pick(own_ge, same, 0, "geo") * jnp.exp(-lam * dist)
        data.append(dict(unit=unit, inv=inv, weight=live * cutoff, slope=slope, mu=mu, lam=lam, att=attract, rep=repulse))
    zeta = [jnp.zeros_like(h) for _ in range(slots)]
    for s in range(slots):
        for t in range(s):
            us, ut = data[s]["unit"], data[t]["unit"]
            q = us[0] * ut[0] + us[1] * ut[1] + us[2] * ut[2]
            away = h - q
            gap = away * away
            g = 1.0 + ratio * gap / (d2 + gap)
            zeta[s] = zeta[s] + data[t]["weight"] * g
            zeta[t] = zeta[t] + data[s]["weight"] * g
    pull, radial = [], []
    for s in range(slots):
        item = data[s]
        z = jnp.exp(power * jnp.log(beta * zeta[s]))
        order = jnp.exp(-jnp.log(1.0 + z) * half_inv)
        bound = order * item["att"]
        pull.append(0.25 * item["weight"] * bound * z / (zeta[s] * (1.0 + z)))
        radial.append(
            0.5 * (item["slope"] * (item["rep"] - bound) + item["weight"] * (item["mu"] * bound - item["lam"] * item["rep"]))
        )
    turn = [[jnp.zeros_like(h) for _ in range(3)] for _ in range(slots)]
    spread = [jnp.zeros_like(h) for _ in range(slots)]
    for s in range(slots):
        for t in range(s):
            us, ut = data[s]["unit"], data[t]["unit"]
            q = us[0] * ut[0] + us[1] * ut[1] + us[2] * ut[2]
            away = h - q
            gap = away * away
            inv = 1.0 / (d2 + gap)
            g = 1.0 + ratio * gap * inv
            tilt = -2.0 * c2 * away * inv * inv
            pair = (pull[s] * data[t]["weight"] + pull[t] * data[s]["weight"]) * tilt
            for comp in range(3):
                turn[s][comp] = turn[s][comp] + pair * ut[comp]
                turn[t][comp] = turn[t][comp] + pair * us[comp]
            spread[s] = spread[s] + pull[t] * g
            spread[t] = spread[t] + pull[s] * g
    grads = []
    for s in range(slots):
        item = data[s]
        unit = item["unit"]
        along = turn[s][0] * unit[0] + turn[s][1] * unit[1] + turn[s][2] * unit[2]
        line = radial[s] + item["slope"] * spread[s] - along * item["inv"]
        grads.append([turn[s][comp] * item["inv"] + line * unit[comp] for comp in range(3)])
    return grads


def step_kernel(
    dims,
    disp_hbm, kinds_hbm, codes_hbm, masks_hbm, kern_hbm, x_hbm, y_hbm,
    out_ref,
    disp_ref, kinds_ref, codes_ref, masks_ref, kern_all, kern_out, kern_rest, x_tab, y_tab, line_in, buf, send2, recv2, send3, recv3, waves, kern_in, rest_in, fields,
    col_out, top_out, low_out, col_in, row_in, spot_out, spot_in, shifted, spill,
    side_out, edge_out, side_in, edge_in, tip_out, tip_in,
    load_sem, p1_sem, k_sem, rest_sem, halo_sem, p2_sem, p3_sem, rim_sem, relay_sem,
):
    nx_dev, ny_dev, layers, slots, rows, total_x, total_y, pw, kyw = dims
    count = nx_dev * ny_dev
    rp = rows // nx_dev
    chunks = rows // ROWS
    b = lax.axis_index("sx")
    a = lax.axis_index("sy")
    me = a * nx_dev + b
    half = ny_dev // 2
    early = a < half
    kind = jnp.where(early, 0, 1)

    def pair_of(dev_x, dev_y):
        first = dev_y < half
        return jnp.where(first, dev_y, ny_dev - 1 - dev_y) * (2 * nx_dev) + dev_x + jnp.where(first, 0, nx_dev)

    mine = pair_of(b, a)
    lane = lax.broadcasted_iota(jnp.int32, (rows, LANES), 1)
    row = lax.broadcasted_iota(jnp.int32, (rows, LANES), 0)
    lane1 = lax.broadcasted_iota(jnp.int32, (ROWS, LANES), 1)

    def wrap(value, size):
        return jnp.where(value >= size, value - size, value)

    def each_other(visit):
        for i in reversed(range(nx_dev)):
            other_x = wrap(b + i, nx_dev)

            def body(j, carry, other_x=other_x):
                visit(other_x, wrap(a + j, ny_dev))
                return carry

            lax.fori_loop(0 if i else 1, ny_dev, body, None, unroll=count <= 64)

    def beside(step_x, step_y):
        return {"sx": wrap(b + step_x % nx_dev, nx_dev), "sy": wrap(a + step_y % ny_dev, ny_dev)}

    def remote(src, dst, sems, index, dev):
        return pltpu.make_async_remote_copy(
            src_ref=src, dst_ref=dst, send_sem=sems.at[0, index], recv_sem=sems.at[1, index],
            device_id=dev, device_id_type=MESH,
        )

    barrier = pltpu.get_barrier_semaphore()

    low = 2 ** ((ny_dev.bit_length() - 1) // 2)
    lines = ny_dev // low
    side, line = lax.rem(a, low), a // low
    cube = [
        {"sx": wrap(b + i, nx_dev), "sy": line * low + wrap(side + j, low)}
        for j in range(low) for i in range(nx_dev) if i or j
    ]
    near = cube + [{"sx": b, "sy": wrap(line + k, lines) * low + side} for k in range(1, lines)]
    for dev in near:
        pl.semaphore_signal(barrier, inc=1, device_id=dev, device_id_type=MESH)

    loads = [
        pltpu.make_async_copy(x_hbm, x_tab, load_sem.at[0]),
        pltpu.make_async_copy(y_hbm, y_tab, load_sem.at[1]),
        pltpu.make_async_copy(disp_hbm, disp_ref, load_sem.at[2]),
        None,
        pltpu.make_async_copy(codes_hbm, codes_ref, load_sem.at[4]),
        pltpu.make_async_copy(masks_hbm, masks_ref, load_sem.at[5]),
        pltpu.make_async_copy(kinds_hbm, kinds_ref, load_sem.at[6]),
    ]
    def stiff_row(slot):
        group, r = slot // pw, slot % pw
        if group == 2 * nx_dev:
            return 0
        o, t = group // nx_dev, group % nx_dev
        late = (o + 1) * nx_dev - 1 - t
        if r:
            late_row = late * pw + pw - r
        else:
            late_row = (late + 1) * pw if late + 1 < 2 * nx_dev else 0
        return jnp.where(early, group * pw + r, late_row)

    for i in (2, 6):
        loads[i].start()
    for slot in range((2 * nx_dev + 1) * pw):
        pltpu.make_async_copy(kern_hbm.at[stiff_row(slot)], kern_all.at[slot], load_sem.at[3]).start()
    for i in (0, 1, 4, 5):
        loads[i].start()

    def field(level, comp):
        if comp < 3:
            return disp_ref[level, comp].reshape(rows, LANES)
        return kinds_ref[level].astype(f32)

    pl.semaphore_wait(barrier, len(near))
    for dev in cube:
        pl.semaphore_signal(relay_sem, inc=1, device_id=dev, device_id_type=MESH)
    loads[2].wait()

    p1 = []
    kc = []
    for k in range(1, nx_dev):
        other = wrap(b + k, nx_dev)
        p1.append(remote(disp_ref.at[0, :, other], line_in.at[b], p1_sem, k, {"sx": other, "sy": a}))
    for copy in p1:
        copy.start()
    for comp in range(3):
        line_in[b, comp] = disp_ref[0, comp, b]
    halo = []
    for i, step in enumerate((1, -1)):
        halo.append(remote(col_out, col_in.at[i], halo_sem, i, beside(step, 0)))
    n = 2
    for j, (step_y, src) in enumerate(((1, low_out), (-1, top_out))):
        halo.append(remote(src, row_in.at[j], halo_sem, n, beside(0, step_y)))
        for i, step_x in enumerate((1, -1)):
            dest = spot_in.at[j, i, pl.ds(0, 1)]
            halo.append(remote(spot_out.at[j, pl.ds(0, 1)], dest, halo_sem, n + 1 + i, beside(step_x, step_y)))
        n += 3
    loads[6].wait()
    packed = jnp.zeros((rows, LANES), f32)
    for q in range(4 * layers):
        base = field(q // 4, q % 4)
        top_out[q : q + 1, :] = base[0:1]
        low_out[q : q + 1, :] = base[rows - 1 : rows]
        packed = jnp.where(lane == q, base[:, 0:1], packed)
        packed = jnp.where(lane == 4 * layers + q, base[:, LANES - 1 : LANES], packed)
    col_out[...] = packed
    spot_out[0, 0:1] = packed[rows - 1 : rows]
    spot_out[1, 0:1] = packed[0:1]

    pltpu.make_async_copy(kern_all, kern_all, load_sem.at[3]).wait()
    spots = [(c, c, 0) for c in range(3)] + [(c, d, ri) for ri in range(2) for c, d in ((0, 1), (0, 2), (1, 2))]

    def stiff_part(group, m):
        c, d, ri = spots[m]
        return kern_all[group * pw : (group + 1) * pw, c, d, ri, :]

    lane_k = lax.broadcasted_iota(jnp.int32, (pw, LANES), 1)
    for group in range(2 * nx_dev):
        if kyw % LANES == 0:
            for m in range(9):
                kern_out[group, m * pw : (m + 1) * pw] = stiff_part(group, m)
        else:
            for m in range(5):
                high = stiff_part(group, m + 5) if m < 4 else jnp.zeros((pw, kyw), f32)
                tile = jnp.concatenate([stiff_part(group, m), high], axis=1)
                if m == 4 and pw == FOLD:
                    turned = pltpu.roll(pltpu.roll(tile, LANES // 2, 1), FOLD // 2, 0)
                    tile = jnp.where(lane_k < LANES // 2, tile, turned)
                kern_out[group, m * pw : (m + 1) * pw] = tile
    kern_rest[...] = jnp.zeros_like(kern_rest)
    for m in range(9 if kyw % LANES == 0 else 5):
        edge_part = stiff_part(2 * nx_dev, m)
        if kyw % LANES:
            high = stiff_part(2 * nx_dev, m + 5) if m < 4 else jnp.zeros((pw, kyw), f32)
            edge_part = jnp.concatenate([edge_part, high], axis=1)
        kern_rest[m : m + 1] = edge_part[0:1]
    kern_in[kind, b] = kern_out[b]
    used = pl.ds(0, 4 * FOLD + FOLD // 2 if kyw % LANES and pw == FOLD else kern_out.shape[1])
    for k in range(1, nx_dev):
        other = wrap(b + k, nx_dev)
        kc.append(remote(kern_out.at[other, used], kern_in.at[kind, b, used], k_sem, k, {"sx": other, "sy": a}))
    for copy in kc:
        copy.start()
    pl.semaphore_wait(relay_sem, len(cube))
    far = []
    for k in range(nx_dev):
        other = wrap(b + k, nx_dev)
        dev = {"sx": other, "sy": ny_dev - 1 - a}
        far.append(remote(kern_out.at[nx_dev + other, used], kern_in.at[kind, b, used], k_sem, nx_dev + k, dev))
    rest_to = {"sx": jnp.zeros_like(b), "sy": jnp.where(a == half, 0, ny_dev - a)}
    rest = remote(kern_rest, rest_in.at[b], rest_sem, b, rest_to)
    for copy in far:
        copy.start()

    @pl.when(a >= half)
    def _():
        rest.start()

    for copy in p1:
        copy.wait()
    if rp == FOLD:
        parts_x = [jnp.concatenate([line_in[src, comp] for src in range(nx_dev)], axis=1) for comp in range(3)]
        lines_in = jnp.concatenate(parts_x, axis=0)
    else:
        for src in range(nx_dev):
            for comp in range(3):
                buf[comp * rp : (comp + 1) * rp, src * LANES : (src + 1) * LANES] = line_in[src, comp]
        lines_in = buf[...]
    loads[0].wait()
    buf[...] = dot3(lines_in, x_tab[0], x_tab[1])
    per = LANES // pw
    lane_p = lax.broadcasted_iota(jnp.int32, (rp, LANES), 1)
    for dest in range(count):
        block, part = dest // per, dest % per
        tile = jnp.zeros((rp, LANES), f32)
        for ri in range(2):
            for comp in range(3):
                at = ri * IM_LANE + comp * pw
                col = ri * (total_x // 2) + block * LANES
                piece = buf[comp * rp : (comp + 1) * rp, col : col + LANES]
                shift = (at - part * pw) % LANES
                if shift:
                    piece = pltpu.roll(piece, shift, 1)
                tile = jnp.where((lane_p >= at) & (lane_p < at + pw), piece, tile)
        if rp == FOLD:
            turned = pltpu.roll(pltpu.roll(tile, LANES // 2, 1), FOLD // 2, 0)
            tile = jnp.where(lane_p < LANES // 2, tile, turned)
        send2[dest] = tile
    recv2[me] = send2[mine]
    some_rows = pl.ds(0, rp // 2 if rp == FOLD else rp)

    def all_start2():
        def send(other_x, other_y):
            src = send2.at[pair_of(other_x, other_y), some_rows]
            remote(src, recv2.at[me, some_rows], p2_sem, 0, {"sx": other_x, "sy": other_y}).start()

        each_other(send)

    lot = pl.ds(0, FOLD + (FOLD // 2 if pw == FOLD else pw))

    def all_start3():
        def send(other_x, other_y):
            src = send3.at[other_y, lot]
            remote(src, recv3.at[mine, lot], p3_sem, 0, {"sx": other_x, "sy": other_y}).start()

        each_other(send)

    def all_wait3():
        for i in range(nx_dev):
            some = send3.at[pl.ds(0, ny_dev - (1 if i == 0 else 0)), lot]
            pltpu.make_async_copy(some, some, p3_sem.at[0, 0]).wait()
        some = recv3.at[pl.ds(0, count - 1), lot]
        pltpu.make_async_copy(some, some, p3_sem.at[1, 0]).wait()

    def all_wait2():
        some = pl.ds(0, count - 1)
        pltpu.make_async_copy(send2.at[some, some_rows], send2.at[some, some_rows], p2_sem.at[0, 0]).wait()
        pltpu.make_async_copy(recv2.at[some, some_rows], recv2.at[some, some_rows], p2_sem.at[1, 0]).wait()

    for copy in halo:
        copy.start()
    all_start2()

    for copy in halo:
        copy.wait()
    first_row, last_row = row == 0, row == rows - 1
    first_lane, last_lane = lane == 0, lane == LANES - 1
    full = (rows, LANES)

    def keep(dx, dy, q, value):
        for chunk in range(chunks):
            shifted[dx + 1, dy + 1, q // 4, q % 4, chunk] = value[chunk * ROWS : (chunk + 1) * ROWS]

    for q in range(4 * layers):
        base = field(q // 4, q % 4)
        left = jnp.broadcast_to(col_in[0][:, 4 * layers + q : 4 * layers + q + 1], full)
        right = jnp.broadcast_to(col_in[1][:, q : q + 1], full)
        for dy in (-1, 0, 1):
            if dy == 0:
                mid, lo, hi = base, left, right
            else:
                edge = first_row if dy == -1 else last_row
                j = 0 if dy == -1 else 1
                turn = 1 if dy == -1 else rows - 1
                mid = jnp.where(edge, row_in[j, q : q + 1, :], pltpu.roll(base, turn, 0))
                at = 4 * layers + q
                lo = jnp.where(edge, spot_in[j, 0, 0:1, at : at + 1], pltpu.roll(left, turn, 0))
                hi = jnp.where(edge, spot_in[j, 1, 0:1, q : q + 1], pltpu.roll(right, turn, 0))
            keep(0, dy, q, mid)
            keep(-1, dy, q, jnp.where(first_lane, lo, pltpu.roll(mid, 1, 1)))
            keep(1, dy, q, jnp.where(last_lane, hi, pltpu.roll(mid, LANES - 1, 1)))

    for copy in kc:
        copy.wait()
    loads[1].wait()
    all_wait2()
    width = 3 * pw

    arrived = recv2[...].reshape(total_y, LANES)
    if rp == FOLD:
        turned = pltpu.roll(arrived, LANES // 2, 1)
        turned = pltpu.roll(turned, FOLD // 2, 0)
        spread_row = lax.broadcasted_iota(jnp.int32, (total_y, LANES), 0) % FOLD
        arrived = jnp.where(spread_row < FOLD // 2, arrived, turned)
    table = jnp.transpose(arrived)[: 2 * IM_LANE]
    both = dot3(table, y_tab[0], y_tab[1])
    cos_part, sin_part = both[:, :total_y], both[:, total_y:]
    for copy in far:
        copy.wait()

    @pl.when(a >= half)
    def _():
        rest.wait_send()

    @pl.when(early & (b == 0))
    def _():
        for src in range(nx_dev):
            pltpu.make_async_copy(rest_in.at[src], rest_in.at[src], rest_sem.at[1, src]).wait()
            for m in range(9 if kyw % LANES == 0 else 5):
                line = rest_in[src, m : m + 1, :]
                if m == 4 and kyw % LANES:
                    line = jnp.where(lane_k[0:1] < LANES // 2, line, kern_in[1, src, m * pw : m * pw + 1, :])
                kern_in[1, src, m * pw : m * pw + 1, :] = line

    row_k = lax.broadcasted_iota(jnp.int32, (pw, LANES), 0)
    pair_row = lax.broadcasted_iota(jnp.int32, (pw, total_y), 0) + mine * pw

    def stiff(which, m):
        if kyw % LANES == 0:
            return jnp.concatenate([kern_in[which, src, m * pw : (m + 1) * pw] for src in range(nx_dev)], axis=1)

        def tile_of(src):
            tile = kern_in[which, src, m % 5 * pw : (m % 5 + 1) * pw]
            if m == 4 and pw == FOLD:
                turned = pltpu.roll(pltpu.roll(tile, LANES // 2, 1), FOLD // 2, 0)
                tile = jnp.where(row_k < FOLD // 2, tile, turned)
            return tile

        pieces = []
        for pair in range(nx_dev // 2):
            one, two = tile_of(2 * pair), tile_of(2 * pair + 1)
            if m < 5:
                two = pltpu.roll(two, LANES // 2, 1)
            else:
                one = pltpu.roll(one, LANES // 2, 1)
            pieces.append(jnp.where(lane_k < LANES // 2, one, two))
        return jnp.concatenate(pieces, axis=1)

    def push(which, sr, si):
        fr, fi = [], []
        for comp in range(3):
            diag = stiff(which, comp)
            fr.append(diag * sr[comp])
            fi.append(diag * si[comp])
        for m, (c, d) in enumerate(((0, 1), (0, 2), (1, 2))):
            kr, ki = stiff(which, 3 + m), stiff(which, 6 + m)
            fr[c] = fr[c] + kr * sr[d] - ki * si[d]
            fi[c] = fi[c] + kr * si[d] + ki * sr[d]
            fr[d] = fr[d] + kr * sr[c] + ki * si[c]
            fi[d] = fi[d] + kr * si[c] - ki * sr[c]
        return fr, fi

    ends = pair_row == 0
    ar, ai, br, bi = [], [], [], []
    for comp in range(3):
        re_at = slice(comp * pw, (comp + 1) * pw)
        im_at = slice(IM_LANE + comp * pw, IM_LANE + (comp + 1) * pw)
        re_c, re_s, im_c, im_s = cos_part[re_at], sin_part[re_at], cos_part[im_at], sin_part[im_at]
        ar.append(re_c + jnp.where(ends, 0.0, im_s))
        ai.append(jnp.where(ends, 0.0, im_c) - re_s)
        br.append(jnp.where(ends, im_c, re_c - im_s))
        bi.append(jnp.where(ends, -im_s, -im_c - re_s))
    ar, ai = push(0, ar, ai)
    br, bi = push(1, br, bi)
    up, down = [], []
    for comp in range(3):
        up.append(jnp.where(ends, ar[comp], ar[comp] + br[comp]))
        down.append(jnp.where(ends, ai[comp], ai[comp] + bi[comp]))
    for comp in range(3):
        up.append(jnp.where(ends, br[comp], ai[comp] - bi[comp]))
        down.append(jnp.where(ends, bi[comp], br[comp] - ar[comp]))
    waves[: 2 * width] = dot3(jnp.concatenate(up, axis=0), y_tab[0, :, :total_y], y_tab[1, :, :total_y]) - dot3(
        jnp.concatenate(down, axis=0), y_tab[0, :, total_y:], y_tab[1, :, total_y:]
    )
    lane_w = lax.broadcasted_iota(jnp.int32, (pw, LANES), 1)
    quarter = LANES // 4
    for dest in range(ny_dev):
        col, part = dest * rows // LANES * LANES, dest * rows % LANES

        def block_of(index, at):
            piece = waves[index * pw : (index + 1) * pw, col : col + LANES]
            shift = (at - part) % LANES
            return pltpu.roll(piece, shift, 1) if shift else piece

        tile = block_of(3, 3 * quarter)
        for comp in (2, 1, 0):
            tile = jnp.where(lane_w < (comp + 1) * quarter, block_of(comp, comp * quarter), tile)
        send3[dest, :pw] = tile
        tile = jnp.where(lane_w < 2 * quarter, block_of(4, quarter), block_of(5, 2 * quarter))
        if pw == FOLD:
            turned = pltpu.roll(pltpu.roll(tile, LANES // 2, 1), FOLD // 2, 0)
            tile = jnp.where((lane_w >= quarter) & (lane_w < 3 * quarter), tile, turned)
        send3[dest, FOLD : FOLD + pw] = tile
    recv3[mine] = send3[a]
    all_start3()

    loads[4].wait()
    loads[5].wait()

    @pl.loop(0, chunks)
    def _(chunk):
        own_sum = []
        parts = {}
        at = pl.ds(pl.multiple_of(chunk * ROWS, ROWS), ROWS)
        for layer in range(layers):
            codes = [codes_ref[layer, slot, at, :] for slot in range(slots)]
            masks = [masks_ref[layer, slot, at, :] for slot in range(slots)]
            grads = tersoff_rows(layer, layers, slots, shifted, chunk, codes, masks)
            total = [sum(grads[s][comp] for s in range(slots)) for comp in range(3)]
            own_sum.append(total)
            for slot in range(slots):
                for entry, dx, dy, dz in bonds_of(layer, layers, slot):
                    hit = codes[slot] == entry
                    for comp in range(3):
                        key = (dx, dy, layer + dz, comp)
                        term = jnp.where(hit, grads[slot][comp], 0.0)
                        parts[key] = parts[key] + term if key in parts else term
        for level in range(layers):
            for comp in range(3):
                key = (0, 0, level, comp)
                here = own_sum[level][comp]
                parts[key] = here - parts[key] if key in parts else here
        for (dx, dy, level, comp), value in parts.items():
            signed = value if (dx, dy) == (0, 0) else -value
            spill[dx + 1, dy + 1, level, comp, at, :] = signed

    left_pack = jnp.zeros(full, f32)
    right_pack = jnp.zeros(full, f32)
    edge_out[...] = jnp.zeros_like(edge_out)
    spots_out = [jnp.zeros((1, LANES), f32) for _ in range(2)]
    lane0 = lane1[0:1]
    for q in range(3 * layers):
        level, comp = q // 3, q % 3
        lines = []
        for dx in (-1, 0, 1):
            part = spill[dx + 1, 1, level, comp]
            down = spill[dx + 1, 2, level, comp]
            up = spill[dx + 1, 0, level, comp]
            part = part + jnp.where(first_row, 0.0, pltpu.roll(down, 1, 0))
            part = part + jnp.where(last_row, 0.0, pltpu.roll(up, rows - 1, 0))
            edge_out[0, dx + 1, q : q + 1, :] = down[rows - 1 : rows]
            edge_out[1, dx + 1, q : q + 1, :] = up[0:1]
            if dx:
                end = LANES - 1 if dx > 0 else 0
                for j, line in enumerate((down[rows - 1 : rows], up[0:1])):
                    hit = lane0 == (ROWS if dx > 0 else 0) + q
                    spots_out[j] = jnp.where(hit, line[:, end : end + 1], spots_out[j])
            lines.append(part)
        left_pack = jnp.where(lane == q, lines[0][:, 0:1], left_pack)
        right_pack = jnp.where(lane == q, lines[2][:, LANES - 1 : LANES], right_pack)
        out_ref[level, comp] = (
            lines[1]
            + jnp.where(first_lane, 0.0, pltpu.roll(lines[2], 1, 1))
            + jnp.where(last_lane, 0.0, pltpu.roll(lines[0], LANES - 1, 1))
        )
    side_out[0] = right_pack
    side_out[1] = left_pack
    for j in range(2):
        edge_out[j, 1] = (
            edge_out[j, 1]
            + jnp.where(lane1 == 0, 0.0, pltpu.roll(edge_out[j, 2], 1, 1))
            + jnp.where(lane1 == LANES - 1, 0.0, pltpu.roll(edge_out[j, 0], LANES - 1, 1))
        )
    for j in range(2):
        tip_out[j, 0:1] = spots_out[j]
    rim = []
    for i, step in enumerate((1, -1)):
        rim.append(remote(side_out.at[i], side_in.at[i], rim_sem, i, beside(step, 0)))
    n = 2
    for j, step_y in enumerate((1, -1)):
        rim.append(remote(edge_out.at[j, 1], edge_in.at[j], rim_sem, n, beside(0, step_y)))
        for i, dx in enumerate((-1, 1)):
            dest = tip_in.at[j, i, pl.ds(0, 1)]
            rim.append(remote(tip_out.at[j, pl.ds(0, 1)], dest, rim_sem, n + 1 + i, beside(dx, step_y)))
        n += 3
    for copy in rim:
        copy.start()

    all_wait3()
    row_w = lax.broadcasted_iota(jnp.int32, (pw, LANES), 0)
    for src in range(count):
        first, second = recv3[src, :pw], recv3[src, FOLD : FOLD + pw]
        if pw == FOLD:
            turned = pltpu.roll(pltpu.roll(second, LANES // 2, 1), FOLD // 2, 0)
            second = jnp.where(row_w < FOLD // 2, second, turned)
        fields[src * pw : (src + 1) * pw] = first
        fields[total_x // 2 + src * pw : total_x // 2 + (src + 1) * pw] = jnp.where(
            lane_w < quarter, pltpu.roll(first, quarter, 1), second
        )
    own_x = pl.ds(pl.multiple_of(b * LANES, LANES), LANES)
    top = fields[...].astype(jnp.bfloat16)
    low_part = (fields[...] - top.astype(f32)).astype(jnp.bfloat16)
    dot = functools.partial(jnp.dot, preferred_element_type=f32)
    lines_x = x_tab[0, own_x, :]
    real = dot(lines_x, top) + (dot(lines_x, low_part) + dot(x_tab[1, own_x, :], top))
    real = jnp.transpose(real) * f32(-1.0 / (total_x * total_y))
    for copy in rim:
        copy.wait()
    for q in range(3 * layers):
        level, comp = q // 3, q % 3
        value = out_ref[level, comp]
        value = value + jnp.where(first_lane, side_in[0][:, q : q + 1], 0.0)
        value = value + jnp.where(last_lane, side_in[1][:, q : q + 1], 0.0)
        for j, edge in enumerate((first_row, last_row)):
            line = edge_in[j, q : q + 1, :]
            value = value + jnp.where(edge, line, 0.0)
            value = value + jnp.where(edge & first_lane, tip_in[j, 1, 0:1, ROWS + q : ROWS + q + 1], 0.0)
            value = value + jnp.where(edge & last_lane, tip_in[j, 0, 0:1, q : q + 1], 0.0)
        out_ref[level, comp] = value
    for comp in range(3):
        out_ref[0, comp] = out_ref[0, comp] + real[comp * rows : (comp + 1) * rows]


def shards(nx_dev, ny_dev, disp, velocity, kinds, neighbours, pad_mask, kernel):
    layers, comps, rows, cols = disp.shape
    slots = neighbours.shape[1]
    total_x, total_y = cols * nx_dev, rows * ny_dev
    count = nx_dev * ny_dev
    kx_block, kyw = kernel.shape[0], kernel.shape[4]
    pw = kx_block // (2 * nx_dev)
    rp = rows // nx_dev
    kern_parts = 9 if kyw % LANES == 0 else 5
    lanes = kyw if kern_parts == 9 else LANES
    x_table = jnp.asarray(line_table(total_x))
    y_table = jnp.asarray(wave_table(total_y))
    chunks = rows // ROWS
    vmem = pl.BlockSpec(memory_space=pltpu.VMEM)
    hbm = pl.BlockSpec(memory_space=pl.ANY)
    tiles = pltpu.VMEM((count, rp, LANES), f32)
    quarter = pltpu.VMEM((nx_dev, 3, rp, LANES), f32)
    sems = lambda n: pltpu.SemaphoreType.DMA((2, n))
    inputs = (disp.reshape(layers, comps, nx_dev, rp, cols), kinds, neighbours, pad_mask, kernel, x_table, y_table)
    force = pl.pallas_call(
        functools.partial(step_kernel, (nx_dev, ny_dev, layers, slots, rows, total_x, total_y, pw, kyw)),
        out_shape=jax.ShapeDtypeStruct(disp.shape, f32),
        in_specs=[hbm] * 7,
        out_specs=vmem,
        scratch_shapes=[
            pltpu.VMEM((layers, comps, nx_dev, rp, cols), f32),
            pltpu.VMEM(kinds.shape, jnp.int32),
            pltpu.VMEM(neighbours.shape, jnp.int32),
            pltpu.VMEM(pad_mask.shape, jnp.int32),
            pltpu.VMEM(((2 * nx_dev + 1) * pw, *kernel.shape[1:]), f32),
            pltpu.VMEM((2 * nx_dev, kern_parts * pw, lanes), f32),
            pltpu.VMEM((2 * ROWS, lanes), f32),
            pltpu.VMEM(x_table.shape, jnp.bfloat16),
            pltpu.VMEM(y_table.shape, jnp.bfloat16),
            quarter,
            pltpu.VMEM((3 * rp, total_x), f32),
            tiles, tiles,
            pltpu.VMEM((ny_dev, 2 * FOLD, LANES), f32),
            pltpu.VMEM((count, 2 * FOLD, LANES), f32),
            pltpu.VMEM((6 * pw, total_y), f32),
            pltpu.VMEM((2, nx_dev, kern_parts * pw, lanes), f32),
            pltpu.VMEM((nx_dev, 2 * ROWS, lanes), f32),
            pltpu.VMEM((total_x, LANES), f32),
            pltpu.VMEM((rows, LANES), f32),
            pltpu.VMEM((4 * layers, LANES), f32),
            pltpu.VMEM((4 * layers, LANES), f32),
            pltpu.VMEM((2, rows, LANES), f32),
            pltpu.VMEM((2, 4 * layers, LANES), f32),
            pltpu.VMEM((2, ROWS, LANES), f32),
            pltpu.VMEM((2, 2, ROWS, LANES), f32),
            pltpu.VMEM((3, 3, layers, 4, chunks, ROWS, LANES), f32),
            pltpu.VMEM((3, 3, layers, 3, rows, LANES), f32),
            pltpu.VMEM((2, rows, LANES), f32),
            pltpu.VMEM((2, 3, ROWS, LANES), f32),
            pltpu.VMEM((2, rows, LANES), f32),
            pltpu.VMEM((2, ROWS, LANES), f32),
            pltpu.VMEM((2, ROWS, LANES), f32),
            pltpu.VMEM((2, 2, ROWS, LANES), f32),
            pltpu.SemaphoreType.DMA((7,)),
            sems(nx_dev), sems(2 * nx_dev), sems(nx_dev), sems(8), sems(1), sems(1), sems(8),
            pltpu.SemaphoreType.REGULAR,
        ],
        compiler_params=pltpu.CompilerParams(
            collective_id=0, has_side_effects=True, vmem_limit_bytes=44 * 1024 * 1024
        ),
    )(*(pltpu.with_memory_space_constraint(value, pltpu.HBM) for value in inputs))
    new_velocity = velocity + impulse_scale * force
    new_disp = disp + drift_scale * new_velocity
    return (new_disp, new_velocity)


def solution(mesh):
    in_specs = (
        P(None, None, "sy", "sx"),
        P(None, None, "sy", "sx"),
        P(None, "sy", "sx"),
        P(None, None, "sy", "sx"),
        P(None, None, "sy", "sx"),
        P("sy", None, None, None, "sx"),
    )
    out_specs = (P(None, None, "sy", "sx"), P(None, None, "sy", "sx"))
    body = functools.partial(shards, mesh.shape["sx"], mesh.shape["sy"])
    return jax.shard_map(body, mesh=mesh, in_specs=in_specs, out_specs=out_specs, check_vma=False)
```
